32 devices in a mesh: dp: 16 (over z, y, x), seq: 2 (over core).
Axes of the slice: x: 2, y: 2, z: 4, core: 2. Of those that a mesh axis runs over, the one named last changes fastest.
Arguments:
- inputs: bfloat16 [64, 1024, 768], P('dp', 'seq'), may hold values from -6 to 6
- horizon: int32 [64], P('dp'), may hold values from 1024 to 4096
- query_weight: bfloat16 [768, 768], P('dp'), may hold values from -0.21875 to 0.21875
- query_bias: bfloat16 [768], P('dp'), may hold values from -3 to 3
- key_weight: bfloat16 [768, 768], P('dp'), may hold values from -0.21875 to 0.21875
- key_bias: bfloat16 [768], P('dp'), may hold values from -3 to 3
- value_weight: bfloat16 [768, 768], P('dp'), may hold values from -0.21875 to 0.21875
- value_bias: bfloat16 [768], P('dp'), may hold values from -0.1796875 to 0.1796875
- out_weight: bfloat16 [768, 768], P('dp'), may hold values from -3.5 to 3.5
- out_bias: bfloat16 [768], P('dp'), may hold values from -3 to 3
- first_gain: bfloat16 [768], P('dp'), may hold values from 0.099609375 to 1.8984375
- first_shift: bfloat16 [768], P('dp'), may hold values from -2 to 2
- up_weight: bfloat16 [768, 3072], P('dp'), may hold values from -0.21875 to 0.21875
- up_bias: bfloat16 [3072], P('dp'), may hold values from -3 to 3
- down_weight: bfloat16 [3072, 768], P('dp'), may hold values from -0.109375 to 0.109375
- down_bias: bfloat16 [768], P('dp'), may hold values from -2 to 2
- second_gain: bfloat16 [768], P('dp'), may hold values from 0.099609375 to 1.8984375
- second_shift: bfloat16 [768], P('dp'), may hold values from -2 to 2
- cotangent: bfloat16 [64, 1024, 768], P('dp', 'seq'), may hold values from -6 to 6
Outputs:
- output: bfloat16 [64, 1024, 768], P('dp', 'seq')
- input_grad: float32 [64, 1024, 768], P('dp', 'seq')
- grad_query_weight: float32 [768, 768], P('dp')
- grad_query_bias: float32 [768], P('dp')
- grad_key_weight: float32 [768, 768], P('dp')
- grad_key_bias: float32 [768], P('dp')
- grad_value_weight: float32 [768, 768], P('dp')
- grad_value_bias: float32 [768], P('dp')
- grad_out_weight: float32 [768, 768], P('dp')
- grad_out_bias: float32 [768], P('dp')
- grad_first_gain: float32 [768], P('dp')
- grad_first_shift: float32 [768], P('dp')
- grad_up_weight: float32 [768, 3072], P('dp')
- grad_up_bias: float32 [3072], P('dp')
- grad_down_weight: float32 [3072, 768], P('dp')
- grad_down_bias: float32 [768], P('dp')
- grad_second_gain: float32 [768], P('dp')
- grad_second_shift: float32 [768], P('dp')
The draws below stay inside these ranges and needn't reach their ends.
All inputs are finite; a program needn't handle non-finite values.
Results may differ from the reference program's by a relative error of at most 0.025.
Values may be sent and summed in bfloat16 or wider, within the bound.
A program may use at most 256 MiB of HBM per device.

```python
import math
import jax
import jax.numpy as jnp
from jax import lax

D = 768
HEADS = 12
HEAD = 64
FF = 3072
SHARD = 512
SEQS = 64
LEN = 1024


def plant(values, own_key, low, largest):
    index_at = [jax.random.randint(jax.random.fold_in(own_key, axis), (), 0, length) for axis, length in enumerate(values.shape)]
    widest = values.shape.index(max(values.shape))
    next_to = index_at[:widest] + [(index_at[widest] + 1) % values.shape[widest]] + index_at[widest + 1:]
    return values.at[tuple(index_at)].set(low).at[tuple(next_to)].set(largest)


def spiked(entries, rng, source, target, blocks, factor):
    owner, partner = [(jnp.arange(entries.shape[dim]) // (entries.shape[dim] // blocks)).reshape([-1 if axis == dim else 1 for axis in range(entries.ndim)]) for dim in (source, target)]
    chosen = jax.random.permutation(rng, blocks)[partner]
    strong = (owner == chosen) | (owner == (partner + blocks // 2) % blocks)
    return jnp.where(strong, factor * entries, entries)


def steps_of(own_key, extent, cuts, low, largest):
    loudness = 1.0
    for dim, parts in cuts:
        heights = jax.random.uniform(jax.random.fold_in(jax.random.fold_in(own_key, 6), dim), (parts,), jnp.float32, low / len(cuts), largest / len(cuts))
        loudness = loudness * jnp.repeat(jnp.exp(heights), extent[dim] // parts).reshape((-1,) + (1,) * (len(extent) - 1 - dim))
    return loudness


def normal_values(key, shape, deviation, bound, pieces=(), kind=jnp.bfloat16):
    factor_of = steps_of(key, shape, pieces, -0.22, 0.18) if pieces else 1.0
    entries = jax.random.normal(key, shape, jnp.float32) * deviation * factor_of
    return jnp.minimum(jnp.maximum(entries, -bound), bound).astype(kind)


def gaussian_with(stream_key, shape, deviation, reach, shards, heavy, dtype=jnp.bfloat16):
    drawn = deviation * jax.random.normal(stream_key, shape, jnp.float32)
    if shards:
        drawn = drawn * steps_of(stream_key, shape, shards, -0.22, 0.18)
    return jnp.clip(spiked(drawn, jax.random.fold_in(stream_key, 3), *heavy), -reach, reach).astype(dtype)


def setup_inputs(seed: int = 0) -> dict:
    streams_of = jax.random.split(jax.random.key(seed), 20)
    inputs = gaussian_with(streams_of[0], (SEQS, LEN, D), 1.0, 6.0, ((0, 16), (1, 2)), (0, 2, 16, 2.0))
    horizon = plant(jax.random.randint(streams_of[1], (SEQS,), LEN, 4 * LEN + 1), jax.random.fold_in(streams_of[1], 1), LEN, 4 * LEN).astype(jnp.int32)
    query_weight = normal_values(streams_of[2], (D, D), D ** -0.5, 0.21875, ((0, 16),))
    query_bias = normal_values(streams_of[3], (D,), 0.5, 3.0, ((0, 16),))
    key_weight = normal_values(streams_of[4], (D, D), D ** -0.5, 0.21875, ((0, 16),))
    key_bias = normal_values(streams_of[5], (D,), 0.5, 3.0, ((0, 16),))
    value_weight = normal_values(streams_of[6], (D, D), D ** -0.5, 0.21875, ((0, 16),))
    value_bias = normal_values(streams_of[7], (D,), 0.03, 0.1796875, ((0, 16),))
    out_weight = normal_values(streams_of[8], (D, D), (max(D * 4 // LEN, 1)) ** -0.5, 3.5, ((0, 16),))
    out_bias = normal_values(streams_of[9], (D,), 0.5, 3.0, ((0, 16),))
    first_gain = jnp.clip(1.0 + 0.18 * jax.random.normal(streams_of[10], (D,), jnp.float32), 0.099609375, 1.8984375).astype(jnp.bfloat16)
    first_shift = normal_values(streams_of[11], (D,), 0.3, 2.0, ((0, 16),))
    up_weight = normal_values(streams_of[12], (D, FF), D ** -0.5, 0.21875, ((0, 16),))
    up_bias = normal_values(streams_of[13], (FF,), 0.5, 3.0, ((0, 16),))
    down_weight = normal_values(streams_of[14], (FF, D), FF ** -0.5, 0.109375, ((0, 16),))
    down_bias = normal_values(streams_of[15], (D,), 0.3, 2.0, ((0, 16),))
    second_gain = jnp.clip(1.0 + 0.18 * jax.random.normal(streams_of[16], (D,), jnp.float32), 0.099609375, 1.8984375).astype(jnp.bfloat16)
    second_shift = normal_values(streams_of[17], (D,), 0.3, 2.0, ((0, 16),))
    cotangent = gaussian_with(streams_of[18], (SEQS, LEN, D), 1.0, 6.0, ((0, 16), (1, 2)), (0, 2, 16, 2.0))
    return dict(inputs=inputs, horizon=horizon, query_weight=query_weight, query_bias=query_bias, key_weight=key_weight, key_bias=key_bias, value_weight=value_weight, value_bias=value_bias, out_weight=out_weight, out_bias=out_bias, first_gain=first_gain, first_shift=first_shift, up_weight=up_weight, up_bias=up_bias, down_weight=down_weight, down_bias=down_bias, second_gain=second_gain, second_shift=second_shift, cotangent=cotangent)


highest = lax.Precision.HIGHEST

@jax.custom_vjp
def low(v):
    return lax.optimization_barrier(v.astype(jnp.bfloat16)).astype(jnp.float32)

@jax.custom_vjp
def low_back(v):
    return v

def low_keep(v):
    return (low(v), None)

def low_pass(kept, grad):
    return (grad,)

def back_keep(v):
    return (v, None)

def back_low(kept, grad):
    return (low(grad),)
low.defvjp(low_keep, low_pass)
low_back.defvjp(back_keep, back_low)

def normalize(values, scale_gain, scale_shift):
    center = values - lax.optimization_barrier(jnp.mean(values, axis=-1, keepdims=True))
    spread = lax.optimization_barrier(jnp.mean(center * center, axis=-1, keepdims=True))
    return center * lax.rsqrt(spread + 1e-05) * scale_gain + scale_shift

def sequence_forward(sequence, params, span_length):
    query_weight, query_bias, key_weight, key_bias, value_weight, value_bias, out_weight, out_bias, first_gain, first_shift, up_weight, up_bias, down_weight, down_bias, second_gain, second_shift = params
    position = jnp.arange(LEN).astype(jnp.float32)
    angles = 0.5 * math.pi * position / span_length.astype(jnp.float32)
    cosine_part = jnp.cos(angles)[:, None, None]
    sine_part = jnp.sin(angles)[:, None, None]

    def project(weight, bias_row):
        return jnp.dot(sequence, weight, precision=highest) + bias_row
    queries = low_back(project(query_weight, query_bias)).reshape(LEN, HEADS, HEAD)
    key_pre = low_back(project(key_weight, key_bias)).reshape(LEN, HEADS, HEAD)
    values = low(low_back(project(value_weight, value_bias))).reshape(LEN, HEADS, HEAD)
    query_pos = jax.nn.softplus(queries)
    key_pos = jax.nn.softplus(key_pre)
    query_cos = low(query_pos * cosine_part)
    query_sin = low(query_pos * sine_part)
    key_cos = low(key_pos * cosine_part)
    key_sin = low(key_pos * sine_part)
    blocks = LEN // SHARD

    def to_blocks(array):
        return array.reshape(blocks, SHARD, HEADS, HEAD)
    causal = (jnp.arange(SHARD)[:, None] >= jnp.arange(SHARD)[None, :]).astype(jnp.float32)

    def block_step(carry, block):
        state_cos, state_sin, total_cos, total_sin = carry
        block_qcos, block_qsin, block_kcos, block_ksin, block_values = block
        scores = jnp.einsum('ihe,jhe->hij', block_qcos, block_kcos, precision=highest)
        scores = scores + jnp.einsum('ihe,jhe->hij', block_qsin, block_ksin, precision=highest)
        scores = low_back(causal[None] * scores)
        numerator = jnp.einsum('hij,jhe->ihe', low(scores), block_values, precision=highest)
        numerator = numerator + jnp.einsum('ihe,hef->ihf', block_qcos, state_cos, precision=highest)
        numerator = numerator + jnp.einsum('ihe,hef->ihf', block_qsin, state_sin, precision=highest)
        numerator = low_back(numerator)
        denominator = lax.optimization_barrier(jnp.sum(scores, axis=2)).T
        denominator = denominator + jnp.einsum('ihe,he->ih', block_qcos, total_cos, precision=highest)
        denominator = denominator + jnp.einsum('ihe,he->ih', block_qsin, total_sin, precision=highest)
        mixed_out = low(numerator / denominator[:, :, None])
        new_carry = (state_cos + jnp.einsum('jhe,jhf->hef', block_kcos, block_values, precision=highest), state_sin + jnp.einsum('jhe,jhf->hef', block_ksin, block_values, precision=highest), total_cos + lax.optimization_barrier(jnp.sum(block_kcos, axis=0)), total_sin + lax.optimization_barrier(jnp.sum(block_ksin, axis=0)))
        return (new_carry, mixed_out)
    zero_state = jnp.zeros((HEADS, HEAD, HEAD), jnp.float32)
    zero_total = jnp.zeros((HEADS, HEAD), jnp.float32)
    final_state, mixed_out = lax.scan(jax.checkpoint(block_step), (zero_state, zero_state, zero_total, zero_total), (to_blocks(query_cos), to_blocks(query_sin), to_blocks(key_cos), to_blocks(key_sin), to_blocks(values)))
    mixed_out = mixed_out.reshape(LEN, D)
    branch = low_back(jnp.dot(mixed_out, out_weight, precision=highest) + out_bias)
    residual = sequence + branch
    normed = normalize(residual, first_gain, first_shift)
    hidden = low_back(jnp.dot(low(normed), up_weight, precision=highest) + up_bias)
    active = low(jax.nn.gelu(hidden, approximate=True))
    ffn_out = low_back(jnp.dot(active, down_weight, precision=highest) + down_bias)
    return normalize(normed + ffn_out, second_gain, second_shift)

def reference(inputs, horizon, query_weight, query_bias, key_weight, key_bias, value_weight, value_bias, out_weight, out_bias, first_gain, first_shift, up_weight, up_bias, down_weight, down_bias, second_gain, second_shift, cotangent):
    params = tuple((weight.astype(jnp.float32) for weight in (query_weight, query_bias, key_weight, key_bias, value_weight, value_bias, out_weight, out_bias, first_gain, first_shift, up_weight, up_bias, down_weight, down_bias, second_gain, second_shift)))

    def one_sequence(totals, sequence_item):
        sequence, span_length, seq_cotangent = sequence_item

        def forward(sequence_in, params_in):
            return sequence_forward(sequence_in, params_in, span_length)
        result, pull_back = jax.vjp(forward, sequence, params)
        back_input, back_params = pull_back(seq_cotangent)
        return (jax.tree.map(jnp.add, totals, back_params), (result.astype(jnp.bfloat16), back_input))
    zero_grads = jax.tree.map(jnp.zeros_like, params)
    totals, (output, input_grad) = lax.scan(one_sequence, zero_grads, (inputs.astype(jnp.float32), horizon, cotangent.astype(jnp.float32)))
    return (output, input_grad, totals[0], totals[1], totals[2], totals[3], totals[4], totals[5], totals[6], totals[7], totals[8], totals[9], totals[10], totals[11], totals[12], totals[13], totals[14], totals[15])
```

```python
import functools
import math

import jax
import jax.numpy as jnp
from jax import lax
from jax.experimental import pallas as pl
from jax.experimental.pallas import tpu as pltpu
from jax.sharding import PartitionSpec as P

HEADS = 12
HEAD = 64
PAIRS = HEADS // 2
LANES = 128
CHUNK = 256
ROWS = 256
NORM_EPS = 1e-05
GELU_A = 0.7978845608
GELU_B = 0.044715
VMEM_LIMIT = 60 * 1024 * 1024
F32, BF16 = jnp.float32, jnp.bfloat16


def dot_nn(a, b):
    return lax.dot_general(a, b, (((1,), (0,)), ((), ())), preferred_element_type=F32)


def dot_nt(a, b):
    return lax.dot_general(a, b, (((1,), (1,)), ((), ())), preferred_element_type=F32)


def dot_tn(a, b):
    return lax.dot_general(a, b, (((0,), (0,)), ((), ())), preferred_element_type=F32)


def low_lanes(rows):
    return lax.broadcasted_iota(jnp.int32, (rows, LANES), 1) < HEAD


def swap(values):
    return pltpu.roll(values, HEAD, 1)


def softplus_and_slope(values):
    e = jnp.exp(-jnp.abs(values))
    plus = jnp.maximum(values, 0.0) + jnp.log1p(e)
    slope = jnp.where(values >= 0.0, 1.0, e) / (1.0 + e)
    return plus, slope


def attend_forward(
    x_ref, w_ref, b_ref, cs_ref, a_ref, k_ref, v_ref, sq_ref, sk_ref, mixed_ref, den_ref, s_ref, state
):
    width = x_ref.shape[1]
    rows = x_ref.shape[0]

    @pl.when(pl.program_id(1) == 0)
    def _():
        state[...] = jnp.zeros_like(state)

    x = x_ref[...]
    cs = cs_ref[...]
    low = low_lanes(rows)
    causal = lax.broadcasted_iota(jnp.int32, (rows, rows), 0) >= lax.broadcasted_iota(
        jnp.int32, (rows, rows), 1
    )

    for half in range(2):
        slope_ref = (sq_ref, sk_ref)[half]
        feature_ref = (a_ref, k_ref)[half]
        pre = dot_nn(x, w_ref[:, half * width : (half + 1) * width])
        pre = pre + b_ref[:, half * width : (half + 1) * width]
        plus, slope = softplus_and_slope(pre)
        slope_ref[...] = slope.astype(BF16)
        for pair in range(PAIRS):
            both = plus[:, pair * LANES : (pair + 1) * LANES]
            other = swap(both)
            even = jnp.where(low, both, other) * cs
            odd = jnp.where(low, other, both) * cs
            feature_ref[:, (2 * pair) * LANES : (2 * pair + 1) * LANES] = even.astype(BF16)
            feature_ref[:, (2 * pair + 1) * LANES : (2 * pair + 2) * LANES] = odd.astype(BF16)
    values = dot_nn(x, w_ref[:, 2 * width :]) + b_ref[:, 2 * width :]
    v_ref[...] = values.astype(BF16)
    for pair in range(PAIRS):
        both = values[:, pair * LANES : (pair + 1) * LANES]
        results = []
        for odd in range(2):
            head = 2 * pair + odd
            query = a_ref[:, head * LANES : (head + 1) * LANES]
            key = k_ref[:, head * LANES : (head + 1) * LANES]
            wide = (jnp.where(low, 1.0, both) if odd else jnp.where(low, both, 1.0)).astype(BF16)
            scores = jnp.where(causal, dot_nt(query, key), 0.0).astype(BF16)
            before = state[head]
            before_low = before.astype(BF16)
            s_ref[head] = before_low
            results.append(dot_nn(scores, wide) + dot_nn(query, before_low))
            state[head] = before + dot_tn(key, wide)
        numer = jnp.where(low, results[0], results[1])
        denom = swap(jnp.where(low, results[1], results[0]))
        mixed_ref[:, pair * LANES : (pair + 1) * LANES] = (numer / denom).astype(BF16)
        den_ref[:, pair * LANES : (pair + 1) * LANES] = denom


def forward_call(x, w, b, cs, chunks):
    total, width = x.shape
    seqs = total // (chunks * CHUNK)
    row = lambda n: pl.BlockSpec((CHUNK, n), lambda s, c: (s * chunks + c, 0))
    once = lambda shape: pl.BlockSpec(
        shape, lambda s, c: (0,) * len(shape), pipeline_mode=pl.Buffered(1)
    )
    wide = HEADS * LANES
    return pl.pallas_call(
        attend_forward,
        grid=(seqs, chunks),
        in_specs=[row(width), once(w.shape), once(b.shape), row(LANES)],
        out_specs=[
            row(wide),
            row(wide),
            row(width),
            row(width),
            row(width),
            row(width),
            row(width),
            pl.BlockSpec((None, HEADS, LANES, LANES), lambda s, c: (s * chunks + c, 0, 0, 0)),
        ],
        out_shape=[
            jax.ShapeDtypeStruct((total, wide), BF16),
            jax.ShapeDtypeStruct((total, wide), BF16),
            jax.ShapeDtypeStruct((total, width), BF16),
            jax.ShapeDtypeStruct((total, width), BF16),
            jax.ShapeDtypeStruct((total, width), BF16),
            jax.ShapeDtypeStruct((total, width), BF16),
            jax.ShapeDtypeStruct((total, width), F32),
            jax.ShapeDtypeStruct((seqs * chunks, HEADS, LANES, LANES), BF16),
        ],
        scratch_shapes=[pltpu.VMEM((HEADS, LANES, LANES), F32)],
        compiler_params=pltpu.CompilerParams(
            dimension_semantics=("arbitrary", "arbitrary"), vmem_limit_bytes=VMEM_LIMIT
        ),
        name="attend_forward",
    )(x, w, b, cs)


def row_mean(values):
    return jnp.mean(values, axis=-1, keepdims=True)


def norm_parts(values):
    center = values - row_mean(values)
    scale = lax.rsqrt(row_mean(center * center) + NORM_EPS)
    return center * scale, scale


def norm_back(grad, gain, unit, scale):
    scaled = grad * gain
    return (scaled - row_mean(scaled) - unit * row_mean(scaled * unit)) * scale


def add_rows(values):
    return jnp.sum(values, axis=0, keepdims=True)


def middle(
    tiles,
    x_ref,
    ct_ref,
    mixed_ref,
    den_ref,
    vec_ref,
    ubias_ref,
    wo_ref,
    wu_ref,
    wd_ref,
    out_ref,
    resid_ref,
    e_ref,
    go_hbm,
    gu_hbm,
    gd_hbm,
    gvec_ref,
    gub_ref,
    act,
    slope,
    go,
    gu,
    gd,
    sems,
):
    step = pl.program_id(0)
    rows, width = x_ref.shape
    hidden_width = wu_ref.shape[1]
    tile = hidden_width // tiles
    low = low_lanes(rows)

    @pl.when(step == 0)
    def _():
        go[...] = jnp.zeros_like(go)
        gu[...] = jnp.zeros_like(gu)
        gd[...] = jnp.zeros_like(gd)
        gvec_ref[...] = jnp.zeros_like(gvec_ref)
        gub_ref[...] = jnp.zeros_like(gub_ref)

    out_bias, gain1, shift1 = vec_ref[0:1], vec_ref[1:2], vec_ref[2:3]
    down_bias, gain2, shift2 = vec_ref[3:4], vec_ref[4:5], vec_ref[5:6]
    mixed = mixed_ref[...]
    resid = x_ref[...].astype(F32) + (dot_nn(mixed, wo_ref[...]) + out_bias)
    unit1, scale1 = norm_parts(resid)
    normed = unit1 * gain1 + shift1
    normed_low = normed.astype(BF16)
    ffn = jnp.zeros((rows, width), F32)
    for t in range(tiles):
        cols = slice(t * tile, (t + 1) * tile)
        hidden = dot_nn(normed_low, wu_ref[:, cols]) + ubias_ref[:, cols]
        square = hidden * hidden
        inner = hidden * (GELU_A + (GELU_A * GELU_B) * square)
        tanh = jnp.tanh(inner)
        half = 0.5 + 0.5 * tanh
        active = (hidden * half).astype(BF16)
        curve = half + (0.5 * hidden) * (1.0 - tanh * tanh) * (
            GELU_A + (3.0 * GELU_A * GELU_B) * square
        )
        act[:, cols] = active
        slope[:, cols] = curve.astype(BF16)
        ffn = ffn + dot_nn(active, wd_ref[cols, :])
    unit2, scale2 = norm_parts(normed + (ffn + down_bias))
    out_ref[...] = (unit2 * gain2 + shift2).astype(BF16)
    grad = ct_ref[...].astype(F32)
    back_final = norm_back(grad, gain2, unit2, scale2)
    back_ffn = back_final.astype(BF16)
    gvec_ref[4:5] += add_rows(grad * unit2)
    gvec_ref[5:6] += add_rows(grad)
    gvec_ref[3:4] += add_rows(back_ffn.astype(F32))
    back_normed = back_final
    for t in range(tiles):
        cols = slice(t * tile, (t + 1) * tile)
        gd[cols, :] += dot_tn(act[:, cols], back_ffn)
        back_active = dot_nt(back_ffn, wd_ref[cols, :])
        back_hidden = (back_active * slope[:, cols].astype(F32)).astype(BF16)
        gub_ref[:, cols] += add_rows(back_hidden.astype(F32))
        gu[:, cols] += dot_tn(normed_low, back_hidden)
        back_normed = back_normed + dot_nt(back_hidden, wu_ref[:, cols])
    gvec_ref[1:2] += add_rows(back_normed * unit1)
    gvec_ref[2:3] += add_rows(back_normed)
    back_resid = norm_back(back_normed, gain1, unit1, scale1)
    resid_ref[...] = back_resid
    back_branch = back_resid.astype(BF16)
    gvec_ref[0:1] += add_rows(back_branch.astype(F32))
    go[...] += dot_tn(mixed, back_branch)
    back_mixed = dot_nt(back_branch, wo_ref[...])
    inverse = 1.0 / den_ref[...]
    back_numer = back_mixed * inverse
    product = back_numer * mixed.astype(F32)
    high = product.astype(BF16)
    rest = (product - high.astype(F32)).astype(BF16)
    same_head = (
        lax.broadcasted_iota(jnp.int32, (2 * LANES, 2 * LANES), 0) // HEAD
        == lax.broadcasted_iota(jnp.int32, (2 * LANES, 2 * LANES), 1) // HEAD
    ).astype(F32).astype(BF16)
    even_lane = lax.broadcasted_iota(jnp.int32, (rows, LANES), 1) % 2 == 0
    for block in range(width // (2 * LANES)):
        cols = slice(block * 2 * LANES, (block + 1) * 2 * LANES)
        sums = dot_nn(high[:, cols], same_head) + dot_nn(rest[:, cols], same_head)
        for inside in range(2):
            pair = 2 * block + inside
            back = -sums[:, inside * LANES : (inside + 1) * LANES]
            back_high = back.astype(BF16).astype(F32)
            spread = swap(jnp.where(even_lane, back_high, back - back_high) * (2.0 / HEAD))
            numer = back_numer[:, pair * LANES : (pair + 1) * LANES]
            e_ref[:, (2 * pair) * LANES : (2 * pair + 1) * LANES] = jnp.where(
                low, numer, spread
            ).astype(BF16)
            e_ref[:, (2 * pair + 1) * LANES : (2 * pair + 2) * LANES] = jnp.where(
                low, spread, numer
            ).astype(BF16)

    @pl.when(step == pl.num_programs(0) - 1)
    def _():
        copies = [
            pltpu.make_async_copy(source, target, sems.at[n])
            for n, (source, target) in enumerate(((go, go_hbm), (gu, gu_hbm), (gd, gd_hbm)))
        ]
        for copy in copies:
            copy.start()
        for copy in copies:
            copy.wait()


def middle_call(x, ct, mixed, den, vec, ubias, wo, wu, wd, tiles=4):
    total, width = x.shape
    hidden_width = wu.shape[1]
    row = lambda n: pl.BlockSpec((ROWS, n), lambda i: (i, 0))
    once = lambda shape: pl.BlockSpec(
        shape, lambda i: (0,) * len(shape), pipeline_mode=pl.Buffered(1)
    )
    keep = lambda shape: pl.BlockSpec(shape, lambda i: (0,) * len(shape))
    anywhere = pl.BlockSpec(memory_space=pl.ANY)
    wide = HEADS * LANES
    return pl.pallas_call(
        functools.partial(middle, tiles),
        grid=(total // ROWS,),
        in_specs=[
            row(width),
            row(width),
            row(width),
            row(width),
            once(vec.shape),
            once(ubias.shape),
            once(wo.shape),
            once(wu.shape),
            once(wd.shape),
        ],
        out_specs=[
            row(width),
            row(width),
            row(wide),
            anywhere,
            anywhere,
            anywhere,
            keep((8, width)),
            keep((1, hidden_width)),
        ],
        out_shape=[
            jax.ShapeDtypeStruct((total, width), BF16),
            jax.ShapeDtypeStruct((total, width), F32),
            jax.ShapeDtypeStruct((total, wide), BF16),
            jax.ShapeDtypeStruct(wo.shape, F32),
            jax.ShapeDtypeStruct(wu.shape, F32),
            jax.ShapeDtypeStruct(wd.shape, F32),
            jax.ShapeDtypeStruct((8, width), F32),
            jax.ShapeDtypeStruct((1, hidden_width), F32),
        ],
        scratch_shapes=[
            pltpu.VMEM((ROWS, hidden_width), BF16),
            pltpu.VMEM((ROWS, hidden_width), BF16),
            pltpu.VMEM(wo.shape, F32),
            pltpu.VMEM(wu.shape, F32),
            pltpu.VMEM(wd.shape, F32),
            pltpu.SemaphoreType.DMA((3,)),
        ],
        compiler_params=pltpu.CompilerParams(
            dimension_semantics=("arbitrary",), vmem_limit_bytes=VMEM_LIMIT
        ),
        name="middle",
    )(x, ct, mixed, den, vec, ubias, wo, wu, wd)


def attend_backward(
    x_ref,
    a_ref,
    k_ref,
    v_ref,
    e_ref,
    s_ref,
    sq_ref,
    sk_ref,
    cs_ref,
    resid_ref,
    w_ref,
    grad_ref,
    gw_ref,
    gb_ref,
    after,
    back,
):
    rows, width = x_ref.shape

    @pl.when((pl.program_id(0) == 0) & (pl.program_id(1) == 0))
    def _():
        gw_ref[...] = jnp.zeros_like(gw_ref)
        gb_ref[...] = jnp.zeros_like(gb_ref)

    @pl.when(pl.program_id(1) == 0)
    def _():
        after[...] = jnp.zeros_like(after)

    cs = cs_ref[...]
    low = low_lanes(rows)
    i = lax.broadcasted_iota(jnp.int32, (rows, rows), 0)
    j = lax.broadcasted_iota(jnp.int32, (rows, rows), 1)
    causal, anti = i >= j, i <= j
    for pair in range(PAIRS):
        both = v_ref[:, pair * LANES : (pair + 1) * LANES].astype(F32)
        back_q, back_k, back_v = [], [], []
        for odd in range(2):
            head = 2 * pair + odd
            cols = slice(head * LANES, (head + 1) * LANES)
            query, key, e = a_ref[:, cols], k_ref[:, cols], e_ref[:, cols]
            wide = (jnp.where(low, 1.0, both) if odd else jnp.where(low, both, 1.0)).astype(BF16)
            state = s_ref[head]
            later = after[head]
            later_low = later.astype(BF16)
            scores_t = jnp.where(anti, dot_nt(key, query), 0.0).astype(BF16)
            back_s = jnp.where(causal, dot_nt(e, wide), 0.0).astype(BF16)
            back_st = jnp.where(anti, dot_nt(wide, e), 0.0).astype(BF16)
            y = (dot_nn(back_s, key) + dot_nt(e, state)) * cs
            back_q.append(y + swap(y))
            y = (dot_nn(back_st, query) + dot_nt(wide, later_low)) * cs
            back_k.append(y + swap(y))
            back_v.append(dot_nn(scores_t, e) + dot_nn(key, later_low))
            after[head] = later + dot_tn(query, e)
        cols = slice(pair * LANES, (pair + 1) * LANES)
        dq = jnp.where(low, back_q[0], back_q[1]) * sq_ref[:, cols].astype(F32)
        dk = jnp.where(low, back_k[0], back_k[1]) * sk_ref[:, cols].astype(F32)
        dv = jnp.where(low, back_v[0], back_v[1])
        for n, piece in enumerate((dq, dk, dv)):
            back[:, n * width + pair * LANES : n * width + (pair + 1) * LANES] = piece.astype(BF16)
    x = x_ref[...]
    total = resid_ref[...]
    for n in range(3):
        cols = slice(n * width, (n + 1) * width)
        piece = back[:, cols]
        gb_ref[:, cols] += add_rows(piece.astype(F32))
        gw_ref[:, cols] += dot_tn(x, piece)
        total = total + dot_nt(piece, w_ref[:, cols])
    grad_ref[...] = total


def backward_call(x, a, k, v, e, s, sq, sk, cs, resid, w, chunks):
    total, width = x.shape
    seqs = total // (chunks * CHUNK)
    place = lambda s, c: s * chunks + chunks - 1 - c
    row = lambda n: pl.BlockSpec((CHUNK, n), lambda s, c: (place(s, c), 0))
    once = lambda shape: pl.BlockSpec(
        shape, lambda s, c: (0,) * len(shape), pipeline_mode=pl.Buffered(1)
    )
    keep = lambda shape: pl.BlockSpec(shape, lambda s, c: (0,) * len(shape))
    wide = HEADS * LANES
    return pl.pallas_call(
        attend_backward,
        grid=(seqs, chunks),
        in_specs=[
            row(width),
            row(wide),
            row(wide),
            row(width),
            row(wide),
            pl.BlockSpec((None, HEADS, LANES, LANES), lambda s, c: (place(s, c), 0, 0, 0)),
            row(width),
            row(width),
            row(LANES),
            row(width),
            once(w.shape),
        ],
        out_specs=[row(width), keep(w.shape), keep((1, w.shape[1]))],
        out_shape=[
            jax.ShapeDtypeStruct((total, width), F32),
            jax.ShapeDtypeStruct(w.shape, F32),
            jax.ShapeDtypeStruct((1, w.shape[1]), F32),
        ],
        scratch_shapes=[
            pltpu.VMEM((HEADS, LANES, LANES), F32),
            pltpu.VMEM((CHUNK, w.shape[1]), BF16),
        ],
        compiler_params=pltpu.CompilerParams(
            dimension_semantics=("arbitrary", "arbitrary"), vmem_limit_bytes=VMEM_LIMIT
        ),
        name="attend_backward",
    )(x, a, k, v, e, s, sq, sk, cs, resid, w)


def block(x, ct, horizon, wqkv, bqkv, wo, vec, wu, ubias, wd):
    seqs, length, width = x.shape
    chunks = length // CHUNK
    position = jnp.arange(length, dtype=F32)
    angles = 0.5 * math.pi * position[None, :] / horizon.astype(F32)[:, None]
    cs = jnp.concatenate(
        [
            jnp.broadcast_to(jnp.cos(angles)[..., None], (seqs, length, HEAD)),
            jnp.broadcast_to(jnp.sin(angles)[..., None], (seqs, length, HEAD)),
        ],
        axis=-1,
    ).reshape(seqs * length, LANES)
    x = x.reshape(seqs * length, width)
    ct = ct.reshape(seqs * length, width)
    a, k, v, sq, sk, mixed, den, s = forward_call(x, wqkv, bqkv, cs, chunks)
    out, resid, e, go, gu, gd, gvec, gub = middle_call(x, ct, mixed, den, vec, ubias, wo, wu, wd)
    grad, gw, gb = backward_call(x, a, k, v, e, s, sq, sk, cs, resid, wqkv, chunks)
    return out, grad, gw, gb, go, gu, gd, gvec, gub


DEPTH, PLANE = 4, 4


class Place:
    def __init__(self):
        self.dp, self.core = lax.axis_index("dp"), lax.axis_index("seq")
        self.z, self.spot = self.dp // PLANE, self.dp % PLANE
        self.other = 1 - self.core
        self.across_x = self.spot + 1 - 2 * (self.spot % 2)
        self.across_y = (self.spot + 2) % PLANE
        self.diagonal = PLANE - 1 - self.spot
        self.x_peer = (self.z * PLANE + self.across_x, self.core)
        self.y_peer = (self.z * PLANE + self.across_y, self.core)
        self.sibling = (self.dp, self.other)

    def level(self, step):
        return (self.z + step) % DEPTH

    def z_peer(self, step):
        return (self.level(step) * PLANE + self.spot, self.core)


def remote(source, target, send, recv, peer):
    copy = pltpu.make_async_remote_copy(
        src_ref=source,
        dst_ref=target,
        send_sem=send,
        recv_sem=recv,
        device_id=peer,
        device_id_type=pl.DeviceIdType.MESH,
    )
    return copy


def meet(here):
    barrier = pltpu.get_barrier_semaphore()
    peers = [here.x_peer, here.y_peer, here.sibling] + [here.z_peer(n) for n in range(1, DEPTH)]
    for peer in peers:
        pl.semaphore_signal(barrier, inc=1, device_id=peer, device_id_type=pl.DeviceIdType.MESH)
    pl.semaphore_wait(barrier, len(peers))


def gather_body(x_ref, ct_ref, q_ref, k_ref, v_ref, o_ref, u_ref, d_ref, b_ref,
                xs_ref, cts_ref, qkv_out, o_out, u_out, d_out, b_out,
                local_sem, swap_sem, z_send, x_send, y_send, c_send, link_recv, core_recv):
    here = Place()
    width = q_ref.shape[1]
    outs = (b_out, qkv_out, o_out, u_out, d_out)
    heights = [out.shape[0] // (DEPTH * PLANE) for out in outs]
    count = len(outs)

    def rows(t, level, spot):
        return pl.ds(pl.multiple_of((level * PLANE + spot) * heights[t], heights[t]), heights[t])

    def piece(t, level, spot):
        half = heights[t] // 2
        start = (level * PLANE + spot) * heights[t] + here.core * half
        return outs[t].at[pl.ds(pl.multiple_of(start, half), half), :]

    own = [None] * count
    own[0] = [(b_ref, b_out.at[rows(0, here.z, here.spot), :])]
    own[1] = [
        (ref, qkv_out.at[rows(1, here.z, here.spot), n * width : (n + 1) * width])
        for n, ref in enumerate((q_ref, k_ref, v_ref))
    ]
    own[2] = [(o_ref, o_out.at[rows(2, here.z, here.spot), :])]
    own[3] = [(u_ref, u_out.at[rows(3, here.z, here.spot), :])]
    own[4] = [(d_ref, d_out.at[rows(4, here.z, here.spot), :])]
    locals_of = []
    n = 0
    for t in range(count):
        copies = []
        for source, target in own[t]:
            copies.append(pltpu.make_async_copy(source, target, local_sem.at[n]))
            copies[-1].start()
            n += 1
        locals_of.append(copies)
    meet(here)
    pairs = x_ref.shape[0] // 2
    block = x_ref.shape[1]
    swaps = []
    for n, (source, target) in enumerate(((x_ref, xs_ref), (ct_ref, cts_ref))):
        place = pl.ds(pl.multiple_of(here.core * block, block), block)
        keep = pltpu.make_async_copy(
            source.at[pl.ds(here.core * pairs, pairs)], target.at[:, place, :], swap_sem.at[n, 0]
        )
        give = remote(
            source.at[pl.ds(here.other * pairs, pairs)],
            target.at[:, place, :],
            swap_sem.at[n, 1],
            swap_sem.at[n, 2],
            here.sibling,
        )
        keep.start()
        give.start()
        swaps += [keep, give]
    sends = []

    def send(t, level, spot, kind):
        at = (t, level * PLANE + spot)
        ref = piece(t, level, spot)
        sem, peer, arrive = {
            "x": (x_send, here.x_peer, link_recv),
            "y": (y_send, here.y_peer, link_recv),
            "c": (c_send, here.sibling, core_recv),
        }[kind]
        copy = remote(ref, ref, sem.at[at], arrive.at[at], peer)
        copy.start()
        sends.append(copy)

    def arrived(t, level, spot, sem):
        ref = piece(t, level, spot)
        remote(ref, ref, sem.at[t, level * PLANE + spot], sem.at[t, level * PLANE + spot], here.x_peer).wait_recv()

    def begin(t):
        for copy in locals_of[t]:
            copy.wait()
        ref = piece(t, here.z, here.spot)
        for n in range(1, DEPTH):
            at = (t, here.z * PLANE + here.spot)
            copy = remote(ref, ref, z_send.at[t, n], link_recv.at[at], here.z_peer(n))
            copy.start()
            sends.append(copy)
        send(t, here.z, here.spot, "x")
        send(t, here.z, here.spot, "y")

    def column(t):
        for n in (1, 3, 2):
            arrived(t, here.level(n), here.spot, link_recv)
            for kind in "xyc":
                send(t, here.level(n), here.spot, kind)

    def cross(t):
        for n in (0, 1, 3, 2):
            arrived(t, here.level(n), here.across_x, link_recv)
            if n < 2:
                send(t, here.level(n), here.across_x, "y")
            send(t, here.level(n), here.across_x, "c")
            arrived(t, here.level(n), here.across_y, link_recv)
            if n >= 2:
                send(t, here.level(n), here.across_y, "x")
            send(t, here.level(n), here.across_y, "c")

    def corner(t):
        for n in range(DEPTH):
            arrived(t, here.level(n), here.diagonal, link_recv)
            send(t, here.level(n), here.diagonal, "c")

    def finish(t):
        for n in range(DEPTH):
            for spot in (here.spot, here.across_x, here.across_y, here.diagonal):
                if n == 0 and spot is here.spot:
                    continue
                half = heights[t] // 2
                start = (here.level(n) * PLANE + spot) * heights[t] + here.other * half
                ref = outs[t].at[pl.ds(pl.multiple_of(start, half), half), :]
                sem = core_recv.at[t, here.level(n) * PLANE + spot]
                remote(ref, ref, sem, sem, here.sibling).wait_recv()

    for t in range(count):
        begin(t)
    for step in range(count + 3):
        for lag, stage in enumerate((column, cross, corner, finish)):
            if 0 <= step - lag < count:
                stage(step - lag)
    for copy in swaps:
        copy.wait()
    for copy in sends:
        copy.wait_send()


def gather_call(x, ct, q, k, v, o, u, d, b):
    chips = DEPTH * PLANE
    anywhere = pl.BlockSpec(memory_space=pl.ANY)
    shape = lambda rows, cols: jax.ShapeDtypeStruct((rows, cols), BF16)
    swapped = jax.ShapeDtypeStruct((x.shape[0] // 2, x.shape[1] * 2, x.shape[2]), BF16)
    count = 5
    sem = pltpu.SemaphoreType.DMA
    return pl.pallas_call(
        gather_body,
        in_specs=[anywhere] * 9,
        out_specs=[anywhere] * 7,
        out_shape=[
            swapped,
            swapped,
            shape(q.shape[0] * chips, 3 * q.shape[1]),
            shape(o.shape[0] * chips, o.shape[1]),
            shape(u.shape[0] * chips, u.shape[1]),
            shape(d.shape[0] * chips, d.shape[1]),
            shape(b.shape[0] * chips, b.shape[1]),
        ],
        scratch_shapes=[
            sem((7,)),
            sem((2, 3)),
            sem((count, DEPTH)),
            sem((count, chips)),
            sem((count, chips)),
            sem((count, chips)),
            sem((count, chips)),
            sem((count, chips)),
        ],
        compiler_params=pltpu.CompilerParams(collective_id=0, has_side_effects=True),
        name="gather_weights",
    )(x, ct, q, k, v, o, u, d, b)


def scatter_body(out_ref, grad_ref, g0, g1, g2, g3, g4,
                 out4_ref, grad4_ref, r_q, r_k, r_v, r_o, r_u, r_d, r_b, *scratch):
    grads = (g0, g1, g2, g3, g4)
    count = len(grads)
    own = scratch[0:5]
    got = scratch[5:10]
    corner_x = scratch[10:15]
    corner_y = scratch[15:20]
    side_x = scratch[20:25]
    side_y = scratch[25:30]
    column = scratch[30:35]
    final = scratch[35:40]
    swap_sem, load_sem, core_send, core_recv, send_sem, recv_sem, z_send, z_recv, last_sem = scratch[40:]
    here = Place()
    half = [g.shape[2] // 2 for g in grads]
    groups = (here.diagonal, here.across_x, here.across_y, here.spot)
    width = r_q.shape[1]
    loads, gives = {}, {}
    for t in range(count):
        for n, spot in enumerate(groups):
            mine = pl.ds(pl.multiple_of(here.core * half[t], half[t]), half[t])
            loads[t, n] = pltpu.make_async_copy(
                grads[t].at[:, spot, mine, :], own[t].at[n], load_sem.at[t, n]
            )
            loads[t, n].start()
    meet(here)
    for t in range(count):
        for n, spot in enumerate(groups):
            theirs = pl.ds(pl.multiple_of(here.other * half[t], half[t]), half[t])
            gives[t, n] = remote(
                grads[t].at[:, spot, theirs, :],
                got[t].at[n],
                core_send.at[t, n],
                core_recv.at[t, n],
                here.sibling,
            )
            gives[t, n].start()
    block = out4_ref.shape[1]
    pairs = out_ref.shape[0]
    swaps = []
    for n, (source, target) in enumerate(((out_ref, out4_ref), (grad_ref, grad4_ref))):
        keep = pltpu.make_async_copy(
            source.at[:, pl.ds(pl.multiple_of(here.core * block, block), block), :],
            target.at[pl.ds(here.core * pairs, pairs)],
            swap_sem.at[n, 0],
        )
        give = remote(
            source.at[:, pl.ds(pl.multiple_of(here.other * block, block), block), :],
            target.at[pl.ds(here.core * pairs, pairs)],
            swap_sem.at[n, 1],
            swap_sem.at[n, 2],
            here.sibling,
        )
        keep.start()
        give.start()
        swaps += [keep, give]
    sends = []

    def add(t, n, z, others):
        total = own[t][n, z].astype(F32)
        for other in others:
            total = total + other.astype(F32)
        return total

    def joined(t, n):
        loads[t, n].wait()
        gives[t, n].wait_recv()

    def push(t, slot, source, target, peer):
        copy = remote(source, target, send_sem.at[t, slot], recv_sem.at[t, slot], peer)
        copy.start()
        sends.append(copy)
        return copy

    pushed = {}

    def first(t):
        joined(t, 0)
        for z in range(DEPTH):
            own[t][0, z] = add(t, 0, z, [got[t][0, z]]).astype(own[t].dtype)
        pushed[t, 0] = push(t, 0, own[t].at[0, 0:2], corner_x[t], here.x_peer)
        pushed[t, 1] = push(t, 1, own[t].at[0, 2:4], corner_y[t], here.y_peer)

    def second(t):
        joined(t, 1)
        joined(t, 2)
        pushed[t, 0].wait_recv()
        pushed[t, 1].wait_recv()
        for z in range(DEPTH):
            extra = [corner_y[t][z - 2]] if z >= 2 else []
            own[t][1, z] = add(t, 1, z, [got[t][1, z]] + extra).astype(own[t].dtype)
            extra = [corner_x[t][z]] if z < 2 else []
            own[t][2, z] = add(t, 2, z, [got[t][2, z]] + extra).astype(own[t].dtype)
        pushed[t, 2] = push(t, 2, own[t].at[1], side_x[t], here.x_peer)
        pushed[t, 3] = push(t, 3, own[t].at[2], side_y[t], here.y_peer)

    def third(t):
        joined(t, 3)
        pushed[t, 2].wait_recv()
        pushed[t, 3].wait_recv()
        for z in range(DEPTH):
            total = add(t, 3, z, [got[t][3, z], side_x[t][z], side_y[t][z]])
            own[t][3, z] = total.astype(own[t].dtype)
        for n in range(1, DEPTH):
            copy = remote(
                own[t].at[3, here.level(n)],
                column[t].at[n],
                z_send.at[t, n],
                z_recv.at[t, n],
                here.z_peer(n),
            )
            copy.start()
            sends.append(copy)
            pushed[t, 3 + n] = copy

    def fourth(t):
        for n in range(1, DEPTH):
            pushed[t, 3 + n].wait_recv()
        total = own[t][3, here.z].astype(F32)
        for n in range(1, DEPTH):
            total = total + column[t][n].astype(F32)
        final[t][...] = total
        if t == 1:
            targets = [(final[t].at[:, n * width : (n + 1) * width], r) for n, r in enumerate((r_q, r_k, r_v))]
        else:
            targets = [(final[t], {0: r_b, 2: r_o, 3: r_u, 4: r_d}[t])]
        for m, (source, target) in enumerate(targets):
            place = target.at[pl.ds(pl.multiple_of(here.core * half[t], half[t]), half[t]), :]
            keep = pltpu.make_async_copy(source, place, last_sem.at[t, m, 0])
            give = remote(source, place, last_sem.at[t, m, 1], last_sem.at[t, m, 2], here.sibling)
            keep.start()
            give.start()
            swaps.extend((keep, give))

    order = (4, 3, 2, 1, 0)
    for step in range(count + 3):
        for lag, stage in enumerate((first, second, third, fourth)):
            if 0 <= step - lag < count:
                stage(order[step - lag])
    for copy in swaps:
        copy.wait()
    for copy in gives.values():
        copy.wait_send()
    for copy in sends:
        copy.wait_send()


def scatter_call(out, grad, gb, gqkv, go, gu, gd):
    chips = DEPTH * PLANE
    anywhere = pl.BlockSpec(memory_space=pl.ANY)
    grads = (gb, gqkv, go, gu, gd)
    views = [g.reshape(DEPTH, PLANE, g.shape[0] // chips, g.shape[1]) for g in grads]
    parts = [(g.shape[2] // 2, g.shape[3], g.dtype) for g in views]
    sem = pltpu.SemaphoreType.DMA
    count = len(grads)
    scratch = []
    for lead in ((4, DEPTH), (4, DEPTH), (2,), (2,), (DEPTH,), (DEPTH,), (DEPTH,)):
        scratch += [pltpu.VMEM(lead + (h, w), dtype) for h, w, dtype in parts]
    scratch += [pltpu.VMEM((h, w), F32) for h, w, _ in parts]
    scratch += [
        sem((2, 3)),
        sem((count, 4)),
        sem((count, 4)),
        sem((count, 4)),
        sem((count, 4)),
        sem((count, 4)),
        sem((count, DEPTH)),
        sem((count, DEPTH)),
        sem((count, 3, 3)),
    ]
    swapped = lambda a: jax.ShapeDtypeStruct((a.shape[0] * 2, a.shape[1] // 2, a.shape[2]), a.dtype)
    shard = lambda g, w: jax.ShapeDtypeStruct((g.shape[2], w), F32)
    width = gqkv.shape[1] // 3
    return pl.pallas_call(
        scatter_body,
        in_specs=[anywhere] * 7,
        out_specs=[anywhere] * 9,
        out_shape=[
            swapped(out),
            swapped(grad),
            shard(views[1], width),
            shard(views[1], width),
            shard(views[1], width),
            shard(views[2], views[2].shape[3]),
            shard(views[3], views[3].shape[3]),
            shard(views[4], views[4].shape[3]),
            shard(views[0], views[0].shape[3]),
        ],
        scratch_shapes=scratch,
        compiler_params=pltpu.CompilerParams(
            collective_id=1, has_side_effects=True, vmem_limit_bytes=VMEM_LIMIT
        ),
        name="scatter_gradients",
    )(out, grad, *views)


def pack_vectors(vectors, up_bias):
    part = vectors[0].shape[0]
    stacked = jnp.concatenate([jnp.stack(vectors), up_bias.reshape(-1, part)])
    return jnp.pad(stacked, ((0, 16 - stacked.shape[0]), (0, LANES - part)))


def unpack_vectors(gathered, part):
    chips = gathered.shape[0] // 16
    grid = gathered.reshape(chips, 16, LANES)[:, :13, :part].astype(F32)
    rows = jnp.transpose(grid[:, :9], (1, 0, 2)).reshape(9, chips * part)
    up_bias = grid[:, 9:].reshape(1, chips * 4 * part)
    return rows[0:3].reshape(1, -1), jnp.pad(rows[3:9], ((0, 2), (0, 0))), up_bias


def pack_vector_grads(gb, gvec, gub, chips):
    width = gvec.shape[1]
    part = width // chips
    rows = jnp.concatenate([gb.reshape(3, width), gvec[0:6]]).reshape(9, chips, part)
    rows = jnp.transpose(rows, (1, 0, 2))
    grid = jnp.concatenate([rows, gub.reshape(chips, 4, part)], axis=1)
    grid = jnp.pad(grid, ((0, 0), (0, 3), (0, LANES - part)))
    return grid.reshape(chips * 16, LANES)


def local(
    inputs,
    horizon,
    query_weight,
    query_bias,
    key_weight,
    key_bias,
    value_weight,
    value_bias,
    out_weight,
    out_bias,
    first_gain,
    first_shift,
    up_weight,
    up_bias,
    down_weight,
    down_bias,
    second_gain,
    second_shift,
    cotangent,
):
    chips = lax.axis_size("dp")
    core = lax.axis_index("seq")
    part = query_bias.shape[0]
    seqs = inputs.shape[0] // 2
    direct = chips == DEPTH * PLANE
    vectors = pack_vectors(
        (
            query_bias,
            key_bias,
            value_bias,
            out_bias,
            first_gain,
            first_shift,
            down_bias,
            second_gain,
            second_shift,
        ),
        up_bias,
    )
    weights = (query_weight, key_weight, value_weight, out_weight, up_weight, down_weight)
    if direct:
        x, ct, wqkv, wo, wu, wd, gathered = gather_call(inputs, cotangent, *weights, vectors)
    else:
        gather = lambda a: lax.all_gather(a, "dp", axis=0, tiled=True)
        x, ct = (lax.all_to_all(a, "seq", 0, 1, tiled=True) for a in (inputs, cotangent))
        wqkv = gather(jnp.concatenate(weights[:3], axis=1))
        wo, wu, wd, gathered = (gather(a) for a in (*weights[3:], vectors))
    bqkv, vec, ubias = unpack_vectors(gathered, part)
    spans = lax.dynamic_slice_in_dim(horizon, core * seqs, seqs)
    out, grad, gw, gb, go, gu, gd, gvec, gub = block(
        x, ct, spans, wqkv, bqkv, wo, vec, wu, ubias, wd
    )
    out, grad = out.reshape(x.shape), grad.reshape(x.shape)
    gvectors = pack_vector_grads(gb, gvec, gub, chips)
    if direct:
        out, grad, gq, gk, gv, go, gu, gd, gvectors = scatter_call(
            out, grad, gvectors, *(g.astype(BF16) for g in (gw, go, gu, gd))
        )
    else:
        out, grad = (lax.all_to_all(a, "seq", 1, 0, tiled=True) for a in (out, grad))
        total = lambda g: lax.psum(
            lax.psum_scatter(g, "dp", scatter_dimension=0, tiled=True), "seq"
        )
        gw, go, gu, gd, gvectors = (total(g) for g in (gw, go, gu, gd, gvectors))
        gq, gk, gv = jnp.split(gw, 3, axis=1)
    rows = gvectors[:, :part]
    return (
        out,
        grad,
        gq,
        rows[0],
        gk,
        rows[1],
        gv,
        rows[2],
        go,
        rows[3],
        rows[4],
        rows[5],
        gu,
        rows[9:13].reshape(-1),
        gd,
        rows[6],
        rows[7],
        rows[8],
    )


def solution(mesh):
    long, wide, thin = P("dp", "seq", None), P("dp", None), P("dp")
    shards = (wide, thin, wide, thin, wide, thin, wide, thin, thin, thin, wide, thin, wide, thin, thin, thin)
    return jax.shard_map(
        local,
        mesh=mesh,
        in_specs=(long, thin, *shards, long),
        out_specs=(long, long, *shards),
        check_vma=False,
    )
```

```python
import functools
import math

import jax
import jax.numpy as jnp
from jax import lax
from jax.experimental import pallas as pl
from jax.experimental.pallas import tpu as pltpu
from jax.sharding import PartitionSpec as P

HEADS = 12
HEAD = 64
PAIRS = HEADS // 2
LANES = 128
CHUNK = 256
ROWS = 256
NORM_EPS = 1e-05
GELU_A = 0.7978845608
GELU_B = 0.044715
VMEM_LIMIT = 60 * 1024 * 1024
F32, BF16 = jnp.float32, jnp.bfloat16


def dot_nn(a, b):
    return lax.dot_general(a, b, (((1,), (0,)), ((), ())), preferred_element_type=F32)


def dot_nt(a, b):
    return lax.dot_general(a, b, (((1,), (1,)), ((), ())), preferred_element_type=F32)


def dot_tn(a, b):
    return lax.dot_general(a, b, (((0,), (0,)), ((), ())), preferred_element_type=F32)


def low_lanes(rows):
    return lax.broadcasted_iota(jnp.int32, (rows, LANES), 1) < HEAD


def swap(values):
    return pltpu.roll(values, HEAD, 1)


def softplus_and_slope(values):
    e = jnp.exp(-jnp.abs(values))
    plus = jnp.maximum(values, 0.0) + jnp.log1p(e)
    slope = jnp.where(values >= 0.0, 1.0, e) / (1.0 + e)
    return plus, slope


def attend_forward(
    x_ref, w_ref, b_ref, cs_ref, a_ref, k_ref, v_ref, sq_ref, sk_ref, mixed_ref, den_ref, s_ref, state
):
    width = x_ref.shape[1]
    rows = x_ref.shape[0]

    @pl.when(pl.program_id(1) == 0)
    def _():
        state[...] = jnp.zeros_like(state)

    x = x_ref[...]
    cs = cs_ref[...]
    low = low_lanes(rows)
    causal = lax.broadcasted_iota(jnp.int32, (rows, rows), 0) >= lax.broadcasted_iota(
        jnp.int32, (rows, rows), 1
    )

    for half in range(2):
        slope_ref = (sq_ref, sk_ref)[half]
        feature_ref = (a_ref, k_ref)[half]
        pre = dot_nn(x, w_ref[:, half * width : (half + 1) * width])
        pre = pre + b_ref[:, half * width : (half + 1) * width]
        plus, slope = softplus_and_slope(pre)
        slope_ref[...] = slope.astype(BF16)
        for pair in range(PAIRS):
            both = plus[:, pair * LANES : (pair + 1) * LANES]
            other = swap(both)
            even = jnp.where(low, both, other) * cs
            odd = jnp.where(low, other, both) * cs
            feature_ref[:, (2 * pair) * LANES : (2 * pair + 1) * LANES] = even.astype(BF16)
            feature_ref[:, (2 * pair + 1) * LANES : (2 * pair + 2) * LANES] = odd.astype(BF16)
    values = dot_nn(x, w_ref[:, 2 * width :]) + b_ref[:, 2 * width :]
    v_ref[...] = values.astype(BF16)
    for pair in range(PAIRS):
        both = values[:, pair * LANES : (pair + 1) * LANES]
        results = []
        for odd in range(2):
            head = 2 * pair + odd
            query = a_ref[:, head * LANES : (head + 1) * LANES]
            key = k_ref[:, head * LANES : (head + 1) * LANES]
            wide = (jnp.where(low, 1.0, both) if odd else jnp.where(low, both, 1.0)).astype(BF16)
            scores = jnp.where(causal, dot_nt(query, key), 0.0).astype(BF16)
            before = state[head]
            before_low = before.astype(BF16)
            s_ref[head] = before_low
            results.append(dot_nn(scores, wide) + dot_nn(query, before_low))
            state[head] = before + dot_tn(key, wide)
        numer = jnp.where(low, results[0], results[1])
        denom = swap(jnp.where(low, results[1], results[0]))
        mixed_ref[:, pair * LANES : (pair + 1) * LANES] = (numer / denom).astype(BF16)
        den_ref[:, pair * LANES : (pair + 1) * LANES] = denom


def forward_call(x, w, b, cs, chunks):
    total, width = x.shape
    seqs = total // (chunks * CHUNK)
    row = lambda n: pl.BlockSpec((CHUNK, n), lambda s, c: (s * chunks + c, 0))
    once = lambda shape: pl.BlockSpec(
        shape, lambda s, c: (0,) * len(shape), pipeline_mode=pl.Buffered(1)
    )
    wide = HEADS * LANES
    return pl.pallas_call(
        attend_forward,
        grid=(seqs, chunks),
        in_specs=[row(width), once(w.shape), once(b.shape), row(LANES)],
        out_specs=[
            row(wide),
            row(wide),
            row(width),
            row(width),
            row(width),
            row(width),
            row(width),
            pl.BlockSpec((None, HEADS, LANES, LANES), lambda s, c: (s * chunks + c, 0, 0, 0)),
        ],
        out_shape=[
            jax.ShapeDtypeStruct((total, wide), BF16),
            jax.ShapeDtypeStruct((total, wide), BF16),
            jax.ShapeDtypeStruct((total, width), BF16),
            jax.ShapeDtypeStruct((total, width), BF16),
            jax.ShapeDtypeStruct((total, width), BF16),
            jax.ShapeDtypeStruct((total, width), BF16),
            jax.ShapeDtypeStruct((total, width), F32),
            jax.ShapeDtypeStruct((seqs * chunks, HEADS, LANES, LANES), BF16),
        ],
        scratch_shapes=[pltpu.VMEM((HEADS, LANES, LANES), F32)],
        compiler_params=pltpu.CompilerParams(
            dimension_semantics=("arbitrary", "arbitrary"), vmem_limit_bytes=VMEM_LIMIT
        ),
        name="attend_forward",
    )(x, w, b, cs)


def row_mean(values):
    return jnp.mean(values, axis=-1, keepdims=True)


def norm_parts(values):
    center = values - row_mean(values)
    scale = lax.rsqrt(row_mean(center * center) + NORM_EPS)
    return center * scale, scale


def norm_back(grad, gain, unit, scale):
    scaled = grad * gain
    return (scaled - row_mean(scaled) - unit * row_mean(scaled * unit)) * scale


def add_rows(values):
    return jnp.sum(values, axis=0, keepdims=True)


def middle(
    tiles,
    x_ref,
    ct_ref,
    mixed_ref,
    den_ref,
    vec_ref,
    ubias_ref,
    wo_ref,
    wu_ref,
    wd_ref,
    out_ref,
    resid_ref,
    e_ref,
    go_hbm,
    gu_hbm,
    gd_hbm,
    gvec_ref,
    gub_ref,
    act,
    slope,
    go,
    gu,
    gd,
    stage,
    sems,
):
    step = pl.program_id(0)
    rows, width = x_ref.shape
    hidden_width = wu_ref.shape[1]
    tile = hidden_width // tiles
    low = low_lanes(rows)

    @pl.when(step == 0)
    def _():
        go[...] = jnp.zeros_like(go)
        gu[...] = jnp.zeros_like(gu)
        gd[...] = jnp.zeros_like(gd)
        gvec_ref[...] = jnp.zeros_like(gvec_ref)
        gub_ref[...] = jnp.zeros_like(gub_ref)

    out_bias, gain1, shift1 = vec_ref[0:1], vec_ref[1:2], vec_ref[2:3]
    down_bias, gain2, shift2 = vec_ref[3:4], vec_ref[4:5], vec_ref[5:6]
    mixed = mixed_ref[...]
    resid = x_ref[...].astype(F32) + (dot_nn(mixed, wo_ref[...]) + out_bias)
    unit1, scale1 = norm_parts(resid)
    normed = unit1 * gain1 + shift1
    normed_low = normed.astype(BF16)
    ffn = jnp.zeros((rows, width), F32)
    for t in range(tiles):
        cols = slice(t * tile, (t + 1) * tile)
        hidden = dot_nn(normed_low, wu_ref[:, cols]) + ubias_ref[:, cols]
        square = hidden * hidden
        inner = hidden * (GELU_A + (GELU_A * GELU_B) * square)
        tanh = jnp.tanh(inner)
        half = 0.5 + 0.5 * tanh
        active = (hidden * half).astype(BF16)
        curve = half + (0.5 * hidden) * (1.0 - tanh * tanh) * (
            GELU_A + (3.0 * GELU_A * GELU_B) * square
        )
        act[:, cols] = active
        slope[:, cols] = curve.astype(BF16)
        ffn = ffn + dot_nn(active, wd_ref[cols, :])
    unit2, scale2 = norm_parts(normed + (ffn + down_bias))
    out_ref[...] = (unit2 * gain2 + shift2).astype(BF16)
    grad = ct_ref[...].astype(F32)
    back_final = norm_back(grad, gain2, unit2, scale2)
    back_ffn = back_final.astype(BF16)
    gvec_ref[4:5] += add_rows(grad * unit2)
    gvec_ref[5:6] += add_rows(grad)
    gvec_ref[3:4] += add_rows(back_ffn.astype(F32))
    back_normed = back_final
    for t in range(tiles):
        cols = slice(t * tile, (t + 1) * tile)
        gd[cols, :] += dot_tn(act[:, cols], back_ffn)
        back_active = dot_nt(back_ffn, wd_ref[cols, :])
        back_hidden = (back_active * slope[:, cols].astype(F32)).astype(BF16)
        gub_ref[:, cols] += add_rows(back_hidden.astype(F32))
        gu[:, cols] += dot_tn(normed_low, back_hidden)
        back_normed = back_normed + dot_nt(back_hidden, wu_ref[:, cols])
    gvec_ref[1:2] += add_rows(back_normed * unit1)
    gvec_ref[2:3] += add_rows(back_normed)
    back_resid = norm_back(back_normed, gain1, unit1, scale1)
    resid_ref[...] = back_resid
    back_branch = back_resid.astype(BF16)
    gvec_ref[0:1] += add_rows(back_branch.astype(F32))
    go[...] += dot_tn(mixed, back_branch)
    back_mixed = dot_nt(back_branch, wo_ref[...])
    inverse = 1.0 / den_ref[...]
    back_numer = back_mixed * inverse
    product = back_numer * mixed.astype(F32)
    high = product.astype(BF16)
    rest = (product - high.astype(F32)).astype(BF16)
    same_head = (
        lax.broadcasted_iota(jnp.int32, (2 * LANES, 2 * LANES), 0) // HEAD
        == lax.broadcasted_iota(jnp.int32, (2 * LANES, 2 * LANES), 1) // HEAD
    ).astype(F32).astype(BF16)
    even_lane = lax.broadcasted_iota(jnp.int32, (rows, LANES), 1) % 2 == 0
    for block in range(width // (2 * LANES)):
        cols = slice(block * 2 * LANES, (block + 1) * 2 * LANES)
        sums = dot_nn(high[:, cols], same_head) + dot_nn(rest[:, cols], same_head)
        for inside in range(2):
            pair = 2 * block + inside
            back = -sums[:, inside * LANES : (inside + 1) * LANES]
            back_high = back.astype(BF16).astype(F32)
            spread = swap(jnp.where(even_lane, back_high, back - back_high) * (2.0 / HEAD))
            numer = back_numer[:, pair * LANES : (pair + 1) * LANES]
            e_ref[:, (2 * pair) * LANES : (2 * pair + 1) * LANES] = jnp.where(
                low, numer, spread
            ).astype(BF16)
            e_ref[:, (2 * pair + 1) * LANES : (2 * pair + 2) * LANES] = jnp.where(
                low, spread, numer
            ).astype(BF16)

    @pl.when(step == pl.num_programs(0) - 1)
    def _():
        blocks = [(go, go_hbm, 0, 0)]
        for t in range(hidden_width // width):
            blocks.append((gu, gu_hbm, 0, t * width))
            blocks.append((gd, gd_hbm, t * width, 0))
        copies = []
        for n, (source, target, top, left) in enumerate(blocks):
            if n >= 2:
                copies[n - 2].wait()
            place = (slice(top, top + width), slice(left, left + width))
            stage[n % 2] = source[place].astype(BF16)
            copies.append(pltpu.make_async_copy(stage.at[n % 2], target.at[place], sems.at[n % 2]))
            copies[n].start()
        for copy in copies[-2:]:
            copy.wait()


def middle_call(x, ct, mixed, den, vec, ubias, wo, wu, wd, tiles=4):
    total, width = x.shape
    hidden_width = wu.shape[1]
    row = lambda n: pl.BlockSpec((ROWS, n), lambda i: (i, 0))
    once = lambda shape: pl.BlockSpec(
        shape, lambda i: (0,) * len(shape), pipeline_mode=pl.Buffered(1)
    )
    keep = lambda shape: pl.BlockSpec(shape, lambda i: (0,) * len(shape))
    anywhere = pl.BlockSpec(memory_space=pl.ANY)
    wide = HEADS * LANES
    return pl.pallas_call(
        functools.partial(middle, tiles),
        grid=(total // ROWS,),
        in_specs=[
            row(width),
            row(width),
            row(width),
            row(width),
            once(vec.shape),
            once(ubias.shape),
            once(wo.shape),
            once(wu.shape),
            once(wd.shape),
        ],
        out_specs=[
            row(width),
            row(width),
            row(wide),
            anywhere,
            anywhere,
            anywhere,
            keep((8, width)),
            keep((1, hidden_width)),
        ],
        out_shape=[
            jax.ShapeDtypeStruct((total, width), BF16),
            jax.ShapeDtypeStruct((total, width), F32),
            jax.ShapeDtypeStruct((total, wide), BF16),
            jax.ShapeDtypeStruct(wo.shape, BF16),
            jax.ShapeDtypeStruct(wu.shape, BF16),
            jax.ShapeDtypeStruct(wd.shape, BF16),
            jax.ShapeDtypeStruct((8, width), F32),
            jax.ShapeDtypeStruct((1, hidden_width), F32),
        ],
        scratch_shapes=[
            pltpu.VMEM((ROWS, hidden_width), BF16),
            pltpu.VMEM((ROWS, hidden_width), BF16),
            pltpu.VMEM(wo.shape, F32),
            pltpu.VMEM(wu.shape, F32),
            pltpu.VMEM(wd.shape, F32),
            pltpu.VMEM((2, width, width), BF16),
            pltpu.SemaphoreType.DMA((2,)),
        ],
        compiler_params=pltpu.CompilerParams(
            dimension_semantics=("arbitrary",), vmem_limit_bytes=VMEM_LIMIT
        ),
        name="middle",
    )(x, ct, mixed, den, vec, ubias, wo, wu, wd)


def attend_backward(
    x_ref,
    a_ref,
    k_ref,
    v_ref,
    e_ref,
    s_ref,
    sq_ref,
    sk_ref,
    cs_ref,
    resid_ref,
    w_ref,
    grad_ref,
    gw_ref,
    gb_ref,
    after,
    back,
    gw,
):
    rows, width = x_ref.shape

    @pl.when((pl.program_id(0) == 0) & (pl.program_id(1) == 0))
    def _():
        gw[...] = jnp.zeros_like(gw)
        gb_ref[...] = jnp.zeros_like(gb_ref)

    @pl.when(pl.program_id(1) == 0)
    def _():
        after[...] = jnp.zeros_like(after)

    cs = cs_ref[...]
    low = low_lanes(rows)
    i = lax.broadcasted_iota(jnp.int32, (rows, rows), 0)
    j = lax.broadcasted_iota(jnp.int32, (rows, rows), 1)
    causal, anti = i >= j, i <= j
    for pair in range(PAIRS):
        both = v_ref[:, pair * LANES : (pair + 1) * LANES].astype(F32)
        back_q, back_k, back_v = [], [], []
        for odd in range(2):
            head = 2 * pair + odd
            cols = slice(head * LANES, (head + 1) * LANES)
            query, key, e = a_ref[:, cols], k_ref[:, cols], e_ref[:, cols]
            wide = (jnp.where(low, 1.0, both) if odd else jnp.where(low, both, 1.0)).astype(BF16)
            state = s_ref[head]
            later = after[head]
            later_low = later.astype(BF16)
            scores_t = jnp.where(anti, dot_nt(key, query), 0.0).astype(BF16)
            back_s = jnp.where(causal, dot_nt(e, wide), 0.0).astype(BF16)
            back_st = jnp.where(anti, dot_nt(wide, e), 0.0).astype(BF16)
            y = (dot_nn(back_s, key) + dot_nt(e, state)) * cs
            back_q.append(y + swap(y))
            y = (dot_nn(back_st, query) + dot_nt(wide, later_low)) * cs
            back_k.append(y + swap(y))
            back_v.append(dot_nn(scores_t, e) + dot_nn(key, later_low))
            after[head] = later + dot_tn(query, e)
        cols = slice(pair * LANES, (pair + 1) * LANES)
        dq = jnp.where(low, back_q[0], back_q[1]) * sq_ref[:, cols].astype(F32)
        dk = jnp.where(low, back_k[0], back_k[1]) * sk_ref[:, cols].astype(F32)
        dv = jnp.where(low, back_v[0], back_v[1])
        for n, piece in enumerate((dq, dk, dv)):
            back[:, n * width + pair * LANES : n * width + (pair + 1) * LANES] = piece.astype(BF16)
    x = x_ref[...]
    total = resid_ref[...]
    for n in range(3):
        cols = slice(n * width, (n + 1) * width)
        piece = back[:, cols]
        gb_ref[:, cols] += add_rows(piece.astype(F32))
        gw[:, cols] += dot_tn(x, piece)
        total = total + dot_nt(piece, w_ref[:, cols])
    grad_ref[...] = total

    @pl.when((pl.program_id(0) == pl.num_programs(0) - 1) & (pl.program_id(1) == pl.num_programs(1) - 1))
    def _():
        gw_ref[...] = gw[...].astype(BF16)


def backward_call(x, a, k, v, e, s, sq, sk, cs, resid, w, chunks):
    total, width = x.shape
    seqs = total // (chunks * CHUNK)
    place = lambda s, c: s * chunks + chunks - 1 - c
    row = lambda n: pl.BlockSpec((CHUNK, n), lambda s, c: (place(s, c), 0))
    once = lambda shape: pl.BlockSpec(
        shape, lambda s, c: (0,) * len(shape), pipeline_mode=pl.Buffered(1)
    )
    keep = lambda shape: pl.BlockSpec(shape, lambda s, c: (0,) * len(shape))
    wide = HEADS * LANES
    return pl.pallas_call(
        attend_backward,
        grid=(seqs, chunks),
        in_specs=[
            row(width),
            row(wide),
            row(wide),
            row(width),
            row(wide),
            pl.BlockSpec((None, HEADS, LANES, LANES), lambda s, c: (place(s, c), 0, 0, 0)),
            row(width),
            row(width),
            row(LANES),
            row(width),
            once(w.shape),
        ],
        out_specs=[row(width), keep(w.shape), keep((1, w.shape[1]))],
        out_shape=[
            jax.ShapeDtypeStruct((total, width), F32),
            jax.ShapeDtypeStruct(w.shape, BF16),
            jax.ShapeDtypeStruct((1, w.shape[1]), F32),
        ],
        scratch_shapes=[
            pltpu.VMEM((HEADS, LANES, LANES), F32),
            pltpu.VMEM((CHUNK, w.shape[1]), BF16),
            pltpu.VMEM(w.shape, F32),
        ],
        compiler_params=pltpu.CompilerParams(
            dimension_semantics=("arbitrary", "arbitrary"), vmem_limit_bytes=VMEM_LIMIT
        ),
        name="attend_backward",
    )(x, a, k, v, e, s, sq, sk, cs, resid, w)


def block(x, ct, horizon, wqkv, bqkv, wo, vec, wu, ubias, wd):
    seqs, length, width = x.shape
    chunks = length // CHUNK
    position = jnp.arange(length, dtype=F32)
    angles = 0.5 * math.pi * position[None, :] / horizon.astype(F32)[:, None]
    cs = jnp.concatenate(
        [
            jnp.broadcast_to(jnp.cos(angles)[..., None], (seqs, length, HEAD)),
            jnp.broadcast_to(jnp.sin(angles)[..., None], (seqs, length, HEAD)),
        ],
        axis=-1,
    ).reshape(seqs * length, LANES)
    x = x.reshape(seqs * length, width)
    ct = ct.reshape(seqs * length, width)
    a, k, v, sq, sk, mixed, den, s = forward_call(x, wqkv, bqkv, cs, chunks)
    out, resid, e, go, gu, gd, gvec, gub = middle_call(x, ct, mixed, den, vec, ubias, wo, wu, wd)
    grad, gw, gb = backward_call(x, a, k, v, e, s, sq, sk, cs, resid, wqkv, chunks)
    return out, grad, gw, gb, go, gu, gd, gvec, gub


DEPTH, PLANE = 4, 4
AHEAD = 2


class Place:
    def __init__(self):
        self.dp, self.core = lax.axis_index("dp"), lax.axis_index("seq")
        self.z, self.spot = self.dp // PLANE, self.dp % PLANE
        self.other = 1 - self.core
        self.across_x = self.spot + 1 - 2 * (self.spot % 2)
        self.across_y = (self.spot + 2) % PLANE
        self.diagonal = PLANE - 1 - self.spot
        self.x_peer = (self.z * PLANE + self.across_x, self.core)
        self.y_peer = (self.z * PLANE + self.across_y, self.core)
        self.sibling = (self.dp, self.other)

    def level(self, step):
        return (self.z + step) % DEPTH

    def z_peer(self, step):
        return (self.level(step) * PLANE + self.spot, self.core)


def remote(source, target, send, recv, peer):
    copy = pltpu.make_async_remote_copy(
        src_ref=source,
        dst_ref=target,
        send_sem=send,
        recv_sem=recv,
        device_id=peer,
        device_id_type=pl.DeviceIdType.MESH,
    )
    return copy


def meet(here):
    barrier = pltpu.get_barrier_semaphore()
    peers = [here.x_peer, here.y_peer, here.sibling] + [here.z_peer(n) for n in range(1, DEPTH)]
    for peer in peers:
        pl.semaphore_signal(barrier, inc=1, device_id=peer, device_id_type=pl.DeviceIdType.MESH)
    pl.semaphore_wait(barrier, len(peers))


def gather_body(x_ref, ct_ref, q_ref, k_ref, v_ref, o_ref, u_ref, d_ref, b_ref,
                xs_ref, cts_ref, qkv_out, o_out, u_out, d_out, b_out,
                bounce, swap_sem, own_send, x_send, y_send, c_send, link_recv, core_recv):
    here = Place()
    width = q_ref.shape[1]
    outs = (b_out, qkv_out, o_out, u_out, d_out)
    heights = [out.shape[0] // (DEPTH * PLANE) for out in outs]
    count = len(outs)

    def rows(t, level, spot):
        return pl.ds(pl.multiple_of((level * PLANE + spot) * heights[t], heights[t]), heights[t])

    def piece(t, level, spot):
        half = heights[t] // 2
        start = (level * PLANE + spot) * heights[t] + here.core * half
        return outs[t].at[pl.ds(pl.multiple_of(start, half), half), :]

    shards = ((b_ref,), (q_ref, k_ref, v_ref), (o_ref,), (u_ref,), (d_ref,))
    sends = []

    def spread(t, peer, sem, arrive, whole):
        half = heights[t] // 2
        take = pl.ds(0, heights[t]) if whole else pl.ds(here.core * half, half)
        at = (here.z * PLANE + here.spot) * heights[t] + (0 if whole else here.core * half)
        place = pl.ds(pl.multiple_of(at, half), heights[t] if whole else half)
        for n, ref in enumerate(shards[t]):
            target = outs[t].at[place, n * ref.shape[1] : (n + 1) * ref.shape[1]]
            copy = remote(ref.at[take, :], target, sem.at[n], arrive, peer)
            copy.start()
            sends.append(copy)

    meet(here)
    pairs = x_ref.shape[0] // 2
    block = x_ref.shape[1]
    swaps, fetches = [], []
    for n, (source, target) in enumerate(((x_ref, xs_ref), (ct_ref, cts_ref))):
        place = pl.ds(pl.multiple_of(here.core * block, block), block)
        fetch = pltpu.make_async_copy(
            source.at[pl.ds(here.core * pairs, pairs)], bounce.at[n], swap_sem.at[n, 0]
        )
        keep = pltpu.make_async_copy(bounce.at[n], target.at[:, place, :], swap_sem.at[n, 3])
        give = remote(
            source.at[pl.ds(here.other * pairs, pairs)],
            target.at[:, place, :],
            swap_sem.at[n, 1],
            swap_sem.at[n, 2],
            here.sibling,
        )
        fetch.start()
        give.start()
        fetches.append((fetch, keep))
        swaps += [keep, give]

    def send(t, level, spot, kind):
        at = (t, level * PLANE + spot)
        ref = piece(t, level, spot)
        sem, peer, arrive = {
            "x": (x_send, here.x_peer, link_recv),
            "y": (y_send, here.y_peer, link_recv),
            "c": (c_send, here.sibling, core_recv),
        }[kind]
        copy = remote(ref, ref, sem.at[at], arrive.at[at], peer)
        copy.start()
        sends.append(copy)

    def arrived(t, level, spot, sem):
        ref = piece(t, level, spot)
        remote(ref, ref, sem.at[t, level * PLANE + spot], sem.at[t, level * PLANE + spot], here.x_peer).wait_recv()

    def begin(t):
        arrive = link_recv.at[t, here.z * PLANE + here.spot]
        spread(t, here.x_peer, own_send.at[t, 0], arrive, False)
        spread(t, here.y_peer, own_send.at[t, 1], arrive, False)
        spread(t, here.sibling, own_send.at[t, 2], core_recv.at[t, here.z * PLANE + here.spot], True)

    def rise(t):
        arrive = link_recv.at[t, here.z * PLANE + here.spot]
        for n in (1, 3, 2):
            spread(t, here.z_peer(n), own_send.at[t, 2 + n], arrive, False)

    def column(t):
        for n in (1, 3, 2):
            arrived(t, here.level(n), here.spot, link_recv)
            for kind in "xyc":
                send(t, here.level(n), here.spot, kind)

    def cross(t):
        for n in (0, 1, 3, 2):
            arrived(t, here.level(n), here.across_x, link_recv)
            if n < 2:
                send(t, here.level(n), here.across_x, "y")
            send(t, here.level(n), here.across_x, "c")
            arrived(t, here.level(n), here.across_y, link_recv)
            if n >= 2:
                send(t, here.level(n), here.across_y, "x")
            send(t, here.level(n), here.across_y, "c")

    def corner(t):
        for n in range(DEPTH):
            arrived(t, here.level(n), here.diagonal, link_recv)
            send(t, here.level(n), here.diagonal, "c")

    def finish(t):
        for n in range(DEPTH):
            for spot in (here.spot, here.across_x, here.across_y, here.diagonal):
                half = heights[t] // 2
                if n == 0 and spot is here.spot:
                    ref = outs[t].at[rows(t, here.z, here.spot), :]
                else:
                    start = (here.level(n) * PLANE + spot) * heights[t] + here.other * half
                    ref = outs[t].at[pl.ds(pl.multiple_of(start, half), half), :]
                sem = core_recv.at[t, here.level(n) * PLANE + spot]
                remote(ref, ref, sem, sem, here.sibling).wait_recv()

    for t in range(count):
        begin(t)
        if t < AHEAD:
            rise(t)
    for step in range(count + 3):
        for lag, stage in enumerate((column, cross, corner, finish)):
            if 0 <= step - lag < count:
                stage(step - lag)
            if lag == 0 and step + AHEAD < count:
                rise(step + AHEAD)
        if step == 0:
            for fetch, keep in fetches:
                fetch.wait()
                keep.start()
    for copy in swaps:
        copy.wait()
    for copy in sends:
        copy.wait_send()


def gather_call(x, ct, q, k, v, o, u, d, b):
    chips = DEPTH * PLANE
    anywhere = pl.BlockSpec(memory_space=pl.ANY)
    shape = lambda rows, cols: jax.ShapeDtypeStruct((rows, cols), BF16)
    swapped = jax.ShapeDtypeStruct((x.shape[0] // 2, x.shape[1] * 2, x.shape[2]), BF16)
    count = 5
    sem = pltpu.SemaphoreType.DMA
    return pl.pallas_call(
        gather_body,
        in_specs=[anywhere] * 9,
        out_specs=[anywhere] * 7,
        out_shape=[
            swapped,
            swapped,
            shape(q.shape[0] * chips, 3 * q.shape[1]),
            shape(o.shape[0] * chips, o.shape[1]),
            shape(u.shape[0] * chips, u.shape[1]),
            shape(d.shape[0] * chips, d.shape[1]),
            shape(b.shape[0] * chips, b.shape[1]),
        ],
        scratch_shapes=[
            pltpu.VMEM((2, x.shape[0] // 2, x.shape[1], x.shape[2]), BF16),
            sem((2, 4)),
            sem((count, 6, 3)),
            sem((count, chips)),
            sem((count, chips)),
            sem((count, chips)),
            sem((count, chips)),
            sem((count, chips)),
        ],
        compiler_params=pltpu.CompilerParams(
            collective_id=0, has_side_effects=True, vmem_limit_bytes=VMEM_LIMIT
        ),
        name="gather_weights",
    )(x, ct, q, k, v, o, u, d, b)


def scatter_body(out_ref, grad_ref, g0, g1, g2, g3, g4,
                 out4_ref, grad4_ref, r_q, r_k, r_v, r_o, r_u, r_d, r_b, *scratch):
    grads = (g0, g1, g2, g3, g4)
    count = len(grads)
    own = scratch[0:5]
    got = scratch[5:10]
    corner_x = scratch[10:15]
    corner_y = scratch[15:20]
    side_x = scratch[20:25]
    side_y = scratch[25:30]
    column = scratch[30:35]
    final = scratch[35:40]
    out_bounce, grad_bounce = scratch[40:42]
    swap_sem, load_sem, core_send, core_recv, send_sem, recv_sem, z_send, z_recv, last_sem = scratch[42:]
    here = Place()
    half = [g.shape[2] // 2 for g in grads]
    groups = (here.diagonal, here.across_x, here.across_y, here.spot)
    width = r_q.shape[1]
    loads, gives = {}, {}
    for t in range(count):
        for n, spot in enumerate(groups):
            mine = pl.ds(pl.multiple_of(here.core * half[t], half[t]), half[t])
            loads[t, n] = pltpu.make_async_copy(
                grads[t].at[:, spot, mine, :], own[t].at[n], load_sem.at[t, n]
            )
            loads[t, n].start()
    meet(here)
    for t in range(count):
        for n, spot in enumerate(groups):
            theirs = pl.ds(pl.multiple_of(here.other * half[t], half[t]), half[t])
            gives[t, n] = remote(
                grads[t].at[:, spot, theirs, :],
                got[t].at[n],
                core_send.at[t, n],
                core_recv.at[t, n],
                here.sibling,
            )
            gives[t, n].start()
    block = out4_ref.shape[1]
    pairs = out_ref.shape[0]
    swaps = []
    fetches = []
    for n, (source, target, bounce) in enumerate(
        ((out_ref, out4_ref, out_bounce), (grad_ref, grad4_ref, grad_bounce))
    ):
        place = target.at[pl.ds(here.core * pairs, pairs)]
        fetch = pltpu.make_async_copy(
            source.at[:, pl.ds(pl.multiple_of(here.core * block, block), block), :],
            bounce,
            swap_sem.at[n, 0],
        )
        keep = pltpu.make_async_copy(bounce, place, swap_sem.at[n, 3])
        give = remote(
            source.at[:, pl.ds(pl.multiple_of(here.other * block, block), block), :],
            place,
            swap_sem.at[n, 1],
            swap_sem.at[n, 2],
            here.sibling,
        )
        fetch.start()
        give.start()
        fetches.append((fetch, keep))
        swaps += [keep, give]
    sends = []

    def add(t, n, z, others):
        total = own[t][n, z].astype(F32)
        for other in others:
            total = total + other.astype(F32)
        return total

    def joined(t, n):
        loads[t, n].wait()
        gives[t, n].wait_recv()

    def push(t, slot, source, target, peer):
        copy = remote(source, target, send_sem.at[t, slot], recv_sem.at[t, slot], peer)
        copy.start()
        sends.append(copy)
        return copy

    pushed = {}

    def first(t):
        joined(t, 0)
        for z in range(DEPTH):
            own[t][0, z] = add(t, 0, z, [got[t][0, z]]).astype(own[t].dtype)
        pushed[t, 0] = push(t, 0, own[t].at[0, 0:2], corner_x[t], here.x_peer)
        pushed[t, 1] = push(t, 1, own[t].at[0, 2:4], corner_y[t], here.y_peer)

    def second(t):
        joined(t, 1)
        joined(t, 2)
        pushed[t, 0].wait_recv()
        pushed[t, 1].wait_recv()
        for z in range(DEPTH):
            extra = [corner_y[t][z - 2]] if z >= 2 else []
            own[t][1, z] = add(t, 1, z, [got[t][1, z]] + extra).astype(own[t].dtype)
            extra = [corner_x[t][z]] if z < 2 else []
            own[t][2, z] = add(t, 2, z, [got[t][2, z]] + extra).astype(own[t].dtype)
        pushed[t, 2] = push(t, 2, own[t].at[1], side_x[t], here.x_peer)
        pushed[t, 3] = push(t, 3, own[t].at[2], side_y[t], here.y_peer)

    def third(t):
        joined(t, 3)
        pushed[t, 2].wait_recv()
        pushed[t, 3].wait_recv()
        for z in range(DEPTH):
            total = add(t, 3, z, [got[t][3, z], side_x[t][z], side_y[t][z]])
            own[t][3, z] = total.astype(own[t].dtype)
        for n in range(1, DEPTH):
            copy = remote(
                own[t].at[3, here.level(n)],
                column[t].at[n],
                z_send.at[t, n],
                z_recv.at[t, n],
                here.z_peer(n),
            )
            copy.start()
            sends.append(copy)
            pushed[t, 3 + n] = copy

    def fourth(t):
        for n in range(1, DEPTH):
            pushed[t, 3 + n].wait_recv()
        total = own[t][3, here.z].astype(F32)
        for n in range(1, DEPTH):
            total = total + column[t][n].astype(F32)
        final[t][...] = total
        if t == 1:
            targets = [(final[t].at[:, n * width : (n + 1) * width], r) for n, r in enumerate((r_q, r_k, r_v))]
        else:
            targets = [(final[t], {0: r_b, 2: r_o, 3: r_u, 4: r_d}[t])]
        for m, (source, target) in enumerate(targets):
            place = target.at[pl.ds(pl.multiple_of(here.core * half[t], half[t]), half[t]), :]
            keep = pltpu.make_async_copy(source, place, last_sem.at[t, m, 0])
            give = remote(source, place, last_sem.at[t, m, 1], last_sem.at[t, m, 2], here.sibling)
            keep.start()
            give.start()
            swaps.extend((keep, give))

    order = (4, 3, 2, 1, 0)
    for step in range(count + 3):
        for lag, stage in enumerate((first, second, third, fourth)):
            if 0 <= step - lag < count:
                stage(order[step - lag])
        if step == 0:
            for fetch, keep in fetches:
                fetch.wait()
                keep.start()
    for copy in swaps:
        copy.wait()
    for copy in gives.values():
        copy.wait_send()
    for copy in sends:
        copy.wait_send()


def scatter_call(out, grad, gb, gqkv, go, gu, gd):
    chips = DEPTH * PLANE
    anywhere = pl.BlockSpec(memory_space=pl.ANY)
    grads = (gb, gqkv, go, gu, gd)
    views = [g.reshape(DEPTH, PLANE, g.shape[0] // chips, g.shape[1]) for g in grads]
    parts = [(g.shape[2] // 2, g.shape[3], g.dtype) for g in views]
    sem = pltpu.SemaphoreType.DMA
    count = len(grads)
    scratch = []
    for lead in ((4, DEPTH), (4, DEPTH), (2,), (2,), (DEPTH,), (DEPTH,), (DEPTH,)):
        scratch += [pltpu.VMEM(lead + (h, w), dtype) for h, w, dtype in parts]
    scratch += [pltpu.VMEM((h, w), F32) for h, w, _ in parts]
    scratch += [
        pltpu.VMEM((out.shape[0], out.shape[1] // 2, out.shape[2]), out.dtype),
        pltpu.VMEM((grad.shape[0], grad.shape[1] // 2, grad.shape[2]), grad.dtype),
        sem((2, 4)),
        sem((count, 4)),
        sem((count, 4)),
        sem((count, 4)),
        sem((count, 4)),
        sem((count, 4)),
        sem((count, DEPTH)),
        sem((count, DEPTH)),
        sem((count, 3, 3)),
    ]
    swapped = lambda a: jax.ShapeDtypeStruct((a.shape[0] * 2, a.shape[1] // 2, a.shape[2]), a.dtype)
    shard = lambda g, w: jax.ShapeDtypeStruct((g.shape[2], w), F32)
    width = gqkv.shape[1] // 3
    return pl.pallas_call(
        scatter_body,
        in_specs=[anywhere] * 7,
        out_specs=[anywhere] * 9,
        out_shape=[
            swapped(out),
            swapped(grad),
            shard(views[1], width),
            shard(views[1], width),
            shard(views[1], width),
            shard(views[2], views[2].shape[3]),
            shard(views[3], views[3].shape[3]),
            shard(views[4], views[4].shape[3]),
            shard(views[0], views[0].shape[3]),
        ],
        scratch_shapes=scratch,
        compiler_params=pltpu.CompilerParams(
            collective_id=1, has_side_effects=True, vmem_limit_bytes=VMEM_LIMIT
        ),
        name="scatter_gradients",
    )(out, grad, *views)


def pack_vectors(vectors, up_bias):
    part = vectors[0].shape[0]
    stacked = jnp.concatenate([jnp.stack(vectors), up_bias.reshape(-1, part)])
    return jnp.pad(stacked, ((0, 16 - stacked.shape[0]), (0, LANES - part)))


def unpack_vectors(gathered, part):
    chips = gathered.shape[0] // 16
    grid = gathered.reshape(chips, 16, LANES)[:, :13, :part].astype(F32)
    rows = jnp.transpose(grid[:, :9], (1, 0, 2)).reshape(9, chips * part)
    up_bias = grid[:, 9:].reshape(1, chips * 4 * part)
    return rows[0:3].reshape(1, -1), jnp.pad(rows[3:9], ((0, 2), (0, 0))), up_bias


def pack_vector_grads(gb, gvec, gub, chips):
    width = gvec.shape[1]
    part = width // chips
    rows = jnp.concatenate([gb.reshape(3, width), gvec[0:6]]).reshape(9, chips, part)
    rows = jnp.transpose(rows, (1, 0, 2))
    grid = jnp.concatenate([rows, gub.reshape(chips, 4, part)], axis=1)
    grid = jnp.pad(grid, ((0, 0), (0, 3), (0, LANES - part)))
    return grid.reshape(chips * 16, LANES)


def local(
    inputs,
    horizon,
    query_weight,
    query_bias,
    key_weight,
    key_bias,
    value_weight,
    value_bias,
    out_weight,
    out_bias,
    first_gain,
    first_shift,
    up_weight,
    up_bias,
    down_weight,
    down_bias,
    second_gain,
    second_shift,
    cotangent,
):
    chips = lax.axis_size("dp")
    core = lax.axis_index("seq")
    part = query_bias.shape[0]
    seqs = inputs.shape[0] // 2
    direct = chips == DEPTH * PLANE
    vectors = pack_vectors(
        (
            query_bias,
            key_bias,
            value_bias,
            out_bias,
            first_gain,
            first_shift,
            down_bias,
            second_gain,
            second_shift,
        ),
        up_bias,
    )
    weights = (query_weight, key_weight, value_weight, out_weight, up_weight, down_weight)
    if direct:
        x, ct, wqkv, wo, wu, wd, gathered = gather_call(inputs, cotangent, *weights, vectors)
    else:
        gather = lambda a: lax.all_gather(a, "dp", axis=0, tiled=True)
        x, ct = (lax.all_to_all(a, "seq", 0, 1, tiled=True) for a in (inputs, cotangent))
        wqkv = gather(jnp.concatenate(weights[:3], axis=1))
        wo, wu, wd, gathered = (gather(a) for a in (*weights[3:], vectors))
    bqkv, vec, ubias = unpack_vectors(gathered, part)
    spans = lax.dynamic_slice_in_dim(horizon, core * seqs, seqs)
    out, grad, gw, gb, go, gu, gd, gvec, gub = block(
        x, ct, spans, wqkv, bqkv, wo, vec, wu, ubias, wd
    )
    out, grad = out.reshape(x.shape), grad.reshape(x.shape)
    gvectors = pack_vector_grads(gb, gvec, gub, chips)
    if direct:
        out, grad, gq, gk, gv, go, gu, gd, gvectors = scatter_call(
            out, grad, gvectors, gw, go, gu, gd
        )
    else:
        out, grad = (lax.all_to_all(a, "seq", 1, 0, tiled=True) for a in (out, grad))
        total = lambda g: lax.psum(
            lax.psum_scatter(g, "dp", scatter_dimension=0, tiled=True), "seq"
        )
        gw, go, gu, gd, gvectors = (total(g.astype(F32)) for g in (gw, go, gu, gd, gvectors))
        gq, gk, gv = jnp.split(gw, 3, axis=1)
    rows = gvectors[:, :part]
    return (
        out,
        grad,
        gq,
        rows[0],
        gk,
        rows[1],
        gv,
        rows[2],
        go,
        rows[3],
        rows[4],
        rows[5],
        gu,
        rows[9:13].reshape(-1),
        gd,
        rows[6],
        rows[7],
        rows[8],
    )


def solution(mesh):
    long, wide, thin = P("dp", "seq", None), P("dp", None), P("dp")
    shards = (wide, thin, wide, thin, wide, thin, wide, thin, thin, thin, wide, thin, wide, thin, thin, thin)
    return jax.shard_map(
        local,
        mesh=mesh,
        in_specs=(long, thin, *shards, long),
        out_specs=(long, long, *shards),
        check_vma=False,
    )
```

```python
import functools
import math

import jax
import jax.numpy as jnp
from jax import lax
from jax.experimental import pallas as pl
from jax.experimental.pallas import tpu as pltpu
from jax.sharding import PartitionSpec as P

HEADS = 12
HEAD = 64
PAIRS = HEADS // 2
LANES = 128
CHUNK = 256
ROWS = 256
NORM_EPS = 1e-05
GELU_A = 0.7978845608
GELU_B = 0.044715
VMEM_LIMIT = 60 * 1024 * 1024
F32, BF16 = jnp.float32, jnp.bfloat16


def dot_nn(a, b):
    return lax.dot_general(a, b, (((1,), (0,)), ((), ())), preferred_element_type=F32)


def dot_nt(a, b):
    return lax.dot_general(a, b, (((1,), (1,)), ((), ())), preferred_element_type=F32)


def dot_tn(a, b):
    return lax.dot_general(a, b, (((0,), (0,)), ((), ())), preferred_element_type=F32)


def low_lanes(rows):
    return lax.broadcasted_iota(jnp.int32, (rows, LANES), 1) < HEAD


def swap(values):
    return pltpu.roll(values, HEAD, 1)


def softplus_and_slope(values):
    e = jnp.exp(-jnp.abs(values))
    plus = jnp.maximum(values, 0.0) + jnp.log1p(e)
    slope = jnp.where(values >= 0.0, 1.0, e) / (1.0 + e)
    return plus, slope


def attend_forward(
    x_ref, w_ref, b_ref, cs_ref, a_ref, k_ref, v_ref, sq_ref, sk_ref, mixed_ref, den_ref, s_ref, state
):
    @pl.when(pl.program_id(1) == 0)
    def _():
        state[...] = jnp.zeros_like(state)

    attend(
        x_ref[...],
        w_ref,
        b_ref,
        cs_ref,
        a_ref,
        k_ref,
        v_ref,
        sq_ref,
        sk_ref,
        mixed_ref,
        den_ref,
        s_ref,
        state,
    )


def attend(
    x, w_ref, b_ref, cs_ref, a_ref, k_ref, v_ref, sq_ref, sk_ref, mixed_ref, den_ref, s_ref, state
):
    rows, width = x.shape
    cs = cs_ref[...]
    low = low_lanes(rows)
    causal = lax.broadcasted_iota(jnp.int32, (rows, rows), 0) >= lax.broadcasted_iota(
        jnp.int32, (rows, rows), 1
    )

    for half in range(2):
        slope_ref = (sq_ref, sk_ref)[half]
        feature_ref = (a_ref, k_ref)[half]
        pre = dot_nn(x, w_ref[:, half * width : (half + 1) * width])
        pre = pre + b_ref[half : half + 1, :]
        plus, slope = softplus_and_slope(pre)
        slope_ref[...] = slope.astype(BF16)
        for pair in range(PAIRS):
            both = plus[:, pair * LANES : (pair + 1) * LANES]
            other = swap(both)
            even = jnp.where(low, both, other) * cs
            odd = jnp.where(low, other, both) * cs
            feature_ref[:, (2 * pair) * LANES : (2 * pair + 1) * LANES] = even.astype(BF16)
            feature_ref[:, (2 * pair + 1) * LANES : (2 * pair + 2) * LANES] = odd.astype(BF16)
    values = dot_nn(x, w_ref[:, 2 * width :]) + b_ref[2:3, :]
    v_ref[...] = values.astype(BF16)
    for pair in range(PAIRS):
        both = values[:, pair * LANES : (pair + 1) * LANES]
        results = []
        for odd in range(2):
            head = 2 * pair + odd
            query = a_ref[:, head * LANES : (head + 1) * LANES]
            key = k_ref[:, head * LANES : (head + 1) * LANES]
            wide = (jnp.where(low, 1.0, both) if odd else jnp.where(low, both, 1.0)).astype(BF16)
            scores = jnp.where(causal, dot_nt(query, key), 0.0).astype(BF16)
            before = state[head]
            before_low = before.astype(BF16)
            s_ref[head] = before_low
            results.append(dot_nn(scores, wide) + dot_nn(query, before_low))
            state[head] = before + dot_tn(key, wide)
        numer = jnp.where(low, results[0], results[1])
        denom = swap(jnp.where(low, results[1], results[0]))
        mixed_ref[:, pair * LANES : (pair + 1) * LANES] = (numer / denom).astype(BF16)
        den_ref[:, pair * LANES : (pair + 1) * LANES] = denom


def forward_call(x, w, b, cs, chunks):
    total, width = x.shape
    seqs = total // (chunks * CHUNK)
    row = lambda n: pl.BlockSpec((CHUNK, n), lambda s, c: (s * chunks + c, 0))
    once = lambda shape: pl.BlockSpec(
        shape, lambda s, c: (0,) * len(shape), pipeline_mode=pl.Buffered(1)
    )
    wide = HEADS * LANES
    return pl.pallas_call(
        attend_forward,
        grid=(seqs, chunks),
        in_specs=[row(width), once(w.shape), once(b.shape), row(LANES)],
        out_specs=[
            row(wide),
            row(wide),
            row(width),
            row(width),
            row(width),
            row(width),
            row(width),
            pl.BlockSpec((None, HEADS, LANES, LANES), lambda s, c: (s * chunks + c, 0, 0, 0)),
        ],
        out_shape=[
            jax.ShapeDtypeStruct((total, wide), BF16),
            jax.ShapeDtypeStruct((total, wide), BF16),
            jax.ShapeDtypeStruct((total, width), BF16),
            jax.ShapeDtypeStruct((total, width), BF16),
            jax.ShapeDtypeStruct((total, width), BF16),
            jax.ShapeDtypeStruct((total, width), BF16),
            jax.ShapeDtypeStruct((total, width), F32),
            jax.ShapeDtypeStruct((seqs * chunks, HEADS, LANES, LANES), BF16),
        ],
        scratch_shapes=[pltpu.VMEM((HEADS, LANES, LANES), F32)],
        compiler_params=pltpu.CompilerParams(
            dimension_semantics=("arbitrary", "arbitrary"), vmem_limit_bytes=VMEM_LIMIT
        ),
        name="attend_forward",
    )(x, w, b, cs)


def row_mean(values):
    return jnp.mean(values, axis=-1, keepdims=True)


def norm_parts(values):
    center = values - row_mean(values)
    scale = lax.rsqrt(row_mean(center * center) + NORM_EPS)
    return center * scale, scale


def norm_back(grad, gain, unit, scale):
    scaled = grad * gain
    return (scaled - row_mean(scaled) - unit * row_mean(scaled * unit)) * scale


def add_rows(values):
    return jnp.sum(values, axis=0, keepdims=True)


def middle(
    tiles,
    x_ref,
    ct_ref,
    mixed_ref,
    den_ref,
    vec_ref,
    ubias_ref,
    wo_ref,
    wu_ref,
    wd_ref,
    out_ref,
    resid_ref,
    e_ref,
    go_hbm,
    gu_hbm,
    gd_hbm,
    gvec_ref,
    gub_ref,
    act,
    slope,
    go,
    gu,
    gd,
    stage,
    sems,
):
    step = pl.program_id(0)
    rows, width = x_ref.shape
    hidden_width = wu_ref.shape[1]
    tile = hidden_width // tiles
    low = low_lanes(rows)

    @pl.when(step == 0)
    def _():
        go[...] = jnp.zeros_like(go)
        gu[...] = jnp.zeros_like(gu)
        gd[...] = jnp.zeros_like(gd)
        gvec_ref[...] = jnp.zeros_like(gvec_ref)
        gub_ref[...] = jnp.zeros_like(gub_ref)

    out_bias, gain1, shift1 = vec_ref[0:1], vec_ref[1:2], vec_ref[2:3]
    down_bias, gain2, shift2 = vec_ref[3:4], vec_ref[4:5], vec_ref[5:6]
    mixed = mixed_ref[...]
    resid = x_ref[...].astype(F32) + (dot_nn(mixed, wo_ref[...]) + out_bias)
    unit1, scale1 = norm_parts(resid)
    normed = unit1 * gain1 + shift1
    normed_low = normed.astype(BF16)
    ffn = jnp.zeros((rows, width), F32)
    for t in range(tiles):
        cols = slice(t * tile, (t + 1) * tile)
        hidden = dot_nn(normed_low, wu_ref[:, cols]) + ubias_ref[:, cols]
        square = hidden * hidden
        inner = hidden * (GELU_A + (GELU_A * GELU_B) * square)
        tanh = jnp.tanh(inner)
        half = 0.5 + 0.5 * tanh
        active = (hidden * half).astype(BF16)
        curve = half + (0.5 * hidden) * (1.0 - tanh * tanh) * (
            GELU_A + (3.0 * GELU_A * GELU_B) * square
        )
        act[:, cols] = active
        slope[:, cols] = curve.astype(BF16)
        ffn = ffn + dot_nn(active, wd_ref[cols, :])
    unit2, scale2 = norm_parts(normed + (ffn + down_bias))
    out_ref[...] = (unit2 * gain2 + shift2).astype(BF16)
    grad = ct_ref[...].astype(F32)
    back_final = norm_back(grad, gain2, unit2, scale2)
    back_ffn = back_final.astype(BF16)
    gvec_ref[4:5] += add_rows(grad * unit2)
    gvec_ref[5:6] += add_rows(grad)
    gvec_ref[3:4] += add_rows(back_ffn.astype(F32))
    back_normed = back_final
    for t in range(tiles):
        cols = slice(t * tile, (t + 1) * tile)
        gd[cols, :] += dot_tn(act[:, cols], back_ffn)
        back_active = dot_nt(back_ffn, wd_ref[cols, :])
        back_hidden = (back_active * slope[:, cols].astype(F32)).astype(BF16)
        gub_ref[:, cols] += add_rows(back_hidden.astype(F32))
        gu[:, cols] += dot_tn(normed_low, back_hidden)
        back_normed = back_normed + dot_nt(back_hidden, wu_ref[:, cols])
    gvec_ref[1:2] += add_rows(back_normed * unit1)
    gvec_ref[2:3] += add_rows(back_normed)
    back_resid = norm_back(back_normed, gain1, unit1, scale1)
    resid_ref[...] = back_resid
    back_branch = back_resid.astype(BF16)
    gvec_ref[0:1] += add_rows(back_branch.astype(F32))
    go[...] += dot_tn(mixed, back_branch)
    back_mixed = dot_nt(back_branch, wo_ref[...])
    inverse = 1.0 / den_ref[...]
    back_numer = back_mixed * inverse
    product = back_numer * mixed.astype(F32)
    high = product.astype(BF16)
    rest = (product - high.astype(F32)).astype(BF16)
    same_head = (
        lax.broadcasted_iota(jnp.int32, (2 * LANES, 2 * LANES), 0) // HEAD
        == lax.broadcasted_iota(jnp.int32, (2 * LANES, 2 * LANES), 1) // HEAD
    ).astype(F32).astype(BF16)
    even_lane = lax.broadcasted_iota(jnp.int32, (rows, LANES), 1) % 2 == 0
    for block in range(width // (2 * LANES)):
        cols = slice(block * 2 * LANES, (block + 1) * 2 * LANES)
        sums = dot_nn(high[:, cols], same_head) + dot_nn(rest[:, cols], same_head)
        for inside in range(2):
            pair = 2 * block + inside
            back = -sums[:, inside * LANES : (inside + 1) * LANES]
            back_high = back.astype(BF16).astype(F32)
            spread = swap(jnp.where(even_lane, back_high, back - back_high) * (2.0 / HEAD))
            numer = back_numer[:, pair * LANES : (pair + 1) * LANES]
            e_ref[:, (2 * pair) * LANES : (2 * pair + 1) * LANES] = jnp.where(
                low, numer, spread
            ).astype(BF16)
            e_ref[:, (2 * pair + 1) * LANES : (2 * pair + 2) * LANES] = jnp.where(
                low, spread, numer
            ).astype(BF16)

    @pl.when(step == pl.num_programs(0) - 1)
    def _():
        blocks = [(go, go_hbm, 0, 0)]
        for t in range(hidden_width // width):
            blocks.append((gu, gu_hbm, 0, t * width))
            blocks.append((gd, gd_hbm, t * width, 0))
        copies = []
        for n, (source, target, top, left) in enumerate(blocks):
            if n >= 2:
                copies[n - 2].wait()
            place = (slice(top, top + width), slice(left, left + width))
            stage[n % 2] = source[place].astype(BF16)
            copies.append(pltpu.make_async_copy(stage.at[n % 2], target.at[place], sems.at[n % 2]))
            copies[n].start()
        for copy in copies[-2:]:
            copy.wait()


def middle_call(x, ct, mixed, den, vec, ubias, wo, wu, wd, tiles=4):
    total, width = x.shape
    hidden_width = wu.shape[1]
    row = lambda n: pl.BlockSpec((ROWS, n), lambda i: (i, 0))
    once = lambda shape: pl.BlockSpec(
        shape, lambda i: (0,) * len(shape), pipeline_mode=pl.Buffered(1)
    )
    keep = lambda shape: pl.BlockSpec(shape, lambda i: (0,) * len(shape))
    anywhere = pl.BlockSpec(memory_space=pl.ANY)
    wide = HEADS * LANES
    return pl.pallas_call(
        functools.partial(middle, tiles),
        grid=(total // ROWS,),
        in_specs=[
            row(width),
            row(width),
            row(width),
            row(width),
            once(vec.shape),
            once(ubias.shape),
            once(wo.shape),
            once(wu.shape),
            once(wd.shape),
        ],
        out_specs=[
            row(width),
            row(width),
            row(wide),
            anywhere,
            anywhere,
            anywhere,
            keep((8, width)),
            keep((1, hidden_width)),
        ],
        out_shape=[
            jax.ShapeDtypeStruct((total, width), BF16),
            jax.ShapeDtypeStruct((total, width), F32),
            jax.ShapeDtypeStruct((total, wide), BF16),
            jax.ShapeDtypeStruct(wo.shape, BF16),
            jax.ShapeDtypeStruct(wu.shape, BF16),
            jax.ShapeDtypeStruct(wd.shape, BF16),
            jax.ShapeDtypeStruct((8, width), F32),
            jax.ShapeDtypeStruct((1, hidden_width), F32),
        ],
        scratch_shapes=[
            pltpu.VMEM((ROWS, hidden_width), BF16),
            pltpu.VMEM((ROWS, hidden_width), BF16),
            pltpu.VMEM(wo.shape, F32),
            pltpu.VMEM(wu.shape, F32),
            pltpu.VMEM(wd.shape, F32),
            pltpu.VMEM((2, width, width), BF16),
            pltpu.SemaphoreType.DMA((2,)),
        ],
        compiler_params=pltpu.CompilerParams(
            dimension_semantics=("arbitrary",), vmem_limit_bytes=VMEM_LIMIT
        ),
        name="middle",
    )(x, ct, mixed, den, vec, ubias, wo, wu, wd)


def attend_back(a_ref, k_ref, v_ref, e_ref, s_ref, sq_ref, sk_ref, cs_ref, after, back, gb_ref):
    rows, width = v_ref.shape
    cs = cs_ref[...]
    low = low_lanes(rows)
    i = lax.broadcasted_iota(jnp.int32, (rows, rows), 0)
    j = lax.broadcasted_iota(jnp.int32, (rows, rows), 1)
    causal, anti = i >= j, i <= j
    for pair in range(PAIRS):
        both = v_ref[:, pair * LANES : (pair + 1) * LANES].astype(F32)
        back_q, back_k, back_v = [], [], []
        for odd in range(2):
            head = 2 * pair + odd
            cols = slice(head * LANES, (head + 1) * LANES)
            query, key, e = a_ref[:, cols], k_ref[:, cols], e_ref[:, cols]
            wide = (jnp.where(low, 1.0, both) if odd else jnp.where(low, both, 1.0)).astype(BF16)
            state = s_ref[head]
            later = after[head]
            later_low = later.astype(BF16)
            scores_t = jnp.where(anti, dot_nt(key, query), 0.0).astype(BF16)
            back_s = jnp.where(causal, dot_nt(e, wide), 0.0).astype(BF16)
            back_st = jnp.where(anti, dot_nt(wide, e), 0.0).astype(BF16)
            y = (dot_nn(back_s, key) + dot_nt(e, state)) * cs
            back_q.append(y + swap(y))
            y = (dot_nn(back_st, query) + dot_nt(wide, later_low)) * cs
            back_k.append(y + swap(y))
            back_v.append(dot_nn(scores_t, e) + dot_nn(key, later_low))
            after[head] = later + dot_tn(query, e)
        cols = slice(pair * LANES, (pair + 1) * LANES)
        dq = jnp.where(low, back_q[0], back_q[1]) * sq_ref[:, cols].astype(F32)
        dk = jnp.where(low, back_k[0], back_k[1]) * sk_ref[:, cols].astype(F32)
        dv = jnp.where(low, back_v[0], back_v[1])
        for n, piece in enumerate((dq, dk, dv)):
            piece = piece.astype(BF16)
            cols = slice(n * width + pair * LANES, n * width + (pair + 1) * LANES)
            back[:, cols] = piece
            gb_ref[:, cols] += add_rows(piece.astype(F32))


def attend_backward(
    x_ref,
    a_ref,
    k_ref,
    v_ref,
    e_ref,
    s_ref,
    sq_ref,
    sk_ref,
    cs_ref,
    resid_ref,
    w_ref,
    grad_ref,
    gw_ref,
    gb_ref,
    after,
    back,
    gw,
):
    rows, width = x_ref.shape

    @pl.when((pl.program_id(0) == 0) & (pl.program_id(1) == 0))
    def _():
        gw[...] = jnp.zeros_like(gw)
        gb_ref[...] = jnp.zeros_like(gb_ref)

    @pl.when(pl.program_id(1) == 0)
    def _():
        after[...] = jnp.zeros_like(after)

    attend_back(a_ref, k_ref, v_ref, e_ref, s_ref, sq_ref, sk_ref, cs_ref, after, back, gb_ref)
    x = x_ref[...]
    total = resid_ref[...]
    for n in range(3):
        cols = slice(n * width, (n + 1) * width)
        piece = back[:, cols]
        gw[:, cols] += dot_tn(x, piece)
        total = total + dot_nt(piece, w_ref[:, cols])
    grad_ref[...] = total

    @pl.when((pl.program_id(0) == pl.num_programs(0) - 1) & (pl.program_id(1) == pl.num_programs(1) - 1))
    def _():
        gw_ref[...] = gw[...].astype(BF16)


def backward_call(x, a, k, v, e, s, sq, sk, cs, resid, w, chunks):
    total, width = x.shape
    seqs = total // (chunks * CHUNK)
    place = lambda s, c: s * chunks + chunks - 1 - c
    row = lambda n: pl.BlockSpec((CHUNK, n), lambda s, c: (place(s, c), 0))
    once = lambda shape: pl.BlockSpec(
        shape, lambda s, c: (0,) * len(shape), pipeline_mode=pl.Buffered(1)
    )
    keep = lambda shape: pl.BlockSpec(shape, lambda s, c: (0,) * len(shape))
    wide = HEADS * LANES
    return pl.pallas_call(
        attend_backward,
        grid=(seqs, chunks),
        in_specs=[
            row(width),
            row(wide),
            row(wide),
            row(width),
            row(wide),
            pl.BlockSpec((None, HEADS, LANES, LANES), lambda s, c: (place(s, c), 0, 0, 0)),
            row(width),
            row(width),
            row(LANES),
            row(width),
            once(w.shape),
        ],
        out_specs=[row(width), keep(w.shape), keep((1, w.shape[1]))],
        out_shape=[
            jax.ShapeDtypeStruct((total, width), F32),
            jax.ShapeDtypeStruct(w.shape, BF16),
            jax.ShapeDtypeStruct((1, w.shape[1]), F32),
        ],
        scratch_shapes=[
            pltpu.VMEM((HEADS, LANES, LANES), F32),
            pltpu.VMEM((CHUNK, w.shape[1]), BF16),
            pltpu.VMEM(w.shape, F32),
        ],
        compiler_params=pltpu.CompilerParams(
            dimension_semantics=("arbitrary", "arbitrary"), vmem_limit_bytes=VMEM_LIMIT
        ),
        name="attend_backward",
    )(x, a, k, v, e, s, sq, sk, cs, resid, w)


def rotation(horizon, length):
    seqs = horizon.shape[0]
    position = jnp.arange(length, dtype=F32)
    angles = 0.5 * math.pi * position[None, :] / horizon.astype(F32)[:, None]
    return jnp.concatenate(
        [
            jnp.broadcast_to(jnp.cos(angles)[..., None], (seqs, length, HEAD)),
            jnp.broadcast_to(jnp.sin(angles)[..., None], (seqs, length, HEAD)),
        ],
        axis=-1,
    ).reshape(seqs * length, LANES)


DEPTH, PLANE = 4, 4


class Place:
    def __init__(self):
        self.dp, self.core = lax.axis_index("dp"), lax.axis_index("seq")
        self.z, self.spot = self.dp // PLANE, self.dp % PLANE
        self.other = 1 - self.core
        self.levels = [(self.z + step) % DEPTH for step in range(DEPTH)]
        self.across_x = self.spot + 1 - 2 * (self.spot % 2)
        self.across_y = (self.spot + 2) % PLANE
        self.diagonal = PLANE - 1 - self.spot
        self.x_peer = (self.z * PLANE + self.across_x, self.core)
        self.y_peer = (self.z * PLANE + self.across_y, self.core)
        self.sibling = (self.dp, self.other)

    def level(self, step):
        return self.levels[step]

    def z_peer(self, step):
        return (self.level(step) * PLANE + self.spot, self.core)


def remote(source, target, send, recv, peer):
    copy = pltpu.make_async_remote_copy(
        src_ref=source,
        dst_ref=target,
        send_sem=send,
        recv_sem=recv,
        device_id=peer,
        device_id_type=pl.DeviceIdType.MESH,
    )
    return copy


def meet(here):
    barrier = pltpu.get_barrier_semaphore()
    peers = [here.x_peer, here.y_peer, here.sibling] + [here.z_peer(n) for n in range(1, DEPTH)]
    for peer in peers:
        pl.semaphore_signal(barrier, inc=1, device_id=peer, device_id_type=pl.DeviceIdType.MESH)
    pl.semaphore_wait(barrier, len(peers))


class Gather:
    def __init__(self, here, shards, outs, own_send, x_send, y_send, c_send, link_recv, core_recv):
        self.here, self.shards, self.outs = here, shards, outs
        self.own_send, self.link_recv, self.core_recv = own_send, link_recv, core_recv
        self.sems = {"x": x_send, "y": y_send, "c": c_send}
        self.heights = [out.shape[0] // (DEPTH * PLANE) for out in outs]
        self.started = []

    def index(self, level, spot):
        return level * PLANE + spot

    def rows(self, t, level, spot):
        height = self.heights[t]
        return pl.ds(pl.multiple_of(self.index(level, spot) * height, height), height)

    def piece(self, t, level, spot, core):
        half = self.heights[t] // 2
        start = self.index(level, spot) * self.heights[t] + core * half
        return self.outs[t].at[pl.ds(pl.multiple_of(start, half), half), :]

    def passing(self, t, level, spot, kind):
        here, at = self.here, self.index(level, spot)
        peer = {"x": here.x_peer, "y": here.y_peer, "c": here.sibling}[kind]
        arrive = self.core_recv if kind == "c" else self.link_recv
        ref = self.piece(t, level, spot, here.core)
        return [remote(ref, ref, self.sems[kind].at[t, at], arrive.at[t, at], peer)]

    def spreading(self, t, slot):
        here, height = self.here, self.heights[t]
        whole = slot == 2
        peer = (here.x_peer, here.y_peer, here.sibling)[slot] if slot < 3 else here.z_peer(slot - 2)
        mine = self.index(here.z, here.spot)
        arrive = (self.core_recv if whole else self.link_recv).at[t, mine]
        half = height // 2
        if whole:
            take, place = pl.ds(0, height), self.rows(t, here.z, here.spot)
        else:
            take = pl.ds(pl.multiple_of(here.core * half, half), half)
            place = pl.ds(pl.multiple_of(mine * height + here.core * half, half), half)
        copies = []
        for n, ref in enumerate(self.shards[t]):
            target = self.outs[t].at[place, n * ref.shape[1] : (n + 1) * ref.shape[1]]
            copies.append(
                remote(ref.at[take, :], target, self.own_send.at[t, slot, n], arrive, peer)
            )
        return copies

    def start(self, make, *args):
        for copy in make(*args):
            copy.start()
        self.started.append((make, args))

    def drain(self):
        for make, args in self.started:
            for copy in make(*args):
                copy.wait_send()

    def arrived(self, t, level, spot):
        ref = self.piece(t, level, spot, self.here.core)
        sem = self.link_recv.at[t, self.index(level, spot)]
        remote(ref, ref, sem, sem, self.here.x_peer).wait_recv()

    def begin(self, t):
        for slot in range(3):
            self.start(self.spreading, t, slot)

    def rise(self, t):
        for n in (1, 3, 2):
            self.start(self.spreading, t, 2 + n)

    def column(self, t):
        here = self.here
        for n in (1, 3, 2):
            self.arrived(t, here.level(n), here.spot)
            for kind in "xyc":
                self.start(self.passing, t, here.level(n), here.spot, kind)

    def cross(self, t):
        here = self.here
        for n in (0, 1, 3, 2):
            for spot, kind in ((here.across_x, "y"), (here.across_y, "x")):
                self.arrived(t, here.level(n), spot)
                if (n < 2) == (kind == "y"):
                    self.start(self.passing, t, here.level(n), spot, kind)
                self.start(self.passing, t, here.level(n), spot, "c")

    def corner(self, t):
        here = self.here
        for n in range(DEPTH):
            self.arrived(t, here.level(n), here.diagonal)
            self.start(self.passing, t, here.level(n), here.diagonal, "c")

    def finish(self, t):
        here = self.here
        for n in range(DEPTH):
            for spot in (here.spot, here.across_x, here.across_y, here.diagonal):
                if n == 0 and spot is here.spot:
                    ref = self.outs[t].at[self.rows(t, here.z, here.spot), :]
                else:
                    ref = self.piece(t, here.level(n), spot, here.other)
                sem = self.core_recv.at[t, self.index(here.level(n), spot)]
                remote(ref, ref, sem, sem, here.sibling).wait_recv()


def place_vectors(gathered, vec_ref, ub_ref, rows_out):
    chips = DEPTH * PLANE
    part = vec_ref.shape[1] // chips
    lane = lax.broadcasted_iota(jnp.int32, (16, LANES), 1)
    blocks = [gathered[c * 16 : (c + 1) * 16, :].astype(F32) for c in range(chips)]
    blocks = [jnp.where(lane < part, block, 0.0) for block in blocks]

    def spots(position):
        return position // LANES, position % LANES

    rows = [jnp.zeros((16, LANES), F32) for _ in range(vec_ref.shape[1] // LANES)]
    for c in range(chips):
        group, shift = spots(c * part)
        turned = pltpu.roll(blocks[c], shift, 1) if shift else blocks[c]
        if shift + part > LANES:
            rows[group] = rows[group] + jnp.where(lane >= shift, turned, 0.0)
            rows[group + 1] = rows[group + 1] + jnp.where(lane < shift, turned, 0.0)
        else:
            rows[group] = rows[group] + turned
    for group, row in enumerate(rows):
        cols = slice(group * LANES, (group + 1) * LANES)
        rows_out[:, cols] = row
        vec_ref[0:6, cols] = row[3:9]
    vec_ref[6:8, :] = jnp.zeros((2, vec_ref.shape[1]), F32)
    wide = [jnp.zeros((16, LANES), F32) for _ in range(ub_ref.shape[1] // LANES)]
    for c in range(chips):
        for r in range(4):
            group, shift = spots((4 * c + r) * part)
            row = jnp.broadcast_to(blocks[c][9 + r : 10 + r], (16, LANES))
            turned = pltpu.roll(row, shift, 1) if shift else row
            if shift + part > LANES:
                wide[group] = wide[group] + jnp.where(lane >= shift, turned, 0.0)
                wide[group + 1] = wide[group + 1] + jnp.where(lane < shift, turned, 0.0)
            else:
                wide[group] = wide[group] + turned
    for group, row in enumerate(wide):
        ub_ref[:, group * LANES : (group + 1) * LANES] = row[0:1]


BETWEEN = {
    1: (("cross", 2), ("column", 3)),
    2: (("corner", 2), ("column", 4)),
    3: (("cross", 3),),
    4: (("finish", 2), ("corner", 3)),
    5: (("cross", 4),),
    6: (("finish", 3),),
}


def gather_attend(
    x_ref, ct_ref, q_ref, k_ref, v_ref, o_ref, u_ref, d_ref, b_ref, cs_ref,
    xs_out, cts_out, qkv_out, o_out, u_out, d_out, b_out,
    a_ref, key_ref, val_ref, sq_ref, sk_ref, mixed_ref, den_ref, s_ref, vec_ref, ub_ref,
    state, xs, bounce, weights, vectors, rows,
    swap_sem, load_sem, own_send, x_send, y_send, c_send, link_recv, core_recv,
):
    here = Place()
    seq, chunk, chunks = pl.program_id(0), pl.program_id(1), pl.num_programs(1)
    step = seq * chunks + chunk
    last = pl.num_programs(0) * chunks - 1
    shards = ((b_ref,), (q_ref, k_ref, v_ref), (o_ref,), (u_ref,), (d_ref,))
    outs = (b_out, qkv_out, o_out, u_out, d_out)
    gather = Gather(
        here, shards, outs, own_send, x_send, y_send, c_send, link_recv, core_recv
    )
    pairs, block = x_ref.shape[0] // 2, x_ref.shape[1]

    def swapping():
        place = pl.ds(pl.multiple_of(here.core * block, block), block)
        mine, theirs = pl.ds(here.core * pairs, pairs), pl.ds(here.other * pairs, pairs)
        keep_x = pltpu.make_async_copy(x_ref.at[mine], xs.at[:, place, :], swap_sem.at[0])
        give_x = remote(
            x_ref.at[theirs], xs.at[:, place, :], swap_sem.at[1], swap_sem.at[2], here.sibling
        )
        fetch = pltpu.make_async_copy(ct_ref.at[mine], bounce, swap_sem.at[3])
        keep_ct = pltpu.make_async_copy(bounce, cts_out.at[:, place, :], swap_sem.at[4])
        give_ct = remote(
            ct_ref.at[theirs], cts_out.at[:, place, :], swap_sem.at[5], swap_sem.at[6], here.sibling
        )
        store = pltpu.make_async_copy(xs, xs_out, swap_sem.at[7])
        return keep_x, give_x, fetch, keep_ct, give_ct, store

    @pl.when(step == 0)
    def _():
        keep_x, give_x, fetch, keep_ct, give_ct, store = swapping()
        keep_x.start()
        fetch.start()
        meet(here)
        for t in range(2):
            gather.begin(t)
            gather.rise(t)
        give_x.start()
        give_ct.start()
        for t in range(2, 5):
            gather.begin(t)
        gather.rise(2)
        gather.column(0)
        gather.column(1)
        gather.rise(3)
        fetch.wait()
        keep_ct.start()
        gather.cross(0)
        gather.cross(1)
        gather.column(2)
        gather.rise(4)
        gather.corner(0)
        gather.corner(1)
        gather.finish(0)
        small = pltpu.make_async_copy(b_out, vectors, load_sem.at[0])
        small.start()
        keep_x.wait()
        give_x.wait()
        store.start()
        gather.finish(1)
        large = pltpu.make_async_copy(qkv_out, weights, load_sem.at[1])
        large.start()
        small.wait()
        place_vectors(vectors[...], vec_ref, ub_ref, rows)
        large.wait()

    for n, stages in BETWEEN.items():

        @pl.when(step == n)
        def _(stages=stages):
            for stage, t in stages:
                getattr(gather, stage)(t)

    @pl.when(chunk == 0)
    def _():
        state[...] = jnp.zeros_like(state)

    x = xs[seq, pl.ds(pl.multiple_of(chunk * CHUNK, CHUNK), CHUNK), :]
    attend(x, weights, rows, cs_ref, a_ref, key_ref, val_ref, sq_ref, sk_ref, mixed_ref, den_ref, s_ref, state)

    @pl.when(step == last)
    def _():
        gather.corner(4)
        gather.finish(4)
        _, _, _, keep_ct, give_ct, store = swapping()
        store.wait()
        keep_ct.wait()
        give_ct.wait()
        gather.drain()


def gather_attend_call(x, ct, q, k, v, o, u, d, b, cs):
    chips = DEPTH * PLANE
    anywhere = pl.BlockSpec(memory_space=pl.ANY)
    shape = lambda rows, cols: jax.ShapeDtypeStruct((rows, cols), BF16)
    seqs, length, width = x.shape[0] // 2, x.shape[1] * 2, x.shape[2]
    swapped = jax.ShapeDtypeStruct((seqs, length, width), BF16)
    chunks, total = length // CHUNK, seqs * length
    row = lambda n: pl.BlockSpec((CHUNK, n), lambda s, c: (s * chunks + c, 0))
    keep = lambda *shape: pl.BlockSpec(shape, lambda s, c: (0,) * len(shape))
    wide, count, sem = HEADS * LANES, 5, pltpu.SemaphoreType.DMA
    return pl.pallas_call(
        gather_attend,
        grid=(seqs, chunks),
        in_specs=[anywhere] * 9 + [row(LANES)],
        out_specs=[anywhere] * 7
        + [row(wide), row(wide)]
        + [row(width)] * 5
        + [
            pl.BlockSpec((None, HEADS, LANES, LANES), lambda s, c: (s * chunks + c, 0, 0, 0)),
            keep(8, width),
            keep(1, u.shape[1]),
        ],
        out_shape=[
            swapped,
            swapped,
            shape(q.shape[0] * chips, 3 * q.shape[1]),
            shape(o.shape[0] * chips, o.shape[1]),
            shape(u.shape[0] * chips, u.shape[1]),
            shape(d.shape[0] * chips, d.shape[1]),
            shape(b.shape[0] * chips, b.shape[1]),
            shape(total, wide),
            shape(total, wide),
            shape(total, width),
            shape(total, width),
            shape(total, width),
            shape(total, width),
            jax.ShapeDtypeStruct((total, width), F32),
            jax.ShapeDtypeStruct((seqs * chunks, HEADS, LANES, LANES), BF16),
            jax.ShapeDtypeStruct((8, width), F32),
            jax.ShapeDtypeStruct((1, u.shape[1]), F32),
        ],
        scratch_shapes=[
            pltpu.VMEM((HEADS, LANES, LANES), F32),
            pltpu.VMEM((seqs, length, width), BF16),
            pltpu.VMEM((seqs, x.shape[1], width), BF16),
            pltpu.VMEM((q.shape[0] * chips, 3 * q.shape[1]), BF16),
            pltpu.VMEM((b.shape[0] * chips, b.shape[1]), BF16),
            pltpu.VMEM((16, width), F32),
            sem((8,)),
            sem((2,)),
            sem((count, 6, 3)),
            sem((count, chips)),
            sem((count, chips)),
            sem((count, chips)),
            sem((count, chips)),
            sem((count, chips)),
        ],
        compiler_params=pltpu.CompilerParams(
            collective_id=0,
            has_side_effects=True,
            vmem_limit_bytes=VMEM_LIMIT,
            dimension_semantics=("arbitrary", "arbitrary"),
        ),
        name="gather_attend",
    )(x, ct, q, k, v, o, u, d, b, cs)


class Reduce:
    def __init__(self, here, grads, own, got, corner_x, corner_y, side_x, side_y, column, final, outs, sems):
        self.here, self.grads, self.outs = here, grads, outs
        self.own, self.got = own, got
        self.corner_x, self.corner_y = corner_x, corner_y
        self.side_x, self.side_y = side_x, side_y
        self.levels, self.final = column, final
        (self.load_sem, self.core_send, self.core_recv, self.send_sem, self.recv_sem, self.z_send, self.z_recv,
         self.last_sem) = sems
        self.groups = (here.diagonal, here.across_x, here.across_y, here.spot)
        self.started = []

    def cut(self, t, core):
        rows, cols = self.got[t].shape[2:]
        if t == 0:
            return pl.ds(pl.multiple_of(core * rows, rows), rows), slice(None)
        return slice(None), pl.ds(pl.multiple_of(core * cols, cols), cols)

    def mine(self, t):
        return self.own[t] if self.grads[t] is not None else self.own[t].at[self.here.core]

    def loading(self, t, n):
        rows, cols = self.cut(t, self.here.core)
        source = self.grads[t].at[:, self.groups[n], rows, cols]
        return pltpu.make_async_copy(source, self.own[t].at[:, self.groups[n]], self.load_sem.at[t, n])

    def giving(self, t, n):
        here, spot = self.here, self.groups[n]
        if self.grads[t] is not None:
            rows, cols = self.cut(t, here.other)
            source = self.grads[t].at[:, spot, rows, cols]
        else:
            source = self.own[t].at[here.other, :, spot]
        return remote(
            source, self.got[t].at[:, spot], self.core_send.at[t, n], self.core_recv.at[t, n], here.sibling
        )

    def pushing(self, t, slot):
        here, own = self.here, self.mine(t)
        source, target, peer = (
            (own.at[0:2, here.diagonal], self.corner_x[t], here.x_peer),
            (own.at[2:4, here.diagonal], self.corner_y[t], here.y_peer),
            (own.at[:, here.across_x], self.side_x[t], here.x_peer),
            (own.at[:, here.across_y], self.side_y[t], here.y_peer),
        )[slot]
        return remote(source, target, self.send_sem.at[t, slot], self.recv_sem.at[t, slot], peer)

    def sinking(self, t, n):
        here = self.here
        return remote(
            self.mine(t).at[here.level(n), here.spot],
            self.levels[t].at[n],
            self.z_send.at[t, n],
            self.z_recv.at[t, n],
            here.z_peer(n),
        )

    def ending(self, t):
        here = self.here
        rows, cols = self.cut(t, here.core)
        place = self.outs[t].at[rows, cols]
        keep = pltpu.make_async_copy(self.final[t], place, self.last_sem.at[t, 0])
        give = remote(
            self.final[t], place, self.last_sem.at[t, 1], self.last_sem.at[t, 2], here.sibling
        )
        return keep, give

    def start(self, make, *args):
        make(*args).start()
        self.started.append((make, args))

    def load(self, t):
        for n in range(4):
            self.loading(t, n).start()

    def begin(self, t):
        for n in range(4):
            self.start(self.giving, t, n)

    def joined(self, t, n):
        if self.grads[t] is not None:
            self.loading(t, n).wait()
        self.giving(t, n).wait_recv()

    def add(self, t, spot, first, count, parts):
        own = self.mine(t)

        def one(z, _):
            total = own[z, spot]
            for part in parts:
                total = total + part(z)
            own[z, spot] = total
            return 0

        lax.fori_loop(first, first + count, one, 0)

    def first(self, t):
        spot, got = self.here.diagonal, self.got[t]
        self.joined(t, 0)
        self.add(t, spot, 0, DEPTH, [lambda z: got[z, spot]])
        self.start(self.pushing, t, 0)
        self.start(self.pushing, t, 1)

    def second(self, t):
        here, got = self.here, self.got[t]
        self.joined(t, 1)
        self.joined(t, 2)
        half = DEPTH // 2
        self.add(t, here.across_x, 0, half, [lambda z: got[z, here.across_x]])
        self.add(t, here.across_y, half, half, [lambda z: got[z, here.across_y]])
        self.pushing(t, 1).wait_recv()
        corner = self.corner_y[t]
        self.add(
            t, here.across_x, half, half, [lambda z: got[z, here.across_x], lambda z: corner[z - half]]
        )
        self.start(self.pushing, t, 2)
        self.pushing(t, 0).wait_recv()
        other = self.corner_x[t]
        self.add(t, here.across_y, 0, half, [lambda z: got[z, here.across_y], lambda z: other[z]])
        self.start(self.pushing, t, 3)

    def third(self, t):
        here, got = self.here, self.got[t]
        side_x, side_y = self.side_x[t], self.side_y[t]
        self.joined(t, 3)
        self.pushing(t, 2).wait_recv()
        self.pushing(t, 3).wait_recv()
        own = self.mine(t)

        def one(z, _):
            total = own[z, here.spot].astype(F32) + got[z, here.spot].astype(F32)
            total = total + (side_x[z].astype(F32) + side_y[z].astype(F32))
            own[z, here.spot] = total.astype(own.dtype)
            return 0

        lax.fori_loop(0, DEPTH, one, 0)
        for n in (2, 1, 3):
            self.start(self.sinking, t, n)

    def fourth(self, t):
        for n in range(1, DEPTH):
            self.sinking(t, n).wait_recv()
        total = self.mine(t)[self.here.z, self.here.spot].astype(F32)
        for n in range(1, DEPTH):
            total = total + self.levels[t][n].astype(F32)
        self.final[t][...] = total
        keep, give = self.ending(t)
        keep.start()
        give.start()

    def drain(self):
        for make, args in self.started:
            make(*args).wait_send()
        for t in range(len(self.outs)):
            for copy in self.ending(t):
                copy.wait()


def pack_rows(vector_rows, ub_ref, buffer):
    chips = DEPTH * PLANE
    part = vector_rows.shape[1] // chips
    lane = lax.broadcasted_iota(jnp.int32, (16, LANES), 1)

    def cut(read, position):
        group, shift = position // LANES, position % LANES
        block = read(group)
        if not shift:
            return block
        turned = pltpu.roll(block, LANES - shift, 1)
        if shift + part > LANES:
            turned = jnp.where(lane < LANES - shift, turned, pltpu.roll(read(group + 1), LANES - shift, 1))
        return turned

    line = lax.broadcasted_iota(jnp.int32, (16, LANES), 0)

    def vectors(g):
        return vector_rows[:, g * LANES : (g + 1) * LANES]

    def up(g):
        return jnp.broadcast_to(ub_ref[0:1, g * LANES : (g + 1) * LANES], (16, LANES))

    for c in range(chips):
        block = cut(vectors, c * part)
        for r in range(4):
            block = jnp.where(line == 9 + r, cut(up, (4 * c + r) * part), block)
        for half in range(2):
            buffer[half, c // PLANE, c % PLANE] = block[8 * half : 8 * half + 8]


DURING = {
    1: (("first", 6), ("first", 5)),
    2: (("first", 4), ("second", 6)),
    3: (("second", 5),),
    4: (("second", 4), ("third", 6)),
    5: (("third", 5),),
    6: (("fourth", 6), ("third", 4)),
    7: (("fourth", 5), ("fourth", 4)),
}
AFTER = {
    0: (("first", 2), ("second", 1)),
    1: (("first", 3),),
    2: (("second", 2), ("first", 0)),
    3: (("third", 1), ("second", 3)),
    4: (("second", 0),),
    5: (("third", 2),),
    6: (("fourth", 1),),
    7: (("third", 3), ("third", 0), ("fourth", 2), ("fourth", 3), ("fourth", 0)),
}


def reduce_attend(
    x_hbm, resid_hbm, w_hbm, out_hbm, gvec_ref, gub_ref, g_o, g_u, g_d,
    a_ref, k_ref, v_ref, e_ref, s_ref, sq_ref, sk_ref, cs_ref,
    out4, grad4, r_b, r_q, r_k, r_v, r_o, r_u, r_d,
    after, back, x_all, weights, gb, rows, bounce, resid_tile, grad_tile, *scratch,
):
    kinds = 7
    names = ("own", "got", "corner_x", "corner_y", "side_x", "side_y", "column", "final")
    parts = [scratch[n * kinds : (n + 1) * kinds] for n in range(len(names))]
    swap_sem, big_sem, tile_sem, *sems = scratch[len(names) * kinds :]
    here = Place()
    seq, chunk, chunks = pl.program_id(0), pl.program_id(1), pl.num_programs(1)
    step = seq * chunks + chunk
    last = pl.num_programs(0) * chunks - 1
    reduce = Reduce(
        here, (None, None, None, None, g_o, g_u, g_d), *parts, (r_b, r_q, r_k, r_v, r_o, r_u, r_d), sems
    )
    pairs, length, width = out_hbm.shape
    block = length // 2
    fetch = pltpu.make_async_copy(
        out_hbm.at[:, pl.ds(pl.multiple_of(here.core * block, block), block), :], bounce, swap_sem.at[0]
    )
    place = out4.at[pl.ds(here.core * pairs, pairs)]
    keep = pltpu.make_async_copy(bounce, place, swap_sem.at[1])
    give = remote(
        out_hbm.at[:, pl.ds(pl.multiple_of(here.other * block, block), block), :],
        place,
        swap_sem.at[2],
        swap_sem.at[3],
        here.sibling,
    )
    big = [
        pltpu.make_async_copy(source, target, big_sem.at[n])
        for n, (source, target) in enumerate(((x_hbm, x_all), (w_hbm, weights)))
    ]

    @pl.when(step == 0)
    def _():
        gb[...] = jnp.zeros_like(gb)
        for t in (6, 5, 4):
            reduce.load(t)
        fetch.start()
        meet(here)
        for t in (6, 5, 4):
            reduce.begin(t)
        give.start()

    for n, stages in DURING.items():

        @pl.when(step == n)
        def _(n=n, stages=stages):
            if n == 1:
                fetch.wait()
                keep.start()
                for copy in big:
                    copy.start()
            for stage, t in stages:
                getattr(reduce, stage)(t)

    @pl.when(chunk == 0)
    def _():
        after[...] = jnp.zeros_like(after)

    at = pl.multiple_of((seq * chunks + chunks - 1 - chunk) * CHUNK, CHUNK)
    attend_back(
        a_ref, k_ref, v_ref, e_ref, s_ref, sq_ref, sk_ref, cs_ref, after, back.at[pl.ds(at, CHUNK), :], gb
    )

    @pl.when(step == last)
    def _():
        for copy in big:
            copy.wait()
        rows[0:3, :] = jnp.concatenate([gb[:, n * width : (n + 1) * width] for n in range(3)])
        rows[3:9, :] = gvec_ref[0:6, :]
        rows[9:16, :] = jnp.zeros((7, width), F32)
        pack_rows(rows, gub_ref, parts[0][0])
        tiles = pairs * length // CHUNK
        loads = [
            pltpu.make_async_copy(
                resid_hbm.at[i * CHUNK : (i + 1) * CHUNK, :], resid_tile.at[i % 2], tile_sem.at[i % 2, 0]
            )
            for i in range(tiles)
        ]
        loads[0].start()
        for n in range(3):
            t = 1 + n
            total = dot_tn(x_all[...], back[:, n * width : (n + 1) * width]).astype(BF16)
            for half in range(2):
                cols = slice(half * (width // 2), (half + 1) * (width // 2))
                own = parts[0][t]
                own[half] = total[:, cols].reshape(own.shape[1:])
            reduce.begin(t)
            if n == 0:
                reduce.begin(0)
            if n == 1:
                reduce.first(1)

        def writes(i):
            s, c = i // chunks_, i % chunks_
            spot = grad4.at[here.core * pairs + s, pl.ds((c % (chunks_ // 2)) * CHUNK, CHUNK), :]
            local = pltpu.make_async_copy(grad_tile.at[i % 2], spot, tile_sem.at[i % 2, 1])
            away = remote(grad_tile.at[i % 2], spot, tile_sem.at[i % 2, 2], arrive_sem.at[i], here.sibling)
            return local, away, here.core == c // (chunks_ // 2)

        chunks_ = length // CHUNK
        arrive_sem = swap_sem.at[4:]

        def written(i):
            local, away, stays = writes(i)

            @pl.when(stays)
            def _():
                local.wait()

            @pl.when(jnp.logical_not(stays))
            def _():
                away.wait_send()

        for i in range(tiles):
            for stage, t in AFTER[i]:
                if i < tiles - 1:
                    getattr(reduce, stage)(t)
            if i + 1 < tiles:
                loads[i + 1].start()
            loads[i].wait()
            if i >= 2:
                written(i - 2)
            piece = back[i * CHUNK : (i + 1) * CHUNK, :]
            grad_tile[i % 2] = resid_tile[i % 2] + dot_nt(piece, weights[...])
            local, away, stays = writes(i)

            @pl.when(stays)
            def _(local=local):
                local.start()

            @pl.when(jnp.logical_not(stays))
            def _(away=away):
                away.start()

        for stage, t in AFTER[tiles - 1]:
            getattr(reduce, stage)(t)
        for i in range(tiles - 2, tiles):
            written(i)
        for i in range(tiles):
            _, away, stays = writes(i)

            @pl.when(stays)
            def _(away=away):
                away.wait_recv()

        keep.wait()
        give.wait()
        reduce.drain()


def reduce_attend_call(x, resid, w, out, gvec, gub, go, gu, gd, a, k, v, e, s, sq, sk, cs):
    chips = DEPTH * PLANE
    seqs, length, width = out.shape
    total, chunks, wide = seqs * length, length // CHUNK, HEADS * LANES
    anywhere = pl.BlockSpec(memory_space=pl.ANY)
    place = lambda s, c: s * chunks + chunks - 1 - c
    row = lambda n: pl.BlockSpec((CHUNK, n), lambda s, c: (place(s, c), 0))
    once = lambda a: pl.BlockSpec(
        a.shape, lambda s, c: (0,) * len(a.shape), pipeline_mode=pl.Buffered(1)
    )
    views = [g.reshape(DEPTH, PLANE, g.shape[0] // chips, g.shape[1]) for g in (go, gu, gd)]
    part = width // chips
    pieces = [(8, LANES, F32)] + [(part, width // 2, BF16)] * 3
    pieces += [(g.shape[2], g.shape[3] // 2, BF16) for g in views]
    kinds, sem = len(pieces), pltpu.SemaphoreType.DMA
    grid = (DEPTH, PLANE)
    scratch = [pltpu.VMEM((2,) + grid + p[:2], p[2]) for p in pieces[:4]]
    scratch += [pltpu.VMEM(grid + p[:2], p[2]) for p in pieces[4:]]
    for lead in (grid, (2,), (2,), (DEPTH,), (DEPTH,), (DEPTH,)):
        scratch += [pltpu.VMEM(lead + p[:2], p[2]) for p in pieces]
    scratch += [pltpu.VMEM(p[:2], F32) for p in pieces]
    scratch += [sem((4 + total // CHUNK,)), sem((2,)), sem((2, 3))]
    scratch += [sem((kinds, 4))] * 7 + [sem((kinds, 3))]
    shard = lambda rows, cols: jax.ShapeDtypeStruct((rows, cols), F32)
    return pl.pallas_call(
        reduce_attend,
        grid=(seqs, chunks),
        in_specs=[anywhere] * 4
        + [once(gvec), once(gub)]
        + [anywhere] * 3
        + [row(wide), row(wide), row(width), row(wide)]
        + [pl.BlockSpec((None, HEADS, LANES, LANES), lambda s, c: (place(s, c), 0, 0, 0))]
        + [row(width), row(width), row(LANES)],
        out_specs=[anywhere] * 9,
        out_shape=[
            jax.ShapeDtypeStruct((seqs * 2, length // 2, width), BF16),
            jax.ShapeDtypeStruct((seqs * 2, length // 2, width), F32),
            shard(16, LANES),
            shard(part, width),
            shard(part, width),
            shard(part, width),
            shard(part, width),
            shard(views[1].shape[2], views[1].shape[3]),
            shard(views[2].shape[2], views[2].shape[3]),
        ],
        scratch_shapes=[
            pltpu.VMEM((HEADS, LANES, LANES), F32),
            pltpu.VMEM((total, 3 * width), BF16),
            pltpu.VMEM((total, width), BF16),
            pltpu.VMEM(w.shape, BF16),
            pltpu.VMEM((1, 3 * width), F32),
            pltpu.VMEM((16, width), F32),
            pltpu.VMEM((seqs, length // 2, width), BF16),
            pltpu.VMEM((2, CHUNK, width), F32),
            pltpu.VMEM((2, CHUNK, width), F32),
        ]
        + scratch,
        compiler_params=pltpu.CompilerParams(
            collective_id=1,
            has_side_effects=True,
            vmem_limit_bytes=VMEM_LIMIT,
            dimension_semantics=("arbitrary", "arbitrary"),
        ),
        name="reduce_attend",
    )(x, resid, w, out, gvec, gub, *views, a, k, v, e, s, sq, sk, cs)


def pack_vectors(vectors, up_bias):
    part = vectors[0].shape[0]
    stacked = jnp.concatenate([jnp.stack(vectors), up_bias.reshape(-1, part)])
    return jnp.pad(stacked, ((0, 16 - stacked.shape[0]), (0, LANES - part)))


def unpack_vectors(gathered, part):
    chips = gathered.shape[0] // 16
    grid = gathered.reshape(chips, 16, LANES)[:, :13, :part].astype(F32)
    rows = jnp.transpose(grid[:, :9], (1, 0, 2)).reshape(9, chips * part)
    up_bias = grid[:, 9:].reshape(1, chips * 4 * part)
    return rows[0:3], jnp.pad(rows[3:9], ((0, 2), (0, 0))), up_bias


def pack_vector_grads(gb, gvec, gub, chips):
    width = gvec.shape[1]
    part = width // chips
    rows = jnp.concatenate([gb.reshape(3, width), gvec[0:6]]).reshape(9, chips, part)
    rows = jnp.transpose(rows, (1, 0, 2))
    grid = jnp.concatenate([rows, gub.reshape(chips, 4, part)], axis=1)
    grid = jnp.pad(grid, ((0, 0), (0, 3), (0, LANES - part)))
    return grid.reshape(chips * 16, LANES)


def local(
    inputs,
    horizon,
    query_weight,
    query_bias,
    key_weight,
    key_bias,
    value_weight,
    value_bias,
    out_weight,
    out_bias,
    first_gain,
    first_shift,
    up_weight,
    up_bias,
    down_weight,
    down_bias,
    second_gain,
    second_shift,
    cotangent,
):
    chips = lax.axis_size("dp")
    core = lax.axis_index("seq")
    part = query_bias.shape[0]
    seqs = inputs.shape[0] // 2
    direct = chips == DEPTH * PLANE
    vectors = pack_vectors(
        (
            query_bias,
            key_bias,
            value_bias,
            out_bias,
            first_gain,
            first_shift,
            down_bias,
            second_gain,
            second_shift,
        ),
        up_bias,
    )
    weights = (query_weight, key_weight, value_weight, out_weight, up_weight, down_weight)
    spans = lax.dynamic_slice_in_dim(horizon, core * seqs, seqs)
    length = 2 * inputs.shape[1]
    chunks = length // CHUNK
    cs = rotation(spans, length)
    flat = lambda a: a.reshape(-1, a.shape[-1])
    if direct:
        x, ct, wqkv, wo, wu, wd, _, *saved, vec, ubias = gather_attend_call(
            inputs, cotangent, *weights, vectors, cs
        )
    else:
        gather = lambda a: lax.all_gather(a, "dp", axis=0, tiled=True)
        x, ct = (lax.all_to_all(a, "seq", 0, 1, tiled=True) for a in (inputs, cotangent))
        wqkv = gather(jnp.concatenate(weights[:3], axis=1))
        wo, wu, wd, gathered = (gather(a) for a in (*weights[3:], vectors))
        bqkv, vec, ubias = unpack_vectors(gathered, part)
        saved = forward_call(flat(x), wqkv, bqkv, cs, chunks)
    a, k, v, sq, sk, mixed, den, s = saved
    fx = flat(x)
    out, resid, e, go, gu, gd, gvec, gub = middle_call(
        fx, flat(ct), mixed, den, vec, ubias, wo, wu, wd
    )
    out = out.reshape(x.shape)
    if direct:
        out, grad, gvectors, gq, gk, gv, go, gu, gd = reduce_attend_call(
            fx, resid, wqkv, out, gvec, gub, go, gu, gd, a, k, v, e, s, sq, sk, cs
        )
    else:
        grad, gw, gb = backward_call(fx, a, k, v, e, s, sq, sk, cs, resid, wqkv, chunks)
        gvectors = pack_vector_grads(gb, gvec, gub, chips)
        out, grad = (
            lax.all_to_all(a, "seq", 1, 0, tiled=True) for a in (out, grad.reshape(x.shape))
        )
        total = lambda g: lax.psum(
            lax.psum_scatter(g.astype(F32), "dp", scatter_dimension=0, tiled=True), "seq"
        )
        gw, go, gu, gd, gvectors = (total(g) for g in (gw, go, gu, gd, gvectors))
        gq, gk, gv = jnp.split(gw, 3, axis=1)
    rows = gvectors[:, :part]
    return (
        out,
        grad,
        gq,
        rows[0],
        gk,
        rows[1],
        gv,
        rows[2],
        go,
        rows[3],
        rows[4],
        rows[5],
        gu,
        rows[9:13].reshape(-1),
        gd,
        rows[6],
        rows[7],
        rows[8],
    )


def solution(mesh):
    long, wide, thin = P("dp", "seq", None), P("dp", None), P("dp")
    shards = (wide, thin, wide, thin, wide, thin, wide, thin, thin, thin, wide, thin, wide, thin, thin, thin)
    return jax.shard_map(
        local,
        mesh=mesh,
        in_specs=(long, thin, *shards, long),
        out_specs=(long, long, *shards),
        check_vma=False,
    )
```

```python
import functools
import math

import jax
import jax.numpy as jnp
from jax import lax
from jax.experimental import pallas as pl
from jax.experimental.pallas import tpu as pltpu
from jax.sharding import PartitionSpec as P

HEADS = 12
HEAD = 64
PAIRS = HEADS // 2
LANES = 128
CHUNK = 256
ROWS = 512
NORM_EPS = 1e-05
GELU_A = 0.7978845608
GELU_B = 0.044715
VMEM_LIMIT = 60 * 1024 * 1024
F32, BF16 = jnp.float32, jnp.bfloat16


def dot_nn(a, b):
    return lax.dot_general(a, b, (((1,), (0,)), ((), ())), preferred_element_type=F32)


def dot_nt(a, b):
    return lax.dot_general(a, b, (((1,), (1,)), ((), ())), preferred_element_type=F32)


def dot_tn(a, b):
    return lax.dot_general(a, b, (((0,), (0,)), ((), ())), preferred_element_type=F32)


def low_lanes(rows):
    return lax.broadcasted_iota(jnp.int32, (rows, LANES), 1) < HEAD


def swap(values):
    return pltpu.roll(values, HEAD, 1)


def softplus_and_slope(values):
    e = jnp.exp(-jnp.abs(values))
    plus = jnp.maximum(values, 0.0) + jnp.log1p(e)
    slope = jnp.where(values >= 0.0, 1.0, e) / (1.0 + e)
    return plus, slope


def attend_forward(
    x_ref, w_ref, b_ref, cs_ref, a_ref, k_ref, v_ref, sq_ref, sk_ref, mixed_ref, den_ref, s_ref, state
):
    @pl.when(pl.program_id(1) == 0)
    def _():
        state[...] = jnp.zeros_like(state)

    attend(
        x_ref[...],
        w_ref,
        b_ref,
        cs_ref,
        a_ref,
        k_ref,
        v_ref,
        sq_ref,
        sk_ref,
        mixed_ref,
        den_ref,
        s_ref,
        state,
    )


def attend(
    x, w_ref, b_ref, cs_ref, a_ref, k_ref, v_ref, sq_ref, sk_ref, mixed_ref, den_ref, s_ref, state
):
    rows, width = x.shape
    cs = cs_ref[...]
    low = low_lanes(rows)
    causal = lax.broadcasted_iota(jnp.int32, (rows, rows), 0) >= lax.broadcasted_iota(
        jnp.int32, (rows, rows), 1
    )

    for half in range(2):
        slope_ref = (sq_ref, sk_ref)[half]
        feature_ref = (a_ref, k_ref)[half]
        pre = dot_nn(x, w_ref[:, half * width : (half + 1) * width])
        pre = pre + b_ref[half : half + 1, :]
        plus, slope = softplus_and_slope(pre)
        slope_ref[...] = slope.astype(BF16)
        for pair in range(PAIRS):
            both = plus[:, pair * LANES : (pair + 1) * LANES]
            other = swap(both)
            even = jnp.where(low, both, other) * cs
            odd = jnp.where(low, other, both) * cs
            feature_ref[:, (2 * pair) * LANES : (2 * pair + 1) * LANES] = even.astype(BF16)
            feature_ref[:, (2 * pair + 1) * LANES : (2 * pair + 2) * LANES] = odd.astype(BF16)
    values = dot_nn(x, w_ref[:, 2 * width :]) + b_ref[2:3, :]
    v_ref[...] = values.astype(BF16)
    for pair in range(PAIRS):
        both = values[:, pair * LANES : (pair + 1) * LANES]
        results = []
        for odd in range(2):
            head = 2 * pair + odd
            query = a_ref[:, head * LANES : (head + 1) * LANES]
            key = k_ref[:, head * LANES : (head + 1) * LANES]
            wide = (jnp.where(low, 1.0, both) if odd else jnp.where(low, both, 1.0)).astype(BF16)
            scores = jnp.where(causal, dot_nt(query, key), 0.0).astype(BF16)
            before = state[head]
            before_low = before.astype(BF16)
            s_ref[head] = before_low
            results.append(dot_nn(scores, wide) + dot_nn(query, before_low))
            state[head] = before + dot_tn(key, wide)
        numer = jnp.where(low, results[0], results[1])
        denom = swap(jnp.where(low, results[1], results[0]))
        mixed_ref[:, pair * LANES : (pair + 1) * LANES] = (numer / denom).astype(BF16)
        den_ref[:, pair * LANES : (pair + 1) * LANES] = denom


def forward_call(x, w, b, cs, chunks):
    total, width = x.shape
    seqs = total // (chunks * CHUNK)
    row = lambda n: pl.BlockSpec((CHUNK, n), lambda s, c: (s * chunks + c, 0))
    once = lambda shape: pl.BlockSpec(
        shape, lambda s, c: (0,) * len(shape), pipeline_mode=pl.Buffered(1)
    )
    wide = HEADS * LANES
    return pl.pallas_call(
        attend_forward,
        grid=(seqs, chunks),
        in_specs=[row(width), once(w.shape), once(b.shape), row(LANES)],
        out_specs=[
            row(wide),
            row(wide),
            row(width),
            row(width),
            row(width),
            row(width),
            row(width),
            pl.BlockSpec((None, HEADS, LANES, LANES), lambda s, c: (s * chunks + c, 0, 0, 0)),
        ],
        out_shape=[
            jax.ShapeDtypeStruct((total, wide), BF16),
            jax.ShapeDtypeStruct((total, wide), BF16),
            jax.ShapeDtypeStruct((total, width), BF16),
            jax.ShapeDtypeStruct((total, width), BF16),
            jax.ShapeDtypeStruct((total, width), BF16),
            jax.ShapeDtypeStruct((total, width), BF16),
            jax.ShapeDtypeStruct((total, width), F32),
            jax.ShapeDtypeStruct((seqs * chunks, HEADS, LANES, LANES), BF16),
        ],
        scratch_shapes=[pltpu.VMEM((HEADS, LANES, LANES), F32)],
        compiler_params=pltpu.CompilerParams(
            dimension_semantics=("arbitrary", "arbitrary"), vmem_limit_bytes=VMEM_LIMIT
        ),
        name="attend_forward",
    )(x, w, b, cs)


def row_mean(values):
    return jnp.mean(values, axis=-1, keepdims=True)


def norm_parts(values):
    center = values - row_mean(values)
    scale = lax.rsqrt(row_mean(center * center) + NORM_EPS)
    return center * scale, scale


def norm_back(grad, gain, unit, scale):
    scaled = grad * gain
    return (scaled - row_mean(scaled) - unit * row_mean(scaled * unit)) * scale


def add_rows(values):
    return jnp.sum(values, axis=0, keepdims=True)


def middle(
    tiles,
    x_ref,
    ct_ref,
    mixed_ref,
    den_ref,
    vec_ref,
    ubias_ref,
    wo_ref,
    wu_ref,
    wd_ref,
    out_ref,
    resid_ref,
    e_ref,
    act,
    hidden_ref,
    normed_ref,
    ffn_ref,
    branch_ref,
    gvec_ref,
    gub_ref,
    slope,
):
    step = pl.program_id(0)
    rows, width = x_ref.shape
    hidden_width = wu_ref.shape[1]
    tile = hidden_width // tiles
    low = low_lanes(rows)

    @pl.when(step == 0)
    def _():
        gvec_ref[...] = jnp.zeros_like(gvec_ref)
        gub_ref[...] = jnp.zeros_like(gub_ref)

    out_bias, gain1, shift1 = vec_ref[0:1], vec_ref[1:2], vec_ref[2:3]
    down_bias, gain2, shift2 = vec_ref[3:4], vec_ref[4:5], vec_ref[5:6]
    mixed = mixed_ref[...]
    resid = x_ref[...].astype(F32) + (dot_nn(mixed, wo_ref[...]) + out_bias)
    unit1, scale1 = norm_parts(resid)
    normed = unit1 * gain1 + shift1
    normed_low = normed.astype(BF16)
    normed_ref[...] = normed_low
    ffn = jnp.zeros((rows, width), F32)
    for t in range(tiles):
        cols = slice(t * tile, (t + 1) * tile)
        hidden = dot_nn(normed_low, wu_ref[:, cols]) + ubias_ref[:, cols]
        square = hidden * hidden
        inner = hidden * (GELU_A + (GELU_A * GELU_B) * square)
        tanh = jnp.tanh(inner)
        half = 0.5 + 0.5 * tanh
        active = (hidden * half).astype(BF16)
        curve = half + (0.5 * hidden) * (1.0 - tanh * tanh) * (
            GELU_A + (3.0 * GELU_A * GELU_B) * square
        )
        act[:, cols] = active
        slope[:, cols] = curve.astype(BF16)
        ffn = ffn + dot_nn(active, wd_ref[cols, :])
    unit2, scale2 = norm_parts(normed + (ffn + down_bias))
    out_ref[...] = (unit2 * gain2 + shift2).astype(BF16)
    grad = ct_ref[...].astype(F32)
    back_final = norm_back(grad, gain2, unit2, scale2)
    back_ffn = back_final.astype(BF16)
    ffn_ref[...] = back_ffn
    gvec_ref[4:5] += add_rows(grad * unit2)
    gvec_ref[5:6] += add_rows(grad)
    gvec_ref[3:4] += add_rows(back_ffn.astype(F32))
    back_normed = back_final
    for t in range(tiles):
        cols = slice(t * tile, (t + 1) * tile)
        back_active = dot_nt(back_ffn, wd_ref[cols, :])
        back_hidden = (back_active * slope[:, cols].astype(F32)).astype(BF16)
        hidden_ref[:, cols] = back_hidden
        gub_ref[:, cols] += add_rows(back_hidden.astype(F32))
        back_normed = back_normed + dot_nt(back_hidden, wu_ref[:, cols])
    gvec_ref[1:2] += add_rows(back_normed * unit1)
    gvec_ref[2:3] += add_rows(back_normed)
    back_resid = norm_back(back_normed, gain1, unit1, scale1)
    resid_ref[...] = back_resid
    back_branch = back_resid.astype(BF16)
    branch_ref[...] = back_branch
    gvec_ref[0:1] += add_rows(back_branch.astype(F32))
    back_mixed = dot_nt(back_branch, wo_ref[...])
    inverse = 1.0 / den_ref[...]
    back_numer = back_mixed * inverse
    product = back_numer * mixed.astype(F32)
    high = product.astype(BF16)
    rest = (product - high.astype(F32)).astype(BF16)
    same_head = (
        lax.broadcasted_iota(jnp.int32, (2 * LANES, 2 * LANES), 0) // HEAD
        == lax.broadcasted_iota(jnp.int32, (2 * LANES, 2 * LANES), 1) // HEAD
    ).astype(F32).astype(BF16)
    even_lane = lax.broadcasted_iota(jnp.int32, (rows, LANES), 1) % 2 == 0
    for block in range(width // (2 * LANES)):
        cols = slice(block * 2 * LANES, (block + 1) * 2 * LANES)
        sums = dot_nn(high[:, cols], same_head) + dot_nn(rest[:, cols], same_head)
        for inside in range(2):
            pair = 2 * block + inside
            back = -sums[:, inside * LANES : (inside + 1) * LANES]
            back_high = back.astype(BF16).astype(F32)
            spread = swap(jnp.where(even_lane, back_high, back - back_high) * (2.0 / HEAD))
            numer = back_numer[:, pair * LANES : (pair + 1) * LANES]
            e_ref[:, (2 * pair) * LANES : (2 * pair + 1) * LANES] = jnp.where(
                low, numer, spread
            ).astype(BF16)
            e_ref[:, (2 * pair + 1) * LANES : (2 * pair + 2) * LANES] = jnp.where(
                low, spread, numer
            ).astype(BF16)


def middle_call(x, ct, mixed, den, vec, ubias, wo, wu, wd, tiles=4):
    total, width = x.shape
    hidden_width = wu.shape[1]
    row = lambda n: pl.BlockSpec((ROWS, n), lambda i: (i, 0))
    once = lambda shape: pl.BlockSpec(
        shape, lambda i: (0,) * len(shape), pipeline_mode=pl.Buffered(1)
    )
    keep = lambda shape: pl.BlockSpec(shape, lambda i: (0,) * len(shape))
    wide = HEADS * LANES
    shape = lambda n, kind=BF16: jax.ShapeDtypeStruct((total, n), kind)
    return pl.pallas_call(
        functools.partial(middle, tiles),
        grid=(total // ROWS,),
        in_specs=[
            row(width),
            row(width),
            row(width),
            row(width),
            once(vec.shape),
            once(ubias.shape),
            once(wo.shape),
            once(wu.shape),
            once(wd.shape),
        ],
        out_specs=[
            row(width),
            row(width),
            row(wide),
            row(hidden_width),
            row(hidden_width),
            row(width),
            row(width),
            row(width),
            keep((8, width)),
            keep((1, hidden_width)),
        ],
        out_shape=[
            shape(width),
            shape(width, F32),
            shape(wide),
            shape(hidden_width),
            shape(hidden_width),
            shape(width),
            shape(width),
            shape(width),
            jax.ShapeDtypeStruct((8, width), F32),
            jax.ShapeDtypeStruct((1, hidden_width), F32),
        ],
        scratch_shapes=[pltpu.VMEM((ROWS, hidden_width), BF16)],
        compiler_params=pltpu.CompilerParams(
            dimension_semantics=("arbitrary",), vmem_limit_bytes=VMEM_LIMIT
        ),
        name="middle",
    )(x, ct, mixed, den, vec, ubias, wo, wu, wd)


def attend_back(a_ref, k_ref, v_ref, e_ref, s_ref, sq_ref, sk_ref, cs_ref, after, back, gb_ref):
    rows, width = v_ref.shape
    cs = cs_ref[...]
    low = low_lanes(rows)
    i = lax.broadcasted_iota(jnp.int32, (rows, rows), 0)
    j = lax.broadcasted_iota(jnp.int32, (rows, rows), 1)
    causal, anti = i >= j, i <= j
    for pair in range(PAIRS):
        both = v_ref[:, pair * LANES : (pair + 1) * LANES].astype(F32)
        back_q, back_k, back_v = [], [], []
        for odd in range(2):
            head = 2 * pair + odd
            cols = slice(head * LANES, (head + 1) * LANES)
            query, key, e = a_ref[:, cols], k_ref[:, cols], e_ref[:, cols]
            wide = (jnp.where(low, 1.0, both) if odd else jnp.where(low, both, 1.0)).astype(BF16)
            state = s_ref[head]
            later = after[head]
            later_low = later.astype(BF16)
            scores_t = jnp.where(anti, dot_nt(key, query), 0.0).astype(BF16)
            back_s = jnp.where(causal, dot_nt(e, wide), 0.0).astype(BF16)
            back_st = jnp.where(anti, dot_nt(wide, e), 0.0).astype(BF16)
            y = (dot_nn(back_s, key) + dot_nt(e, state)) * cs
            back_q.append(y + swap(y))
            y = (dot_nn(back_st, query) + dot_nt(wide, later_low)) * cs
            back_k.append(y + swap(y))
            back_v.append(dot_nn(scores_t, e) + dot_nn(key, later_low))
            after[head] = later + dot_tn(query, e)
        cols = slice(pair * LANES, (pair + 1) * LANES)
        dq = jnp.where(low, back_q[0], back_q[1]) * sq_ref[:, cols].astype(F32)
        dk = jnp.where(low, back_k[0], back_k[1]) * sk_ref[:, cols].astype(F32)
        dv = jnp.where(low, back_v[0], back_v[1])
        for n, piece in enumerate((dq, dk, dv)):
            piece = piece.astype(BF16)
            cols = slice(n * width + pair * LANES, n * width + (pair + 1) * LANES)
            back[:, cols] = piece
            gb_ref[:, cols] += add_rows(piece.astype(F32))


def attend_backward(
    x_ref,
    a_ref,
    k_ref,
    v_ref,
    e_ref,
    s_ref,
    sq_ref,
    sk_ref,
    cs_ref,
    resid_ref,
    w_ref,
    grad_ref,
    gw_ref,
    gb_ref,
    after,
    back,
    gw,
):
    rows, width = x_ref.shape

    @pl.when((pl.program_id(0) == 0) & (pl.program_id(1) == 0))
    def _():
        gw[...] = jnp.zeros_like(gw)
        gb_ref[...] = jnp.zeros_like(gb_ref)

    @pl.when(pl.program_id(1) == 0)
    def _():
        after[...] = jnp.zeros_like(after)

    attend_back(a_ref, k_ref, v_ref, e_ref, s_ref, sq_ref, sk_ref, cs_ref, after, back, gb_ref)
    x = x_ref[...]
    total = resid_ref[...]
    for n in range(3):
        cols = slice(n * width, (n + 1) * width)
        piece = back[:, cols]
        gw[:, cols] += dot_tn(x, piece)
        total = total + dot_nt(piece, w_ref[:, cols])
    grad_ref[...] = total

    @pl.when((pl.program_id(0) == pl.num_programs(0) - 1) & (pl.program_id(1) == pl.num_programs(1) - 1))
    def _():
        gw_ref[...] = gw[...].astype(BF16)


def backward_call(x, a, k, v, e, s, sq, sk, cs, resid, w, chunks):
    total, width = x.shape
    seqs = total // (chunks * CHUNK)
    place = lambda s, c: s * chunks + chunks - 1 - c
    row = lambda n: pl.BlockSpec((CHUNK, n), lambda s, c: (place(s, c), 0))
    once = lambda shape: pl.BlockSpec(
        shape, lambda s, c: (0,) * len(shape), pipeline_mode=pl.Buffered(1)
    )
    keep = lambda shape: pl.BlockSpec(shape, lambda s, c: (0,) * len(shape))
    wide = HEADS * LANES
    return pl.pallas_call(
        attend_backward,
        grid=(seqs, chunks),
        in_specs=[
            row(width),
            row(wide),
            row(wide),
            row(width),
            row(wide),
            pl.BlockSpec((None, HEADS, LANES, LANES), lambda s, c: (place(s, c), 0, 0, 0)),
            row(width),
            row(width),
            row(LANES),
            row(width),
            once(w.shape),
        ],
        out_specs=[row(width), keep(w.shape), keep((1, w.shape[1]))],
        out_shape=[
            jax.ShapeDtypeStruct((total, width), F32),
            jax.ShapeDtypeStruct(w.shape, BF16),
            jax.ShapeDtypeStruct((1, w.shape[1]), F32),
        ],
        scratch_shapes=[
            pltpu.VMEM((HEADS, LANES, LANES), F32),
            pltpu.VMEM((CHUNK, w.shape[1]), BF16),
            pltpu.VMEM(w.shape, F32),
        ],
        compiler_params=pltpu.CompilerParams(
            dimension_semantics=("arbitrary", "arbitrary"), vmem_limit_bytes=VMEM_LIMIT
        ),
        name="attend_backward",
    )(x, a, k, v, e, s, sq, sk, cs, resid, w)


def rotation(horizon, length):
    seqs = horizon.shape[0]
    position = jnp.arange(length, dtype=F32)
    angles = 0.5 * math.pi * position[None, :] / horizon.astype(F32)[:, None]
    return jnp.concatenate(
        [
            jnp.broadcast_to(jnp.cos(angles)[..., None], (seqs, length, HEAD)),
            jnp.broadcast_to(jnp.sin(angles)[..., None], (seqs, length, HEAD)),
        ],
        axis=-1,
    ).reshape(seqs * length, LANES)


DEPTH, PLANE = 4, 4


class Place:
    def __init__(self):
        self.dp, self.core = lax.axis_index("dp"), lax.axis_index("seq")
        self.z, self.spot = self.dp // PLANE, self.dp % PLANE
        self.other = 1 - self.core
        self.levels = [(self.z + step) % DEPTH for step in range(DEPTH)]
        self.across_x = self.spot + 1 - 2 * (self.spot % 2)
        self.across_y = (self.spot + 2) % PLANE
        self.diagonal = PLANE - 1 - self.spot
        self.x_peer = (self.z * PLANE + self.across_x, self.core)
        self.y_peer = (self.z * PLANE + self.across_y, self.core)
        self.sibling = (self.dp, self.other)

    def level(self, step):
        return self.levels[step]

    def z_peer(self, step):
        return (self.level(step) * PLANE + self.spot, self.core)


def remote(source, target, send, recv, peer):
    copy = pltpu.make_async_remote_copy(
        src_ref=source,
        dst_ref=target,
        send_sem=send,
        recv_sem=recv,
        device_id=peer,
        device_id_type=pl.DeviceIdType.MESH,
    )
    return copy


def meet(here):
    barrier = pltpu.get_barrier_semaphore()
    peers = [here.x_peer, here.y_peer, here.sibling] + [here.z_peer(n) for n in range(1, DEPTH)]
    for peer in peers:
        pl.semaphore_signal(barrier, inc=1, device_id=peer, device_id_type=pl.DeviceIdType.MESH)
    pl.semaphore_wait(barrier, len(peers))


class Gather:
    def __init__(self, here, shards, outs, own_send, x_send, y_send, c_send, link_recv, core_recv):
        self.here, self.shards, self.outs = here, shards, outs
        self.own_send, self.link_recv, self.core_recv = own_send, link_recv, core_recv
        self.sems = {"x": x_send, "y": y_send, "c": c_send}
        self.heights = [out.shape[0] // (DEPTH * PLANE) for out in outs]
        self.started = []

    def index(self, level, spot):
        return level * PLANE + spot

    def rows(self, t, level, spot):
        height = self.heights[t]
        return pl.ds(pl.multiple_of(self.index(level, spot) * height, height), height)

    def piece(self, t, level, spot, core):
        half = self.heights[t] // 2
        start = self.index(level, spot) * self.heights[t] + core * half
        return self.outs[t].at[pl.ds(pl.multiple_of(start, half), half), :]

    def passing(self, t, level, spot, kind):
        here, at = self.here, self.index(level, spot)
        peer = {"x": here.x_peer, "y": here.y_peer, "c": here.sibling}[kind]
        arrive = self.core_recv if kind == "c" else self.link_recv
        ref = self.piece(t, level, spot, here.core)
        return [remote(ref, ref, self.sems[kind].at[t, at], arrive.at[t, at], peer)]

    def spreading(self, t, slot):
        here, height = self.here, self.heights[t]
        whole = slot == 2
        peer = (here.x_peer, here.y_peer, here.sibling)[slot] if slot < 3 else here.z_peer(slot - 2)
        mine = self.index(here.z, here.spot)
        arrive = (self.core_recv if whole else self.link_recv).at[t, mine]
        half = height // 2
        if whole:
            take, place = pl.ds(0, height), self.rows(t, here.z, here.spot)
        else:
            take = pl.ds(pl.multiple_of(here.core * half, half), half)
            place = pl.ds(pl.multiple_of(mine * height + here.core * half, half), half)
        copies = []
        for n, ref in enumerate(self.shards[t]):
            target = self.outs[t].at[place, n * ref.shape[1] : (n + 1) * ref.shape[1]]
            copies.append(
                remote(ref.at[take, :], target, self.own_send.at[t, slot, n], arrive, peer)
            )
        return copies

    def start(self, make, *args):
        for copy in make(*args):
            copy.start()
        self.started.append((make, args))

    def drain(self):
        for make, args in self.started:
            for copy in make(*args):
                copy.wait_send()

    def arrived(self, t, level, spot):
        ref = self.piece(t, level, spot, self.here.core)
        sem = self.link_recv.at[t, self.index(level, spot)]
        remote(ref, ref, sem, sem, self.here.x_peer).wait_recv()

    def begin(self, t):
        for slot in range(3):
            self.start(self.spreading, t, slot)

    def rise(self, t):
        for n in (1, 3, 2):
            self.start(self.spreading, t, 2 + n)

    def column(self, t):
        here = self.here
        for n in (1, 3, 2):
            self.arrived(t, here.level(n), here.spot)
            for kind in "xyc":
                self.start(self.passing, t, here.level(n), here.spot, kind)

    def cross(self, t):
        here = self.here
        for n in (0, 1, 3, 2):
            for spot, kind in ((here.across_x, "y"), (here.across_y, "x")):
                self.arrived(t, here.level(n), spot)
                if (n < 2) == (kind == "y"):
                    self.start(self.passing, t, here.level(n), spot, kind)
                self.start(self.passing, t, here.level(n), spot, "c")

    def corner(self, t):
        here = self.here
        for n in range(DEPTH):
            self.arrived(t, here.level(n), here.diagonal)
            self.start(self.passing, t, here.level(n), here.diagonal, "c")

    def finish(self, t):
        here = self.here
        for n in range(DEPTH):
            for spot in (here.spot, here.across_x, here.across_y, here.diagonal):
                if n == 0 and spot is here.spot:
                    ref = self.outs[t].at[self.rows(t, here.z, here.spot), :]
                else:
                    ref = self.piece(t, here.level(n), spot, here.other)
                sem = self.core_recv.at[t, self.index(here.level(n), spot)]
                remote(ref, ref, sem, sem, here.sibling).wait_recv()


def place_vectors(gathered, vec_ref, ub_ref, rows_out):
    chips = DEPTH * PLANE
    part = vec_ref.shape[1] // chips
    lane = lax.broadcasted_iota(jnp.int32, (16, LANES), 1)
    blocks = [gathered[c * 16 : (c + 1) * 16, :].astype(F32) for c in range(chips)]
    blocks = [jnp.where(lane < part, block, 0.0) for block in blocks]

    def spots(position):
        return position // LANES, position % LANES

    rows = [jnp.zeros((16, LANES), F32) for _ in range(vec_ref.shape[1] // LANES)]
    for c in range(chips):
        group, shift = spots(c * part)
        turned = pltpu.roll(blocks[c], shift, 1) if shift else blocks[c]
        if shift + part > LANES:
            rows[group] = rows[group] + jnp.where(lane >= shift, turned, 0.0)
            rows[group + 1] = rows[group + 1] + jnp.where(lane < shift, turned, 0.0)
        else:
            rows[group] = rows[group] + turned
    for group, row in enumerate(rows):
        cols = slice(group * LANES, (group + 1) * LANES)
        rows_out[:, cols] = row
        vec_ref[0:6, cols] = row[3:9]
    vec_ref[6:8, :] = jnp.zeros((2, vec_ref.shape[1]), F32)
    wide = [jnp.zeros((16, LANES), F32) for _ in range(ub_ref.shape[1] // LANES)]
    for c in range(chips):
        for r in range(4):
            group, shift = spots((4 * c + r) * part)
            row = jnp.broadcast_to(blocks[c][9 + r : 10 + r], (16, LANES))
            turned = pltpu.roll(row, shift, 1) if shift else row
            if shift + part > LANES:
                wide[group] = wide[group] + jnp.where(lane >= shift, turned, 0.0)
                wide[group + 1] = wide[group + 1] + jnp.where(lane < shift, turned, 0.0)
            else:
                wide[group] = wide[group] + turned
    for group, row in enumerate(wide):
        ub_ref[:, group * LANES : (group + 1) * LANES] = row[0:1]


BETWEEN = {
    1: (("cross", 2), ("column", 3)),
    2: (("corner", 2), ("column", 4)),
    3: (("cross", 3),),
    4: (("finish", 2), ("corner", 3)),
    5: (("cross", 4),),
    6: (("finish", 3),),
}


def gather_attend(
    x_ref, ct_ref, q_ref, k_ref, v_ref, o_ref, u_ref, d_ref, b_ref, cs_ref,
    xs_out, cts_out, qkv_out, o_out, u_out, d_out, b_out,
    a_ref, key_ref, val_ref, sq_ref, sk_ref, mixed_ref, den_ref, s_ref, vec_ref, ub_ref,
    state, xs, bounce, weights, vectors, rows,
    swap_sem, load_sem, own_send, x_send, y_send, c_send, link_recv, core_recv,
):
    here = Place()
    seq, chunk, chunks = pl.program_id(0), pl.program_id(1), pl.num_programs(1)
    step = seq * chunks + chunk
    last = pl.num_programs(0) * chunks - 1
    shards = ((b_ref,), (q_ref, k_ref, v_ref), (o_ref,), (u_ref,), (d_ref,))
    outs = (b_out, qkv_out, o_out, u_out, d_out)
    gather = Gather(
        here, shards, outs, own_send, x_send, y_send, c_send, link_recv, core_recv
    )
    pairs, block = x_ref.shape[0] // 2, x_ref.shape[1]

    def swapping():
        place = pl.ds(pl.multiple_of(here.core * block, block), block)
        mine, theirs = pl.ds(here.core * pairs, pairs), pl.ds(here.other * pairs, pairs)
        keep_x = pltpu.make_async_copy(x_ref.at[mine], xs.at[:, place, :], swap_sem.at[0])
        give_x = remote(
            x_ref.at[theirs], xs.at[:, place, :], swap_sem.at[1], swap_sem.at[2], here.sibling
        )
        fetch = pltpu.make_async_copy(ct_ref.at[mine], bounce, swap_sem.at[3])
        keep_ct = pltpu.make_async_copy(bounce, cts_out.at[:, place, :], swap_sem.at[4])
        give_ct = remote(
            ct_ref.at[theirs], cts_out.at[:, place, :], swap_sem.at[5], swap_sem.at[6], here.sibling
        )
        store = pltpu.make_async_copy(xs, xs_out, swap_sem.at[7])
        return keep_x, give_x, fetch, keep_ct, give_ct, store

    @pl.when(step == 0)
    def _():
        keep_x, give_x, fetch, keep_ct, give_ct, store = swapping()
        keep_x.start()
        fetch.start()
        meet(here)
        for t in range(2):
            gather.begin(t)
            gather.rise(t)
        give_x.start()
        give_ct.start()
        for t in range(2, 5):
            gather.begin(t)
        gather.rise(2)
        gather.column(0)
        gather.column(1)
        gather.rise(3)
        fetch.wait()
        keep_ct.start()
        gather.cross(0)
        gather.cross(1)
        gather.column(2)
        gather.rise(4)
        gather.corner(0)
        gather.corner(1)
        gather.finish(0)
        small = pltpu.make_async_copy(b_out, vectors, load_sem.at[0])
        small.start()
        keep_x.wait()
        give_x.wait()
        store.start()
        gather.finish(1)
        large = pltpu.make_async_copy(qkv_out, weights, load_sem.at[1])
        large.start()
        small.wait()
        place_vectors(vectors[...], vec_ref, ub_ref, rows)
        large.wait()

    for n, stages in BETWEEN.items():

        @pl.when(step == n)
        def _(stages=stages):
            for stage, t in stages:
                getattr(gather, stage)(t)

    @pl.when(chunk == 0)
    def _():
        state[...] = jnp.zeros_like(state)

    x = xs[seq, pl.ds(pl.multiple_of(chunk * CHUNK, CHUNK), CHUNK), :]
    attend(x, weights, rows, cs_ref, a_ref, key_ref, val_ref, sq_ref, sk_ref, mixed_ref, den_ref, s_ref, state)

    @pl.when(step == last)
    def _():
        gather.corner(4)
        gather.finish(4)
        _, _, _, keep_ct, give_ct, store = swapping()
        store.wait()
        keep_ct.wait()
        give_ct.wait()
        gather.drain()


def gather_attend_call(x, ct, q, k, v, o, u, d, b, cs):
    chips = DEPTH * PLANE
    anywhere = pl.BlockSpec(memory_space=pl.ANY)
    shape = lambda rows, cols: jax.ShapeDtypeStruct((rows, cols), BF16)
    seqs, length, width = x.shape[0] // 2, x.shape[1] * 2, x.shape[2]
    swapped = jax.ShapeDtypeStruct((seqs, length, width), BF16)
    chunks, total = length // CHUNK, seqs * length
    row = lambda n: pl.BlockSpec((CHUNK, n), lambda s, c: (s * chunks + c, 0))
    keep = lambda *shape: pl.BlockSpec(shape, lambda s, c: (0,) * len(shape))
    wide, count, sem = HEADS * LANES, 5, pltpu.SemaphoreType.DMA
    return pl.pallas_call(
        gather_attend,
        grid=(seqs, chunks),
        in_specs=[anywhere] * 9 + [row(LANES)],
        out_specs=[anywhere] * 7
        + [row(wide), row(wide)]
        + [row(width)] * 5
        + [
            pl.BlockSpec((None, HEADS, LANES, LANES), lambda s, c: (s * chunks + c, 0, 0, 0)),
            keep(8, width),
            keep(1, u.shape[1]),
        ],
        out_shape=[
            swapped,
            swapped,
            shape(q.shape[0] * chips, 3 * q.shape[1]),
            shape(o.shape[0] * chips, o.shape[1]),
            shape(u.shape[0] * chips, u.shape[1]),
            shape(d.shape[0] * chips, d.shape[1]),
            shape(b.shape[0] * chips, b.shape[1]),
            shape(total, wide),
            shape(total, wide),
            shape(total, width),
            shape(total, width),
            shape(total, width),
            shape(total, width),
            jax.ShapeDtypeStruct((total, width), F32),
            jax.ShapeDtypeStruct((seqs * chunks, HEADS, LANES, LANES), BF16),
            jax.ShapeDtypeStruct((8, width), F32),
            jax.ShapeDtypeStruct((1, u.shape[1]), F32),
        ],
        scratch_shapes=[
            pltpu.VMEM((HEADS, LANES, LANES), F32),
            pltpu.VMEM((seqs, length, width), BF16),
            pltpu.VMEM((seqs, x.shape[1], width), BF16),
            pltpu.VMEM((q.shape[0] * chips, 3 * q.shape[1]), BF16),
            pltpu.VMEM((b.shape[0] * chips, b.shape[1]), BF16),
            pltpu.VMEM((16, width), F32),
            sem((8,)),
            sem((2,)),
            sem((count, 6, 3)),
            sem((count, chips)),
            sem((count, chips)),
            sem((count, chips)),
            sem((count, chips)),
            sem((count, chips)),
        ],
        compiler_params=pltpu.CompilerParams(
            collective_id=0,
            has_side_effects=True,
            vmem_limit_bytes=VMEM_LIMIT,
            dimension_semantics=("arbitrary", "arbitrary"),
        ),
        name="gather_attend",
    )(x, ct, q, k, v, o, u, d, b, cs)


class Reduce:
    def __init__(self, here, full, got, corner_x, corner_y, side_x, side_y, column, final, outs, sems):
        self.here, self.outs = here, outs
        self.full, self.got = full, got
        self.corner_x, self.corner_y = corner_x, corner_y
        self.side_x, self.side_y = side_x, side_y
        self.levels, self.final = column, final
        self.core_send, self.core_recv, self.send_sem, self.recv_sem, self.z_send, self.z_recv, self.last_sem = sems
        self.started = []

    def cut(self, t):
        core, (rows, cols) = self.here.core, self.final[t].shape
        if t == 0:
            return pl.ds(pl.multiple_of(core * rows, rows), rows), slice(None)
        return self.window(t, core)

    def window(self, t, core):
        rows, cols = self.final[t].shape
        if t in (UP_A, UP_B):
            start = (2 * core + (t - UP_A)) * cols
            return slice(None), pl.ds(pl.multiple_of(start, cols), cols)
        place = pl.ds(pl.multiple_of(core * cols, cols), cols)
        if t in (DOWN_A, DOWN_B):
            return slice((t - DOWN_A) * rows, (t - DOWN_A + 1) * rows), place
        return slice(None), place

    def part(self, t, core):
        if t == 0:
            return self.full[t].at[core]
        rows, cols = self.window(t, core)
        return self.full[t].at[:, :, rows, cols]

    def mine(self, t):
        return self.part(t, self.here.core)

    def giving(self, t, n):
        source, target = self.part(t, self.here.other), self.got[t]
        if t in (DOWN_A, DOWN_B):
            source, target = source.at[n], target.at[n]
        return remote(
            source, target, self.core_send.at[t, n], self.core_recv.at[t, n], self.here.sibling
        )

    def gifts(self, t):
        return DEPTH if t in (DOWN_A, DOWN_B) else 1

    def pushing(self, t, slot):
        here, own = self.here, self.mine(t)
        source, target, peer = (
            (own.at[0:2, here.diagonal], self.corner_x[t], here.x_peer),
            (own.at[2:4, here.diagonal], self.corner_y[t], here.y_peer),
            (own.at[:, here.across_x], self.side_x[t], here.x_peer),
            (own.at[:, here.across_y], self.side_y[t], here.y_peer),
        )[slot]
        return remote(source, target, self.send_sem.at[t, slot], self.recv_sem.at[t, slot], peer)

    def sinking(self, t, n):
        here = self.here
        return remote(
            self.mine(t).at[here.level(n), here.spot],
            self.levels[t].at[n],
            self.z_send.at[t, n],
            self.z_recv.at[t, n],
            here.z_peer(n),
        )

    def ending(self, t):
        here = self.here
        rows, cols = self.cut(t)
        place = self.outs[t].at[rows, cols]
        keep = pltpu.make_async_copy(self.final[t], place, self.last_sem.at[t, 0])
        give = remote(
            self.final[t], place, self.last_sem.at[t, 1], self.last_sem.at[t, 2], here.sibling
        )
        return keep, give

    def start(self, make, *args):
        make(*args).start()
        self.started.append((make, args))

    def add(self, t, spot, first, count, parts):
        own = self.mine(t)

        def one(z, _):
            total = own[z, spot]
            for part in parts:
                total = total + part(z)
            own[z, spot] = total
            return 0

        lax.fori_loop(first, first + count, one, 0)

    def first(self, t):
        spot, got = self.here.diagonal, self.got[t]
        for n in range(self.gifts(t)):
            self.giving(t, n).wait_recv()
        self.add(t, spot, 0, DEPTH, [lambda z: got[z, spot]])
        self.start(self.pushing, t, 0)
        self.start(self.pushing, t, 1)

    def second(self, t):
        here, got = self.here, self.got[t]
        half = DEPTH // 2
        self.add(t, here.across_x, 0, half, [lambda z: got[z, here.across_x]])
        self.add(t, here.across_y, half, half, [lambda z: got[z, here.across_y]])
        self.pushing(t, 1).wait_recv()
        corner = self.corner_y[t]
        self.add(
            t, here.across_x, half, half, [lambda z: got[z, here.across_x], lambda z: corner[z - half]]
        )
        self.start(self.pushing, t, 2)
        self.pushing(t, 0).wait_recv()
        other = self.corner_x[t]
        self.add(t, here.across_y, 0, half, [lambda z: got[z, here.across_y], lambda z: other[z]])
        self.start(self.pushing, t, 3)

    def third(self, t):
        here, got = self.here, self.got[t]
        side_x, side_y = self.side_x[t], self.side_y[t]
        self.pushing(t, 2).wait_recv()
        self.pushing(t, 3).wait_recv()
        own = self.mine(t)

        def one(z, _):
            total = own[z, here.spot].astype(F32) + got[z, here.spot].astype(F32)
            total = total + (side_x[z].astype(F32) + side_y[z].astype(F32))
            own[z, here.spot] = total.astype(own.dtype)
            return 0

        lax.fori_loop(0, DEPTH, one, 0)
        for n in (2, 1, 3):
            self.start(self.sinking, t, n)

    def fourth(self, t):
        for n in range(1, DEPTH):
            self.sinking(t, n).wait_recv()
        total = self.mine(t)[self.here.z, self.here.spot].astype(F32)
        for n in range(1, DEPTH):
            total = total + self.levels[t][n].astype(F32)
        self.final[t][...] = total
        keep, give = self.ending(t)
        keep.start()
        give.start()

    def run(self, stages):
        for stage, t in stages:
            getattr(self, stage)(t)

    def drain(self):
        for make, args in self.started:
            make(*args).wait_send()
        for t in range(len(self.outs)):
            for n in range(self.gifts(t)):
                self.giving(t, n).wait_send()
            for copy in self.ending(t):
                copy.wait()


def pack_rows(vector_rows, ub_ref, buffer):
    chips = DEPTH * PLANE
    part = vector_rows.shape[1] // chips
    lane = lax.broadcasted_iota(jnp.int32, (16, LANES), 1)

    def cut(read, position):
        group, shift = position // LANES, position % LANES
        block = read(group)
        if not shift:
            return block
        turned = pltpu.roll(block, LANES - shift, 1)
        if shift + part > LANES:
            turned = jnp.where(lane < LANES - shift, turned, pltpu.roll(read(group + 1), LANES - shift, 1))
        return turned

    line = lax.broadcasted_iota(jnp.int32, (16, LANES), 0)

    def vectors(g):
        return vector_rows[:, g * LANES : (g + 1) * LANES]

    def up(g):
        return jnp.broadcast_to(ub_ref[0:1, g * LANES : (g + 1) * LANES], (16, LANES))

    for c in range(chips):
        block = cut(vectors, c * part)
        for r in range(4):
            block = jnp.where(line == 9 + r, cut(up, (4 * c + r) * part), block)
        for half in range(2):
            buffer[half, c // PLANE, c % PLANE] = block[8 * half : 8 * half + 8]


STEP = 256


def product(left, right, width, write):
    def one(n, _):
        offset = pl.multiple_of(n * STEP, STEP)
        write(offset, dot_tn(left[...], right[:, pl.ds(offset, STEP)]).astype(BF16))
        return 0

    lax.fori_loop(0, width // STEP, one, 0)


UP_A, UP_B, DOWN_A, DOWN_B = 5, 6, 7, 8
EARLY = {
    0: (("first", DOWN_A), ("first", DOWN_B)),
    2: (("second", DOWN_A),),
    3: (("second", DOWN_B),),
}
START = (("first", UP_A), ("first", UP_B), ("third", DOWN_A))
DURING = {
    1: (("third", DOWN_B), ("first", 4)),
    2: (("second", UP_A),),
    3: (("fourth", DOWN_A), ("second", UP_B)),
    4: (("fourth", DOWN_B), ("third", UP_A), ("second", 4)),
    5: (("third", UP_B),),
    6: (("third", 4), ("fourth", UP_A)),
    7: (("fourth", UP_B), ("fourth", 4)),
}
WEIGHTS = {1: (("first", 1),), 2: (("first", 2), ("second", 1))}
AFTER = {
    0: (("first", 3),),
    1: (("first", 0),),
    2: (("second", 2),),
    3: (("third", 1),),
    4: (("second", 3),),
    5: (("second", 0),),
    6: (("third", 2),),
    7: (("third", 3), ("fourth", 1), ("third", 0), ("fourth", 2), ("fourth", 3), ("fourth", 0)),
}


def reduce_attend(
    x_hbm, resid_hbm, w_hbm, out_hbm, gvec_ref, gub_ref,
    act_hbm, hidden_hbm, normed_hbm, ffn_hbm, mixed_hbm, branch_hbm,
    a_ref, k_ref, v_ref, e_ref, s_ref, sq_ref, sk_ref, cs_ref,
    out4, grad4, r_b, r_q, r_k, r_v, r_o, r_u, r_d,
    after, back, x_all, weights, gb, rows, bounce, resid_tile, grad_tile, *scratch,
):
    kinds = 9
    names = ("got", "corner_x", "corner_y", "side_x", "side_y", "column", "final")
    full, scratch = scratch[:7], scratch[7:]
    full = (*full[:5], full[5], full[5], full[6], full[6])
    parts = [full] + [scratch[n * kinds : (n + 1) * kinds] for n in range(len(names))]
    swap_sem, big_sem, tile_sem, feed_sem, *sems = scratch[len(names) * kinds :]
    here = Place()
    seq, chunk, chunks = pl.program_id(0), pl.program_id(1), pl.num_programs(1)
    step = seq * chunks + chunk
    last = pl.num_programs(0) * chunks - 1
    reduce = Reduce(here, *parts, (r_b, r_q, r_k, r_v, r_o, r_u, r_u, r_d, r_d), sems)
    pairs, length, width = out_hbm.shape
    block = length // 2
    swaps = []
    for n in range(pairs):
        source = out_hbm.at[n]
        mine = pl.ds(pl.multiple_of(here.core * block, block), block)
        theirs = pl.ds(pl.multiple_of(here.other * block, block), block)
        place = out4.at[here.core * pairs + n]
        swaps.append(
            (
                pltpu.make_async_copy(source.at[mine, :], bounce, swap_sem.at[n, 0]),
                pltpu.make_async_copy(bounce, place, swap_sem.at[n, 1]),
                remote(source.at[theirs, :], place, swap_sem.at[n, 2], swap_sem.at[n, 3], here.sibling),
            )
        )
    big = [
        pltpu.make_async_copy(source, target, big_sem.at[n])
        for n, (source, target) in enumerate(((x_hbm, x_all), (w_hbm, weights)))
    ]
    levels = act_hbm.shape[1] // width

    def slot(n):
        return back.at[:, pl.ds(pl.multiple_of(n * width, width), width)]

    def block_of(n):
        return pl.ds(pl.multiple_of(n * width, width), width)

    def later(n):
        return (n + 2 * here.other) % levels

    def act_feed(n):
        return pltpu.make_async_copy(act_hbm.at[:, block_of(n)], slot(n % 2), feed_sem.at[n % 2])

    def hidden_feed(n):
        return pltpu.make_async_copy(hidden_hbm.at[:, block_of(later(n))], slot(n % 2), feed_sem.at[n % 2])

    def square(t, left, right):
        def write(offset, value):
            full[t][:, :, :, pl.ds(offset, STEP)] = value.reshape(full[t].shape[:3] + (STEP,))

        product(left, right, width, write)

    @pl.when(step == 0)
    def _():
        gb[...] = jnp.zeros_like(gb)
        ffn_feed = pltpu.make_async_copy(ffn_hbm, slot(2), feed_sem.at[2])
        normed_feed = pltpu.make_async_copy(normed_hbm, x_all, big_sem.at[2])
        mixed_feed = pltpu.make_async_copy(mixed_hbm, slot(2), feed_sem.at[2])
        branch_feed = pltpu.make_async_copy(branch_hbm, slot(0), feed_sem.at[0])
        ffn_feed.start()
        act_feed(0).start()
        act_feed(1).start()
        normed_feed.start()
        meet(here)
        swaps[0][0].start()
        for _, _, send in swaps:
            send.start()
        ffn_feed.wait()

        def down_level(n, _):
            act_feed(n).wait()

            def write(offset, value):
                full[DOWN_A][n, :, :, pl.ds(offset, STEP)] = value.reshape(
                    full[DOWN_A].shape[1:3] + (STEP,)
                )

            product(slot(n % 2), slot(2), width, write)

            @pl.when(n + 2 < levels)
            def _():
                act_feed(n + 2).start()

            @pl.when(n + 2 >= levels)
            def _():
                hidden_feed(n + 2 - levels).start()

            reduce.giving(DOWN_A, n).start()
            reduce.giving(DOWN_B, n).start()
            return 0

        lax.fori_loop(0, levels, down_level, 0)
        mixed_feed.start()
        normed_feed.wait()

        def up_block(n, _):
            for m, stages in EARLY.items():

                @pl.when(n == m)
                def _(stages=stages):
                    reduce.run(stages)

            hidden_feed(n).wait()

            def write(offset, value):
                place = pl.ds(pl.multiple_of(later(n) * width + offset, STEP), STEP)
                full[UP_A][:, :, :, place] = value.reshape(full[UP_A].shape[:3] + (STEP,))

            product(x_all, slot(n % 2), width, write)

            @pl.when(n + 2 < levels)
            def _():
                hidden_feed(n + 2).start()

            @pl.when(n == levels - 2)
            def _():
                branch_feed.start()

            for m in range(2):

                @pl.when(n == m)
                def _(m=m):
                    reduce.giving(UP_A + m, 0).start()

            return 0

        lax.fori_loop(0, levels, up_block, 0)
        mixed_feed.wait()
        branch_feed.wait()
        square(4, slot(2), slot(0))
        reduce.giving(4, 0).start()
        swaps[0][0].wait()
        swaps[0][1].start()
        for copy in big:
            copy.start()
        reduce.run(START)

    for n, stages in DURING.items():

        @pl.when(step == n)
        def _(n=n, stages=stages):
            if n == 1:
                swaps[0][1].wait()
                swaps[1][0].start()
            if n == 2:
                swaps[1][0].wait()
                swaps[1][1].start()
            reduce.run(stages)

    @pl.when(chunk == 0)
    def _():
        after[...] = jnp.zeros_like(after)

    at = pl.multiple_of((seq * chunks + chunks - 1 - chunk) * CHUNK, CHUNK)
    attend_back(
        a_ref, k_ref, v_ref, e_ref, s_ref, sq_ref, sk_ref, cs_ref, after, back.at[pl.ds(at, CHUNK), :], gb
    )

    @pl.when(step == last)
    def _():
        for copy in big:
            copy.wait()
        rows[0:3, :] = jnp.concatenate([gb[:, n * width : (n + 1) * width] for n in range(3)])
        rows[3:9, :] = gvec_ref[0:6, :]
        rows[9:16, :] = jnp.zeros((7, width), F32)
        pack_rows(rows, gub_ref, full[0])
        reduce.giving(0, 0).start()
        tiles = pairs * length // CHUNK
        per_seq = length // CHUNK

        def rows_of(i):
            return pl.ds(pl.multiple_of(i * CHUNK, CHUNK), CHUNK)

        def load(i):
            return pltpu.make_async_copy(
                resid_hbm.at[rows_of(i), :], resid_tile.at[i % 2], tile_sem.at[i % 2, 0]
            )

        load(0).start()
        for n in range(3):
            square(1 + n, x_all, slot(n))
            reduce.giving(1 + n, 0).start()
            reduce.run(WEIGHTS.get(n, ()))

        def writes(i):
            s, c = i // per_seq, i % per_seq
            spot = grad4.at[here.core * pairs + s, pl.ds((c % (per_seq // 2)) * CHUNK, CHUNK), :]
            local = pltpu.make_async_copy(grad_tile.at[i % 2], spot, tile_sem.at[i % 2, 1])
            away = remote(grad_tile.at[i % 2], spot, tile_sem.at[i % 2, 2], swap_sem.at[2 + i, 0], here.sibling)
            return local, away, here.core == c // (per_seq // 2)

        def written(i):
            local, away, stays = writes(i)

            @pl.when(stays)
            def _():
                local.wait()

            @pl.when(jnp.logical_not(stays))
            def _():
                away.wait_send()

        def tile(i, _):
            for n in range(tiles - 1):

                @pl.when(i == n)
                def _():
                    reduce.run(AFTER[n])

            @pl.when(i + 1 < tiles)
            def _():
                load(i + 1).start()

            load(i).wait()

            @pl.when(i >= 2)
            def _():
                written(i - 2)

            grad_tile[i % 2] = resid_tile[i % 2] + dot_nt(back[rows_of(i), :], weights[...])
            local, away, stays = writes(i)

            @pl.when(stays)
            def _():
                local.start()

            @pl.when(jnp.logical_not(stays))
            def _():
                away.start()

            return 0

        lax.fori_loop(0, tiles, tile, 0)
        reduce.run(AFTER[tiles - 1])
        for i in range(tiles - 2, tiles):
            written(i)
        for i in range(tiles):
            _, away, stays = writes(i)

            @pl.when(stays)
            def _(away=away):
                away.wait_recv()

        swaps[1][1].wait()
        for _, _, send in swaps:
            send.wait()
        reduce.drain()


def reduce_attend_call(
    x, resid, w, out, gvec, gub, act, hidden, normed, ffn, mixed, branch, a, k, v, e, s, sq, sk, cs
):
    chips = DEPTH * PLANE
    seqs, length, width = out.shape
    total, chunks, wide = seqs * length, length // CHUNK, HEADS * LANES
    anywhere = pl.BlockSpec(memory_space=pl.ANY)
    place = lambda s, c: s * chunks + chunks - 1 - c
    row = lambda n: pl.BlockSpec((CHUNK, n), lambda s, c: (place(s, c), 0))
    once = lambda a: pl.BlockSpec(
        a.shape, lambda s, c: (0,) * len(a.shape), pipeline_mode=pl.Buffered(1)
    )
    part, tall = width // chips, act.shape[1]
    pieces = [(8, LANES, F32)] + [(part, width // 2, BF16)] * 4
    pieces += [(part, tall // 4, BF16)] * 2 + [(tall // chips // 2, width // 2, BF16)] * 2
    kinds, sem = len(pieces), pltpu.SemaphoreType.DMA
    grid = (DEPTH, PLANE)
    scratch = [pltpu.VMEM((2,) + grid + pieces[0][:2], F32)]
    scratch += [pltpu.VMEM(grid + (part, width), BF16)] * 4
    scratch += [pltpu.VMEM(grid + (part, tall), BF16), pltpu.VMEM(grid + (tall // chips, width), BF16)]
    for lead in (grid, (2,), (2,), (DEPTH,), (DEPTH,), (DEPTH,)):
        scratch += [pltpu.VMEM(lead + p[:2], p[2]) for p in pieces]
    scratch += [pltpu.VMEM(p[:2], F32) for p in pieces]
    scratch += [sem((2 + total // CHUNK, 4)), sem((3,)), sem((2, 3)), sem((3,))]
    scratch += [sem((kinds, 4))] * 6 + [sem((kinds, 3))]
    shard = lambda rows, cols: jax.ShapeDtypeStruct((rows, cols), F32)
    return pl.pallas_call(
        reduce_attend,
        grid=(seqs, chunks),
        in_specs=[anywhere] * 4
        + [once(gvec), once(gub)]
        + [anywhere] * 6
        + [row(wide), row(wide), row(width), row(wide)]
        + [pl.BlockSpec((None, HEADS, LANES, LANES), lambda s, c: (place(s, c), 0, 0, 0))]
        + [row(width), row(width), row(LANES)],
        out_specs=[anywhere] * 9,
        out_shape=[
            jax.ShapeDtypeStruct((seqs * 2, length // 2, width), BF16),
            jax.ShapeDtypeStruct((seqs * 2, length // 2, width), F32),
            shard(16, LANES),
            shard(part, width),
            shard(part, width),
            shard(part, width),
            shard(part, width),
            shard(part, tall),
            shard(tall // chips, width),
        ],
        scratch_shapes=[
            pltpu.VMEM((HEADS, LANES, LANES), F32),
            pltpu.VMEM((total, 3 * width), BF16),
            pltpu.VMEM((total, width), BF16),
            pltpu.VMEM(w.shape, BF16),
            pltpu.VMEM((1, 3 * width), F32),
            pltpu.VMEM((16, width), F32),
            pltpu.VMEM((length // 2, width), BF16),
            pltpu.VMEM((2, CHUNK, width), F32),
            pltpu.VMEM((2, CHUNK, width), F32),
        ]
        + scratch,
        compiler_params=pltpu.CompilerParams(
            collective_id=1,
            has_side_effects=True,
            vmem_limit_bytes=VMEM_LIMIT,
            dimension_semantics=("arbitrary", "arbitrary"),
        ),
        name="reduce_attend",
    )(x, resid, w, out, gvec, gub, act, hidden, normed, ffn, mixed, branch, a, k, v, e, s, sq, sk, cs)


def pack_vectors(vectors, up_bias):
    part = vectors[0].shape[0]
    stacked = jnp.concatenate([jnp.stack(vectors), up_bias.reshape(-1, part)])
    return jnp.pad(stacked, ((0, 16 - stacked.shape[0]), (0, LANES - part)))


def unpack_vectors(gathered, part):
    chips = gathered.shape[0] // 16
    grid = gathered.reshape(chips, 16, LANES)[:, :13, :part].astype(F32)
    rows = jnp.transpose(grid[:, :9], (1, 0, 2)).reshape(9, chips * part)
    up_bias = grid[:, 9:].reshape(1, chips * 4 * part)
    return rows[0:3], jnp.pad(rows[3:9], ((0, 2), (0, 0))), up_bias


def pack_vector_grads(gb, gvec, gub, chips):
    width = gvec.shape[1]
    part = width // chips
    rows = jnp.concatenate([gb.reshape(3, width), gvec[0:6]]).reshape(9, chips, part)
    rows = jnp.transpose(rows, (1, 0, 2))
    grid = jnp.concatenate([rows, gub.reshape(chips, 4, part)], axis=1)
    grid = jnp.pad(grid, ((0, 0), (0, 3), (0, LANES - part)))
    return grid.reshape(chips * 16, LANES)


def local(
    inputs,
    horizon,
    query_weight,
    query_bias,
    key_weight,
    key_bias,
    value_weight,
    value_bias,
    out_weight,
    out_bias,
    first_gain,
    first_shift,
    up_weight,
    up_bias,
    down_weight,
    down_bias,
    second_gain,
    second_shift,
    cotangent,
):
    chips = lax.axis_size("dp")
    core = lax.axis_index("seq")
    part = query_bias.shape[0]
    seqs = inputs.shape[0] // 2
    direct = chips == DEPTH * PLANE
    vectors = pack_vectors(
        (
            query_bias,
            key_bias,
            value_bias,
            out_bias,
            first_gain,
            first_shift,
            down_bias,
            second_gain,
            second_shift,
        ),
        up_bias,
    )
    weights = (query_weight, key_weight, value_weight, out_weight, up_weight, down_weight)
    spans = lax.dynamic_slice_in_dim(horizon, core * seqs, seqs)
    length = 2 * inputs.shape[1]
    chunks = length // CHUNK
    cs = rotation(spans, length)
    flat = lambda a: a.reshape(-1, a.shape[-1])
    if direct:
        x, ct, wqkv, wo, wu, wd, _, *saved, vec, ubias = gather_attend_call(
            inputs, cotangent, *weights, vectors, cs
        )
    else:
        gather = lambda a: lax.all_gather(a, "dp", axis=0, tiled=True)
        x, ct = (lax.all_to_all(a, "seq", 0, 1, tiled=True) for a in (inputs, cotangent))
        wqkv = gather(jnp.concatenate(weights[:3], axis=1))
        wo, wu, wd, gathered = (gather(a) for a in (*weights[3:], vectors))
        bqkv, vec, ubias = unpack_vectors(gathered, part)
        saved = forward_call(flat(x), wqkv, bqkv, cs, chunks)
    a, k, v, sq, sk, mixed, den, s = saved
    fx = flat(x)
    out, resid, e, act, hidden, normed, ffn, branch, gvec, gub = middle_call(
        fx, flat(ct), mixed, den, vec, ubias, wo, wu, wd
    )
    out = out.reshape(x.shape)
    if direct:
        out, grad, gvectors, gq, gk, gv, go, gu, gd = reduce_attend_call(
            fx, resid, wqkv, out, gvec, gub, act, hidden, normed, ffn, mixed, branch,
            a, k, v, e, s, sq, sk, cs,
        )
    else:
        go, gu, gd = dot_tn(mixed, branch), dot_tn(normed, hidden), dot_tn(act, ffn)
        grad, gw, gb = backward_call(fx, a, k, v, e, s, sq, sk, cs, resid, wqkv, chunks)
        gvectors = pack_vector_grads(gb, gvec, gub, chips)
        out, grad = (
            lax.all_to_all(a, "seq", 1, 0, tiled=True) for a in (out, grad.reshape(x.shape))
        )
        total = lambda g: lax.psum(
            lax.psum_scatter(g.astype(F32), "dp", scatter_dimension=0, tiled=True), "seq"
        )
        gw, go, gu, gd, gvectors = (total(g) for g in (gw, go, gu, gd, gvectors))
        gq, gk, gv = jnp.split(gw, 3, axis=1)
    rows = gvectors[:, :part]
    return (
        out,
        grad,
        gq,
        rows[0],
        gk,
        rows[1],
        gv,
        rows[2],
        go,
        rows[3],
        rows[4],
        rows[5],
        gu,
        rows[9:13].reshape(-1),
        gd,
        rows[6],
        rows[7],
        rows[8],
    )


def solution(mesh):
    long, wide, thin = P("dp", "seq", None), P("dp", None), P("dp")
    shards = (wide, thin, wide, thin, wide, thin, wide, thin, thin, thin, wide, thin, wide, thin, thin, thin)
    return jax.shard_map(
        local,
        mesh=mesh,
        in_specs=(long, thin, *shards, long),
        out_specs=(long, long, *shards),
        check_vma=False,
    )
```

```python
import functools
import math

import jax
import jax.numpy as jnp
from jax import lax
from jax.experimental import pallas as pl
from jax.experimental.pallas import tpu as pltpu
from jax.sharding import PartitionSpec as P

HEADS = 12
HEAD = 64
PAIRS = HEADS // 2
LANES = 128
CHUNK = 256
ROWS = 512
PARTS = 2
NORM_EPS = 1e-05
GELU_A = 0.7978845608
GELU_B = 0.044715
VMEM_LIMIT = 60 * 1024 * 1024
F32, BF16 = jnp.float32, jnp.bfloat16


def dot_nn(a, b):
    return lax.dot_general(a, b, (((1,), (0,)), ((), ())), preferred_element_type=F32)


def dot_nt(a, b):
    return lax.dot_general(a, b, (((1,), (1,)), ((), ())), preferred_element_type=F32)


def dot_tn(a, b):
    return lax.dot_general(a, b, (((0,), (0,)), ((), ())), preferred_element_type=F32)


def low_lanes(rows):
    return lax.broadcasted_iota(jnp.int32, (rows, LANES), 1) < HEAD


def swap(values):
    return pltpu.roll(values, HEAD, 1)


def softplus_and_slope(values):
    e = jnp.exp(-jnp.abs(values))
    plus = jnp.maximum(values, 0.0) + jnp.log1p(e)
    slope = jnp.where(values >= 0.0, 1.0, e) / (1.0 + e)
    return plus, slope


def attend_forward(
    x_ref, w_ref, b_ref, cs_ref, a_ref, k_ref, v_ref, sq_ref, sk_ref, mixed_ref, den_ref, s_ref, state
):
    @pl.when(pl.program_id(1) == 0)
    def _():
        state[...] = jnp.zeros_like(state)

    attend(
        x_ref[...],
        w_ref,
        b_ref,
        cs_ref,
        a_ref,
        k_ref,
        v_ref,
        sq_ref,
        sk_ref,
        mixed_ref,
        den_ref,
        s_ref,
        state,
    )


def attend(
    x, w_ref, b_ref, cs_ref, a_ref, k_ref, v_ref, sq_ref, sk_ref, mixed_ref, den_ref, s_ref, state
):
    rows, width = x.shape
    cs = cs_ref[...]
    low = low_lanes(rows)
    causal = lax.broadcasted_iota(jnp.int32, (rows, rows), 0) >= lax.broadcasted_iota(
        jnp.int32, (rows, rows), 1
    )

    for half in range(2):
        slope_ref = (sq_ref, sk_ref)[half]
        feature_ref = (a_ref, k_ref)[half]
        pre = dot_nn(x, w_ref[:, half * width : (half + 1) * width])
        pre = pre + b_ref[half : half + 1, :]
        plus, slope = softplus_and_slope(pre)
        slope_ref[...] = slope.astype(BF16)
        for pair in range(PAIRS):
            both = plus[:, pair * LANES : (pair + 1) * LANES]
            other = swap(both)
            even = jnp.where(low, both, other) * cs
            odd = jnp.where(low, other, both) * cs
            feature_ref[:, (2 * pair) * LANES : (2 * pair + 1) * LANES] = even.astype(BF16)
            feature_ref[:, (2 * pair + 1) * LANES : (2 * pair + 2) * LANES] = odd.astype(BF16)
    values = dot_nn(x, w_ref[:, 2 * width :]) + b_ref[2:3, :]
    v_ref[...] = values.astype(BF16)
    for pair in range(PAIRS):
        both = values[:, pair * LANES : (pair + 1) * LANES]
        results = []
        for odd in range(2):
            head = 2 * pair + odd
            query = a_ref[:, head * LANES : (head + 1) * LANES]
            key = k_ref[:, head * LANES : (head + 1) * LANES]
            wide = (jnp.where(low, 1.0, both) if odd else jnp.where(low, both, 1.0)).astype(BF16)
            scores = jnp.where(causal, dot_nt(query, key), 0.0).astype(BF16)
            before = state[head]
            before_low = before.astype(BF16)
            s_ref[head] = before_low
            results.append(dot_nn(scores, wide) + dot_nn(query, before_low))
            state[head] = before + dot_tn(key, wide)
        numer = jnp.where(low, results[0], results[1])
        denom = swap(jnp.where(low, results[1], results[0]))
        mixed_ref[:, pair * LANES : (pair + 1) * LANES] = (numer / denom).astype(BF16)
        den_ref[:, pair * LANES : (pair + 1) * LANES] = denom


def forward_call(x, w, b, cs, chunks):
    total, width = x.shape
    seqs = total // (chunks * CHUNK)
    row = lambda n: pl.BlockSpec((CHUNK, n), lambda s, c: (s * chunks + c, 0))
    once = lambda shape: pl.BlockSpec(
        shape, lambda s, c: (0,) * len(shape), pipeline_mode=pl.Buffered(1)
    )
    wide = HEADS * LANES
    return pl.pallas_call(
        attend_forward,
        grid=(seqs, chunks),
        in_specs=[row(width), once(w.shape), once(b.shape), row(LANES)],
        out_specs=[
            row(wide),
            row(wide),
            row(width),
            row(width),
            row(width),
            row(width),
            row(width),
            pl.BlockSpec((None, HEADS, LANES, LANES), lambda s, c: (s * chunks + c, 0, 0, 0)),
        ],
        out_shape=[
            jax.ShapeDtypeStruct((total, wide), BF16),
            jax.ShapeDtypeStruct((total, wide), BF16),
            jax.ShapeDtypeStruct((total, width), BF16),
            jax.ShapeDtypeStruct((total, width), BF16),
            jax.ShapeDtypeStruct((total, width), BF16),
            jax.ShapeDtypeStruct((total, width), BF16),
            jax.ShapeDtypeStruct((total, width), F32),
            jax.ShapeDtypeStruct((seqs * chunks, HEADS, LANES, LANES), BF16),
        ],
        scratch_shapes=[pltpu.VMEM((HEADS, LANES, LANES), F32)],
        compiler_params=pltpu.CompilerParams(
            dimension_semantics=("arbitrary", "arbitrary"), vmem_limit_bytes=VMEM_LIMIT
        ),
        name="attend_forward",
    )(x, w, b, cs)


def row_mean(values):
    return jnp.mean(values, axis=-1, keepdims=True)


def norm_parts(values):
    center = values - row_mean(values)
    scale = lax.rsqrt(row_mean(center * center) + NORM_EPS)
    return center * scale, scale


def norm_back(grad, gain, unit, scale):
    scaled = grad * gain
    return (scaled - row_mean(scaled) - unit * row_mean(scaled * unit)) * scale


def add_rows(values):
    return jnp.sum(values, axis=0, keepdims=True)


def middle(
    tiles,
    x_ref,
    ct_ref,
    mixed_ref,
    den_ref,
    vec_ref,
    ubias_ref,
    wo_ref,
    wu_ref,
    wd_ref,
    out_ref,
    resid_ref,
    e_ref,
    act,
    hidden_ref,
    normed_ref,
    ffn_ref,
    branch_ref,
    gvec_ref,
    gub_ref,
    slope,
):
    step = pl.program_id(0)
    rows, width = x_ref.shape
    hidden_width = wu_ref.shape[1]
    tile = hidden_width // tiles

    @pl.when(step == 0)
    def _():
        gvec_ref[...] = jnp.zeros_like(gvec_ref)
        gub_ref[...] = jnp.zeros_like(gub_ref)

    out_bias, gain1, shift1 = vec_ref[0:1], vec_ref[1:2], vec_ref[2:3]
    down_bias, gain2, shift2 = vec_ref[3:4], vec_ref[4:5], vec_ref[5:6]
    depth = rows // PARTS
    groups = [slice(n * depth, (n + 1) * depth) for n in range(PARTS)]
    low = low_lanes(depth)
    even_lane = lax.broadcasted_iota(jnp.int32, (depth, LANES), 1) % 2 == 0
    same_head = (
        lax.broadcasted_iota(jnp.int32, (2 * LANES, 2 * LANES), 0) // HEAD
        == lax.broadcasted_iota(jnp.int32, (2 * LANES, 2 * LANES), 1) // HEAD
    ).astype(F32).astype(BF16)

    def mix(part):
        mixed = mixed_ref[part, :]
        resid = x_ref[part, :].astype(F32) + (dot_nn(mixed, wo_ref[...]) + out_bias)
        unit1, scale1 = norm_parts(resid)
        normed = unit1 * gain1 + shift1
        normed_low = normed.astype(BF16)
        normed_ref[part, :] = normed_low
        return unit1, scale1, normed, normed_low

    def feed(part, state):
        unit1, scale1, normed, normed_low = state
        ffn = jnp.zeros((depth, width), F32)
        for t in range(tiles):
            cols = slice(t * tile, (t + 1) * tile)
            hidden = dot_nn(normed_low, wu_ref[:, cols]) + ubias_ref[:, cols]
            square = hidden * hidden
            inner = hidden * (GELU_A + (GELU_A * GELU_B) * square)
            tanh = jnp.tanh(inner)
            half = 0.5 + 0.5 * tanh
            active = (hidden * half).astype(BF16)
            curve = half + (0.5 * hidden) * (1.0 - tanh * tanh) * (
                GELU_A + (3.0 * GELU_A * GELU_B) * square
            )
            act[part, cols] = active
            slope[part, cols] = curve.astype(BF16)
            ffn = ffn + dot_nn(active, wd_ref[cols, :])
        unit2, scale2 = norm_parts(normed + (ffn + down_bias))
        out_ref[part, :] = (unit2 * gain2 + shift2).astype(BF16)
        grad = ct_ref[part, :].astype(F32)
        back_final = norm_back(grad, gain2, unit2, scale2)
        back_ffn = back_final.astype(BF16)
        ffn_ref[part, :] = back_ffn
        gvec_ref[4:5] += add_rows(grad * unit2)
        gvec_ref[5:6] += add_rows(grad)
        gvec_ref[3:4] += add_rows(back_ffn.astype(F32))
        return unit1, scale1, back_final, back_ffn

    def feed_back(part, state):
        unit1, scale1, back_normed, back_ffn = state
        for t in range(tiles):
            cols = slice(t * tile, (t + 1) * tile)
            back_active = dot_nt(back_ffn, wd_ref[cols, :])
            back_hidden = (back_active * slope[part, cols].astype(F32)).astype(BF16)
            hidden_ref[part, cols] = back_hidden
            gub_ref[:, cols] += add_rows(back_hidden.astype(F32))
            back_normed = back_normed + dot_nt(back_hidden, wu_ref[:, cols])
        gvec_ref[1:2] += add_rows(back_normed * unit1)
        gvec_ref[2:3] += add_rows(back_normed)
        back_resid = norm_back(back_normed, gain1, unit1, scale1)
        resid_ref[part, :] = back_resid
        back_branch = back_resid.astype(BF16)
        branch_ref[part, :] = back_branch
        gvec_ref[0:1] += add_rows(back_branch.astype(F32))
        return back_branch

    def mix_back(part, back_branch):
        back_mixed = dot_nt(back_branch, wo_ref[...])
        back_numer = back_mixed / den_ref[part, :]
        product = back_numer * mixed_ref[part, :].astype(F32)
        high = product.astype(BF16)
        rest = (product - high.astype(F32)).astype(BF16)
        for block in range(width // (2 * LANES)):
            cols = slice(block * 2 * LANES, (block + 1) * 2 * LANES)
            sums = dot_nn(high[:, cols], same_head) + dot_nn(rest[:, cols], same_head)
            for inside in range(2):
                pair = 2 * block + inside
                back = -sums[:, inside * LANES : (inside + 1) * LANES]
                back_high = back.astype(BF16).astype(F32)
                spread = swap(jnp.where(even_lane, back_high, back - back_high) * (2.0 / HEAD))
                numer = back_numer[:, pair * LANES : (pair + 1) * LANES]
                e_ref[part, (2 * pair) * LANES : (2 * pair + 1) * LANES] = jnp.where(
                    low, numer, spread
                ).astype(BF16)
                e_ref[part, (2 * pair + 1) * LANES : (2 * pair + 2) * LANES] = jnp.where(
                    low, spread, numer
                ).astype(BF16)

    states = [mix(part) for part in groups]
    for stage in (feed, feed_back, mix_back):
        states = [stage(part, state) for part, state in zip(groups, states)]


def middle_call(x, ct, mixed, den, vec, ubias, wo, wu, wd, tiles=4):
    total, width = x.shape
    hidden_width = wu.shape[1]
    row = lambda n: pl.BlockSpec((ROWS, n), lambda i: (i, 0))
    once = lambda shape: pl.BlockSpec(
        shape, lambda i: (0,) * len(shape), pipeline_mode=pl.Buffered(1)
    )
    keep = lambda shape: pl.BlockSpec(shape, lambda i: (0,) * len(shape))
    wide = HEADS * LANES
    shape = lambda n, kind=BF16: jax.ShapeDtypeStruct((total, n), kind)
    return pl.pallas_call(
        functools.partial(middle, tiles),
        grid=(total // ROWS,),
        in_specs=[
            row(width),
            row(width),
            row(width),
            row(width),
            once(vec.shape),
            once(ubias.shape),
            once(wo.shape),
            once(wu.shape),
            once(wd.shape),
        ],
        out_specs=[
            row(width),
            row(width),
            row(wide),
            row(hidden_width),
            row(hidden_width),
            row(width),
            row(width),
            row(width),
            keep((8, width)),
            keep((1, hidden_width)),
        ],
        out_shape=[
            shape(width),
            shape(width, F32),
            shape(wide),
            shape(hidden_width),
            shape(hidden_width),
            shape(width),
            shape(width),
            shape(width),
            jax.ShapeDtypeStruct((8, width), F32),
            jax.ShapeDtypeStruct((1, hidden_width), F32),
        ],
        scratch_shapes=[pltpu.VMEM((ROWS, hidden_width), BF16)],
        compiler_params=pltpu.CompilerParams(
            dimension_semantics=("arbitrary",), vmem_limit_bytes=VMEM_LIMIT
        ),
        name="middle",
    )(x, ct, mixed, den, vec, ubias, wo, wu, wd)


def attend_back(a_ref, k_ref, v_ref, e_ref, s_ref, sq_ref, sk_ref, cs_ref, after, back, gb_ref):
    rows, width = v_ref.shape
    cs = cs_ref[...]
    low = low_lanes(rows)
    i = lax.broadcasted_iota(jnp.int32, (rows, rows), 0)
    j = lax.broadcasted_iota(jnp.int32, (rows, rows), 1)
    causal, anti = i >= j, i <= j
    for pair in range(PAIRS):
        both = v_ref[:, pair * LANES : (pair + 1) * LANES].astype(F32)
        back_q, back_k, back_v = [], [], []
        for odd in range(2):
            head = 2 * pair + odd
            cols = slice(head * LANES, (head + 1) * LANES)
            query, key, e = a_ref[:, cols], k_ref[:, cols], e_ref[:, cols]
            wide = (jnp.where(low, 1.0, both) if odd else jnp.where(low, both, 1.0)).astype(BF16)
            state = s_ref[head]
            later = after[head]
            later_low = later.astype(BF16)
            scores_t = jnp.where(anti, dot_nt(key, query), 0.0).astype(BF16)
            back_s = jnp.where(causal, dot_nt(e, wide), 0.0).astype(BF16)
            back_st = jnp.where(anti, dot_nt(wide, e), 0.0).astype(BF16)
            y = (dot_nn(back_s, key) + dot_nt(e, state)) * cs
            back_q.append(y + swap(y))
            y = (dot_nn(back_st, query) + dot_nt(wide, later_low)) * cs
            back_k.append(y + swap(y))
            back_v.append(dot_nn(scores_t, e) + dot_nn(key, later_low))
            after[head] = later + dot_tn(query, e)
        cols = slice(pair * LANES, (pair + 1) * LANES)
        dq = jnp.where(low, back_q[0], back_q[1]) * sq_ref[:, cols].astype(F32)
        dk = jnp.where(low, back_k[0], back_k[1]) * sk_ref[:, cols].astype(F32)
        dv = jnp.where(low, back_v[0], back_v[1])
        for n, piece in enumerate((dq, dk, dv)):
            piece = piece.astype(BF16)
            cols = slice(n * width + pair * LANES, n * width + (pair + 1) * LANES)
            back[:, cols] = piece
            gb_ref[:, cols] += add_rows(piece.astype(F32))


def attend_backward(
    x_ref,
    a_ref,
    k_ref,
    v_ref,
    e_ref,
    s_ref,
    sq_ref,
    sk_ref,
    cs_ref,
    resid_ref,
    w_ref,
    grad_ref,
    gw_ref,
    gb_ref,
    after,
    back,
    gw,
):
    rows, width = x_ref.shape

    @pl.when((pl.program_id(0) == 0) & (pl.program_id(1) == 0))
    def _():
        gw[...] = jnp.zeros_like(gw)
        gb_ref[...] = jnp.zeros_like(gb_ref)

    @pl.when(pl.program_id(1) == 0)
    def _():
        after[...] = jnp.zeros_like(after)

    attend_back(a_ref, k_ref, v_ref, e_ref, s_ref, sq_ref, sk_ref, cs_ref, after, back, gb_ref)
    x = x_ref[...]
    total = resid_ref[...]
    for n in range(3):
        cols = slice(n * width, (n + 1) * width)
        piece = back[:, cols]
        gw[:, cols] += dot_tn(x, piece)
        total = total + dot_nt(piece, w_ref[:, cols])
    grad_ref[...] = total

    @pl.when((pl.program_id(0) == pl.num_programs(0) - 1) & (pl.program_id(1) == pl.num_programs(1) - 1))
    def _():
        gw_ref[...] = gw[...].astype(BF16)


def backward_call(x, a, k, v, e, s, sq, sk, cs, resid, w, chunks):
    total, width = x.shape
    seqs = total // (chunks * CHUNK)
    place = lambda s, c: s * chunks + chunks - 1 - c
    row = lambda n: pl.BlockSpec((CHUNK, n), lambda s, c: (place(s, c), 0))
    once = lambda shape: pl.BlockSpec(
        shape, lambda s, c: (0,) * len(shape), pipeline_mode=pl.Buffered(1)
    )
    keep = lambda shape: pl.BlockSpec(shape, lambda s, c: (0,) * len(shape))
    wide = HEADS * LANES
    return pl.pallas_call(
        attend_backward,
        grid=(seqs, chunks),
        in_specs=[
            row(width),
            row(wide),
            row(wide),
            row(width),
            row(wide),
            pl.BlockSpec((None, HEADS, LANES, LANES), lambda s, c: (place(s, c), 0, 0, 0)),
            row(width),
            row(width),
            row(LANES),
            row(width),
            once(w.shape),
        ],
        out_specs=[row(width), keep(w.shape), keep((1, w.shape[1]))],
        out_shape=[
            jax.ShapeDtypeStruct((total, width), F32),
            jax.ShapeDtypeStruct(w.shape, BF16),
            jax.ShapeDtypeStruct((1, w.shape[1]), F32),
        ],
        scratch_shapes=[
            pltpu.VMEM((HEADS, LANES, LANES), F32),
            pltpu.VMEM((CHUNK, w.shape[1]), BF16),
            pltpu.VMEM(w.shape, F32),
        ],
        compiler_params=pltpu.CompilerParams(
            dimension_semantics=("arbitrary", "arbitrary"), vmem_limit_bytes=VMEM_LIMIT
        ),
        name="attend_backward",
    )(x, a, k, v, e, s, sq, sk, cs, resid, w)


def rotation(horizon, length):
    seqs = horizon.shape[0]
    position = jnp.arange(length, dtype=F32)
    angles = 0.5 * math.pi * position[None, :] / horizon.astype(F32)[:, None]
    return jnp.concatenate(
        [
            jnp.broadcast_to(jnp.cos(angles)[..., None], (seqs, length, HEAD)),
            jnp.broadcast_to(jnp.sin(angles)[..., None], (seqs, length, HEAD)),
        ],
        axis=-1,
    ).reshape(seqs * length, LANES)


DEPTH, PLANE = 4, 4


class Place:
    def __init__(self):
        self.dp, self.core = lax.axis_index("dp"), lax.axis_index("seq")
        self.z, self.spot = self.dp // PLANE, self.dp % PLANE
        self.other = 1 - self.core
        self.levels = [(self.z + step) % DEPTH for step in range(DEPTH)]
        self.across_x = self.spot + 1 - 2 * (self.spot % 2)
        self.across_y = (self.spot + 2) % PLANE
        self.diagonal = PLANE - 1 - self.spot
        self.x_peer = (self.z * PLANE + self.across_x, self.core)
        self.y_peer = (self.z * PLANE + self.across_y, self.core)
        self.sibling = (self.dp, self.other)

    def level(self, step):
        return self.levels[step]

    def z_peer(self, step):
        return (self.level(step) * PLANE + self.spot, self.core)


def remote(source, target, send, recv, peer):
    copy = pltpu.make_async_remote_copy(
        src_ref=source,
        dst_ref=target,
        send_sem=send,
        recv_sem=recv,
        device_id=peer,
        device_id_type=pl.DeviceIdType.MESH,
    )
    return copy


def meet(here):
    barrier = pltpu.get_barrier_semaphore()
    peers = [here.x_peer, here.y_peer, here.sibling] + [here.z_peer(n) for n in range(1, DEPTH)]
    for peer in peers:
        pl.semaphore_signal(barrier, inc=1, device_id=peer, device_id_type=pl.DeviceIdType.MESH)
    pl.semaphore_wait(barrier, len(peers))


class Gather:
    def __init__(self, here, kinds, own_send, x_send, y_send, c_send, link_recv, core_recv):
        self.here, self.kinds = here, kinds
        self.own_send, self.link_recv, self.core_recv = own_send, link_recv, core_recv
        self.sems = {"x": x_send, "y": y_send, "c": c_send}
        self.started = []

    def index(self, level, spot):
        return level * PLANE + spot

    def whole(self, t, level, spot):
        out, _, height, top, rows, left, cols = self.kinds[t]
        start = pl.multiple_of(self.index(level, spot) * height + top, rows)
        return out.at[pl.ds(start, rows), left : left + cols]

    def piece(self, t, level, spot, core):
        out, _, height, top, rows, left, cols = self.kinds[t]
        half = rows // 2
        start = pl.multiple_of(self.index(level, spot) * height + top + core * half, half)
        return out.at[pl.ds(start, half), left : left + cols]

    def passing(self, t, level, spot, kind):
        here, at = self.here, self.index(level, spot)
        peer = {"x": here.x_peer, "y": here.y_peer, "c": here.sibling}[kind]
        arrive = self.core_recv if kind == "c" else self.link_recv
        ref = self.piece(t, level, spot, here.core)
        return [remote(ref, ref, self.sems[kind].at[t, at], arrive.at[t, at], peer)]

    def spreading(self, t, slot):
        here = self.here
        _, shards, _, top, rows, left, cols = self.kinds[t]
        peer = (here.x_peer, here.y_peer, here.sibling)[slot] if slot < 3 else here.z_peer(slot - 2)
        mine = self.index(here.z, here.spot)
        if slot == 2:
            place, take = self.whole(t, here.z, here.spot), pl.ds(top, rows)
            arrive = self.core_recv.at[t, mine]
        else:
            place, half = self.piece(t, here.z, here.spot, here.core), rows // 2
            take = pl.ds(pl.multiple_of(top + here.core * half, half), half)
            arrive = self.link_recv.at[t, mine]
        copies = []
        for n, ref in enumerate(shards):
            target = place
            if len(shards) > 1:
                target = place.at[:, n * ref.shape[1] : (n + 1) * ref.shape[1]]
                source = ref.at[take, :]
            else:
                source = ref.at[take, left : left + cols]
            copies.append(remote(source, target, self.own_send.at[t, slot, n], arrive, peer))
        return copies

    def start(self, make, *args):
        for copy in make(*args):
            copy.start()
        self.started.append((make, args))

    def drain(self):
        for make, args in self.started:
            for copy in make(*args):
                copy.wait_send()

    def run(self, stages):
        for stage, t in stages:
            getattr(self, stage)(t)

    def arrived(self, t, level, spot):
        ref = self.piece(t, level, spot, self.here.core)
        sem = self.link_recv.at[t, self.index(level, spot)]
        remote(ref, ref, sem, sem, self.here.x_peer).wait_recv()

    def begin(self, t):
        for slot in range(3):
            self.start(self.spreading, t, slot)

    def rise(self, t):
        for n in (1, 3, 2):
            self.start(self.spreading, t, 2 + n)

    def column(self, t):
        here = self.here
        for n in (1, 3, 2):
            self.arrived(t, here.level(n), here.spot)
            for kind in "xyc":
                self.start(self.passing, t, here.level(n), here.spot, kind)

    def cross(self, t):
        here = self.here
        for n in (0, 1, 3, 2):
            for spot, kind in ((here.across_x, "y"), (here.across_y, "x")):
                self.arrived(t, here.level(n), spot)
                if (n < 2) == (kind == "y"):
                    self.start(self.passing, t, here.level(n), spot, kind)
                self.start(self.passing, t, here.level(n), spot, "c")

    def corner(self, t):
        here = self.here
        for n in range(DEPTH):
            self.arrived(t, here.level(n), here.diagonal)
            self.start(self.passing, t, here.level(n), here.diagonal, "c")

    def finish(self, t):
        here = self.here
        for n in range(DEPTH):
            for spot in (here.spot, here.across_x, here.across_y, here.diagonal):
                if n == 0 and spot is here.spot:
                    ref = self.whole(t, here.z, here.spot)
                else:
                    ref = self.piece(t, here.level(n), spot, here.other)
                sem = self.core_recv.at[t, self.index(here.level(n), spot)]
                remote(ref, ref, sem, sem, here.sibling).wait_recv()


def place_vectors(gathered, vec_ref, ub_ref, rows_out):
    chips = DEPTH * PLANE
    part = vec_ref.shape[1] // chips
    lane = lax.broadcasted_iota(jnp.int32, (16, LANES), 1)
    blocks = [gathered[c * 16 : (c + 1) * 16, :].astype(F32) for c in range(chips)]
    blocks = [jnp.where(lane < part, block, 0.0) for block in blocks]

    def spots(position):
        return position // LANES, position % LANES

    rows = [jnp.zeros((16, LANES), F32) for _ in range(vec_ref.shape[1] // LANES)]
    for c in range(chips):
        group, shift = spots(c * part)
        turned = pltpu.roll(blocks[c], shift, 1) if shift else blocks[c]
        if shift + part > LANES:
            rows[group] = rows[group] + jnp.where(lane >= shift, turned, 0.0)
            rows[group + 1] = rows[group + 1] + jnp.where(lane < shift, turned, 0.0)
        else:
            rows[group] = rows[group] + turned
    for group, row in enumerate(rows):
        cols = slice(group * LANES, (group + 1) * LANES)
        rows_out[:, cols] = row
        vec_ref[0:6, cols] = row[3:9]
    vec_ref[6:8, :] = jnp.zeros((2, vec_ref.shape[1]), F32)
    wide = [jnp.zeros((16, LANES), F32) for _ in range(ub_ref.shape[1] // LANES)]
    for c in range(chips):
        for r in range(4):
            group, shift = spots((4 * c + r) * part)
            row = jnp.broadcast_to(blocks[c][9 + r : 10 + r], (16, LANES))
            turned = pltpu.roll(row, shift, 1) if shift else row
            if shift + part > LANES:
                wide[group] = wide[group] + jnp.where(lane >= shift, turned, 0.0)
                wide[group + 1] = wide[group + 1] + jnp.where(lane < shift, turned, 0.0)
            else:
                wide[group] = wide[group] + turned
    for group, row in enumerate(wide):
        ub_ref[:, group * LANES : (group + 1) * LANES] = row[0:1]


U_A, U_B, D_A, D_B = 3, 4, 5, 6
OPENING = (
    ("begin", 0), ("rise", 0), ("begin", 1), ("rise", 1),
    ("begin", 2), ("begin", U_A), ("begin", U_B), ("begin", D_A), ("begin", D_B),
    ("rise", 2), ("rise", U_A),
    ("column", 0), ("column", 1), ("rise", U_B), ("cross", 0), ("column", 2), ("rise", D_A),
    ("cross", 1), ("column", U_A), ("rise", D_B), ("corner", 0), ("corner", 1), ("finish", 0),
)
BETWEEN = {
    1: (("cross", 2), ("column", U_B)),
    2: (("cross", U_A), ("corner", 2), ("column", D_A)),
    3: (("cross", U_B), ("corner", U_A)),
    4: (("column", D_B), ("finish", 2)),
    5: (("cross", D_A), ("corner", U_B), ("finish", U_A)),
    6: (("finish", U_B),),
    7: (("cross", D_B), ("corner", D_A)),
}
SWAPPED = 13
CLOSING = (("corner", D_B), ("finish", D_A), ("finish", D_B))


def gather_attend(
    x_ref, ct_ref, q_ref, k_ref, v_ref, o_ref, u_ref, d_ref, b_ref, cs_ref,
    xs_out, cts_out, qkv_out, o_out, u_out, d_out, b_out,
    a_ref, key_ref, val_ref, sq_ref, sk_ref, mixed_ref, den_ref, s_ref, vec_ref, ub_ref,
    state, xs, bounce, weights, vectors, rows,
    swap_sem, load_sem, own_send, x_send, y_send, c_send, link_recv, core_recv,
):
    here = Place()
    seq, chunk, chunks = pl.program_id(0), pl.program_id(1), pl.num_programs(1)
    step = seq * chunks + chunk
    last = pl.num_programs(0) * chunks - 1
    tall, wide, width = d_ref.shape[0] // 2, u_ref.shape[1] // 2, q_ref.shape[1]
    kinds = [
        (out, shards, shards[0].shape[0], 0, shards[0].shape[0], 0, out.shape[1])
        for out, shards in ((b_out, (b_ref,)), (qkv_out, (q_ref, k_ref, v_ref)), (o_out, (o_ref,)))
    ]
    kinds += [(u_out, (u_ref,), u_ref.shape[0], 0, u_ref.shape[0], n * wide, wide) for n in range(2)]
    kinds += [(d_out, (d_ref,), 2 * tall, n * tall, tall, 0, width) for n in range(2)]
    gather = Gather(here, kinds, own_send, x_send, y_send, c_send, link_recv, core_recv)
    pairs, block = x_ref.shape[0] // 2, x_ref.shape[1]

    def swapping():
        place = pl.ds(pl.multiple_of(here.core * block, block), block)
        mine, theirs = pl.ds(here.core * pairs, pairs), pl.ds(here.other * pairs, pairs)
        keep_x = pltpu.make_async_copy(x_ref.at[mine], xs.at[:, place, :], swap_sem.at[0])
        give_x = remote(
            x_ref.at[theirs], xs.at[:, place, :], swap_sem.at[1], swap_sem.at[2], here.sibling
        )
        fetch = pltpu.make_async_copy(ct_ref.at[mine], bounce, swap_sem.at[3])
        keep_ct = pltpu.make_async_copy(bounce, cts_out.at[:, place, :], swap_sem.at[4])
        give_ct = remote(
            ct_ref.at[theirs], cts_out.at[:, place, :], swap_sem.at[5], swap_sem.at[6], here.sibling
        )
        store = pltpu.make_async_copy(xs, xs_out, swap_sem.at[7])
        return keep_x, give_x, fetch, keep_ct, give_ct, store

    @pl.when(step == 0)
    def _():
        keep_x, give_x, fetch, keep_ct, give_ct, store = swapping()
        keep_x.start()
        fetch.start()
        meet(here)
        gather.run(OPENING[:4])
        give_x.start()
        give_ct.start()
        gather.run(OPENING[4:SWAPPED])
        fetch.wait()
        keep_ct.start()
        gather.run(OPENING[SWAPPED:])
        small = pltpu.make_async_copy(b_out, vectors, load_sem.at[0])
        small.start()
        keep_x.wait()
        give_x.wait()
        store.start()
        gather.finish(1)
        large = pltpu.make_async_copy(qkv_out, weights, load_sem.at[1])
        large.start()
        small.wait()
        place_vectors(vectors[...], vec_ref, ub_ref, rows)
        large.wait()

    for n, stages in BETWEEN.items():

        @pl.when(step == n)
        def _(stages=stages):
            gather.run(stages)

    @pl.when(chunk == 0)
    def _():
        state[...] = jnp.zeros_like(state)

    x = xs[seq, pl.ds(pl.multiple_of(chunk * CHUNK, CHUNK), CHUNK), :]
    attend(x, weights, rows, cs_ref, a_ref, key_ref, val_ref, sq_ref, sk_ref, mixed_ref, den_ref, s_ref, state)

    @pl.when(step == last)
    def _():
        gather.run(CLOSING)
        _, _, _, keep_ct, give_ct, store = swapping()
        store.wait()
        keep_ct.wait()
        give_ct.wait()
        gather.drain()


def gather_attend_call(x, ct, q, k, v, o, u, d, b, cs):
    chips = DEPTH * PLANE
    anywhere = pl.BlockSpec(memory_space=pl.ANY)
    shape = lambda rows, cols: jax.ShapeDtypeStruct((rows, cols), BF16)
    seqs, length, width = x.shape[0] // 2, x.shape[1] * 2, x.shape[2]
    swapped = jax.ShapeDtypeStruct((seqs, length, width), BF16)
    chunks, total = length // CHUNK, seqs * length
    row = lambda n: pl.BlockSpec((CHUNK, n), lambda s, c: (s * chunks + c, 0))
    keep = lambda *shape: pl.BlockSpec(shape, lambda s, c: (0,) * len(shape))
    wide, count, sem = HEADS * LANES, 7, pltpu.SemaphoreType.DMA
    return pl.pallas_call(
        gather_attend,
        grid=(seqs, chunks),
        in_specs=[anywhere] * 9 + [row(LANES)],
        out_specs=[anywhere] * 7
        + [row(wide), row(wide)]
        + [row(width)] * 5
        + [
            pl.BlockSpec((None, HEADS, LANES, LANES), lambda s, c: (s * chunks + c, 0, 0, 0)),
            keep(8, width),
            keep(1, u.shape[1]),
        ],
        out_shape=[
            swapped,
            swapped,
            shape(q.shape[0] * chips, 3 * q.shape[1]),
            shape(o.shape[0] * chips, o.shape[1]),
            shape(u.shape[0] * chips, u.shape[1]),
            shape(d.shape[0] * chips, d.shape[1]),
            shape(b.shape[0] * chips, b.shape[1]),
            shape(total, wide),
            shape(total, wide),
            shape(total, width),
            shape(total, width),
            shape(total, width),
            shape(total, width),
            jax.ShapeDtypeStruct((total, width), F32),
            jax.ShapeDtypeStruct((seqs * chunks, HEADS, LANES, LANES), BF16),
            jax.ShapeDtypeStruct((8, width), F32),
            jax.ShapeDtypeStruct((1, u.shape[1]), F32),
        ],
        scratch_shapes=[
            pltpu.VMEM((HEADS, LANES, LANES), F32),
            pltpu.VMEM((seqs, length, width), BF16),
            pltpu.VMEM((seqs, x.shape[1], width), BF16),
            pltpu.VMEM((q.shape[0] * chips, 3 * q.shape[1]), BF16),
            pltpu.VMEM((b.shape[0] * chips, b.shape[1]), BF16),
            pltpu.VMEM((16, width), F32),
            sem((8,)),
            sem((2,)),
            sem((count, 6, 3)),
            sem((count, chips)),
            sem((count, chips)),
            sem((count, chips)),
            sem((count, chips)),
            sem((count, chips)),
        ],
        compiler_params=pltpu.CompilerParams(
            collective_id=0,
            has_side_effects=True,
            vmem_limit_bytes=VMEM_LIMIT,
            dimension_semantics=("arbitrary", "arbitrary"),
        ),
        name="gather_attend",
    )(x, ct, q, k, v, o, u, d, b, cs)


class Reduce:
    def __init__(self, here, full, got, corner_x, corner_y, side_x, side_y, column, final, outs, sems):
        self.here, self.outs = here, outs
        self.full, self.got = full, got
        self.corner_x, self.corner_y = corner_x, corner_y
        self.side_x, self.side_y = side_x, side_y
        self.levels, self.final = column, final
        self.core_send, self.core_recv, self.send_sem, self.recv_sem, self.z_send, self.z_recv, self.last_sem = sems
        self.started = []

    def cut(self, t):
        core, (rows, cols) = self.here.core, self.final[t].shape
        if t == 0:
            return pl.ds(pl.multiple_of(core * rows, rows), rows), slice(None)
        return self.window(t, core)

    def window(self, t, core):
        rows, cols = self.final[t].shape
        if t in (UP_A, UP_B):
            start = (2 * core + (t - UP_A)) * cols
            return slice(None), pl.ds(pl.multiple_of(start, cols), cols)
        place = pl.ds(pl.multiple_of(core * cols, cols), cols)
        if t in (DOWN_A, DOWN_B):
            return slice((t - DOWN_A) * rows, (t - DOWN_A + 1) * rows), place
        return slice(None), place

    def part(self, t, core):
        if t == 0:
            return self.full[t].at[core]
        rows, cols = self.window(t, core)
        return self.full[t].at[:, :, rows, cols]

    def mine(self, t):
        return self.part(t, self.here.core)

    def giving(self, t, n):
        source, target = self.part(t, self.here.other), self.got[t]
        if t in (DOWN_A, DOWN_B):
            source, target = source.at[n], target.at[n]
        return remote(
            source, target, self.core_send.at[t, n], self.core_recv.at[t, n], self.here.sibling
        )

    def gifts(self, t):
        return DEPTH if t in (DOWN_A, DOWN_B) else 1

    def pushing(self, t, slot):
        here, own = self.here, self.mine(t)
        source, target, peer = (
            (own.at[0:2, here.diagonal], self.corner_x[t], here.x_peer),
            (own.at[2:4, here.diagonal], self.corner_y[t], here.y_peer),
            (own.at[:, here.across_x], self.side_x[t], here.x_peer),
            (own.at[:, here.across_y], self.side_y[t], here.y_peer),
        )[slot]
        return remote(source, target, self.send_sem.at[t, slot], self.recv_sem.at[t, slot], peer)

    def sinking(self, t, n):
        here = self.here
        return remote(
            self.mine(t).at[here.level(n), here.spot],
            self.levels[t].at[n],
            self.z_send.at[t, n],
            self.z_recv.at[t, n],
            here.z_peer(n),
        )

    def ending(self, t):
        here = self.here
        rows, cols = self.cut(t)
        place = self.outs[t].at[rows, cols]
        keep = pltpu.make_async_copy(self.final[t], place, self.last_sem.at[t, 0])
        give = remote(
            self.final[t], place, self.last_sem.at[t, 1], self.last_sem.at[t, 2], here.sibling
        )
        return keep, give

    def start(self, make, *args):
        make(*args).start()
        self.started.append((make, args))

    def add(self, t, spot, first, count, parts):
        own = self.mine(t)

        def one(z, _):
            total = own[z, spot]
            for part in parts:
                total = total + part(z)
            own[z, spot] = total
            return 0

        lax.fori_loop(first, first + count, one, 0)

    def first(self, t):
        spot, got = self.here.diagonal, self.got[t]
        for n in range(self.gifts(t)):
            self.giving(t, n).wait_recv()
        self.add(t, spot, 0, DEPTH, [lambda z: got[z, spot]])
        self.start(self.pushing, t, 0)
        self.start(self.pushing, t, 1)

    def second(self, t):
        here, got = self.here, self.got[t]
        half = DEPTH // 2
        self.add(t, here.across_x, 0, half, [lambda z: got[z, here.across_x]])
        self.add(t, here.across_y, half, half, [lambda z: got[z, here.across_y]])
        self.pushing(t, 1).wait_recv()
        corner = self.corner_y[t]
        self.add(
            t, here.across_x, half, half, [lambda z: got[z, here.across_x], lambda z: corner[z - half]]
        )
        self.start(self.pushing, t, 2)
        self.pushing(t, 0).wait_recv()
        other = self.corner_x[t]
        self.add(t, here.across_y, 0, half, [lambda z: got[z, here.across_y], lambda z: other[z]])
        self.start(self.pushing, t, 3)

    def third(self, t):
        here, got = self.here, self.got[t]
        side_x, side_y = self.side_x[t], self.side_y[t]
        self.pushing(t, 2).wait_recv()
        self.pushing(t, 3).wait_recv()
        own = self.mine(t)

        def one(z, _):
            total = own[z, here.spot].astype(F32) + got[z, here.spot].astype(F32)
            total = total + (side_x[z].astype(F32) + side_y[z].astype(F32))
            own[z, here.spot] = total.astype(own.dtype)
            return 0

        lax.fori_loop(0, DEPTH, one, 0)
        for n in (2, 1, 3):
            self.start(self.sinking, t, n)

    def fourth(self, t):
        for n in range(1, DEPTH):
            self.sinking(t, n).wait_recv()
        total = self.mine(t)[self.here.z, self.here.spot].astype(F32)
        for n in range(1, DEPTH):
            total = total + self.levels[t][n].astype(F32)
        self.final[t][...] = total
        keep, give = self.ending(t)
        keep.start()
        give.start()

    def run(self, stages):
        for stage, t in stages:
            getattr(self, stage)(t)

    def drain(self):
        for make, args in self.started:
            make(*args).wait_send()
        for t in range(len(self.outs)):
            for n in range(self.gifts(t)):
                self.giving(t, n).wait_send()
            for copy in self.ending(t):
                copy.wait()


def pack_rows(vector_rows, ub_ref, buffer):
    chips = DEPTH * PLANE
    part = vector_rows.shape[1] // chips
    lane = lax.broadcasted_iota(jnp.int32, (16, LANES), 1)

    def cut(read, position):
        group, shift = position // LANES, position % LANES
        block = read(group)
        if not shift:
            return block
        turned = pltpu.roll(block, LANES - shift, 1)
        if shift + part > LANES:
            turned = jnp.where(lane < LANES - shift, turned, pltpu.roll(read(group + 1), LANES - shift, 1))
        return turned

    line = lax.broadcasted_iota(jnp.int32, (16, LANES), 0)

    def vectors(g):
        return vector_rows[:, g * LANES : (g + 1) * LANES]

    def up(g):
        return jnp.broadcast_to(ub_ref[0:1, g * LANES : (g + 1) * LANES], (16, LANES))

    for c in range(chips):
        block = cut(vectors, c * part)
        for r in range(4):
            block = jnp.where(line == 9 + r, cut(up, (4 * c + r) * part), block)
        for half in range(2):
            buffer[half, c // PLANE, c % PLANE] = block[8 * half : 8 * half + 8]


STEP = 256


def product(left, right, width, write):
    def one(n, _):
        offset = pl.multiple_of(n * STEP, STEP)
        write(offset, dot_tn(left[...], right[:, pl.ds(offset, STEP)]).astype(BF16))
        return 0

    lax.fori_loop(0, width // STEP, one, 0)


UP_A, UP_B, DOWN_A, DOWN_B = 5, 6, 7, 8
EARLY = {
    0: (("first", DOWN_A), ("first", DOWN_B)),
    2: (("second", DOWN_A),),
    3: (("second", DOWN_B),),
}
START = (("first", UP_A), ("first", UP_B), ("third", DOWN_A))
DURING = {
    1: (("third", DOWN_B), ("first", 4)),
    2: (("second", UP_A),),
    3: (("fourth", DOWN_A), ("second", UP_B)),
    4: (("fourth", DOWN_B), ("third", UP_A), ("second", 4)),
    5: (("third", UP_B),),
    6: (("third", 4), ("fourth", UP_A)),
    7: (("fourth", UP_B), ("fourth", 4)),
}
WEIGHTS = {1: (("first", 1),), 2: (("first", 2), ("second", 1))}
AFTER = {
    0: (("first", 3),),
    1: (("first", 0),),
    2: (("second", 2),),
    3: (("third", 1),),
    4: (("second", 3),),
    5: (("second", 0),),
    6: (("third", 2),),
    7: (("third", 3), ("fourth", 1), ("third", 0), ("fourth", 2), ("fourth", 3), ("fourth", 0)),
}


def reduce_attend(
    x_hbm, resid_hbm, w_hbm, out_hbm, gvec_ref, gub_ref,
    act_hbm, hidden_hbm, normed_hbm, ffn_hbm, mixed_hbm, branch_hbm,
    a_ref, k_ref, v_ref, e_ref, s_ref, sq_ref, sk_ref, cs_ref,
    out4, grad4, r_b, r_q, r_k, r_v, r_o, r_u, r_d,
    after, back, x_all, weights, gb, rows, bounce, resid_tile, grad_tile, *scratch,
):
    kinds = 9
    names = ("got", "corner_x", "corner_y", "side_x", "side_y", "column", "final")
    full, scratch = scratch[:7], scratch[7:]
    full = (*full[:5], full[5], full[5], full[6], full[6])
    parts = [full] + [scratch[n * kinds : (n + 1) * kinds] for n in range(len(names))]
    swap_sem, big_sem, tile_sem, feed_sem, *sems = scratch[len(names) * kinds :]
    here = Place()
    seq, chunk, chunks = pl.program_id(0), pl.program_id(1), pl.num_programs(1)
    step = seq * chunks + chunk
    last = pl.num_programs(0) * chunks - 1
    reduce = Reduce(here, *parts, (r_b, r_q, r_k, r_v, r_o, r_u, r_u, r_d, r_d), sems)
    pairs, length, width = out_hbm.shape
    block = length // 2
    swaps = []
    for n in range(pairs):
        source = out_hbm.at[n]
        mine = pl.ds(pl.multiple_of(here.core * block, block), block)
        theirs = pl.ds(pl.multiple_of(here.other * block, block), block)
        place = out4.at[here.core * pairs + n]
        swaps.append(
            (
                pltpu.make_async_copy(source.at[mine, :], bounce, swap_sem.at[n, 0]),
                pltpu.make_async_copy(bounce, place, swap_sem.at[n, 1]),
                remote(source.at[theirs, :], place, swap_sem.at[n, 2], swap_sem.at[n, 3], here.sibling),
            )
        )
    big = [
        pltpu.make_async_copy(source, target, big_sem.at[n])
        for n, (source, target) in enumerate(((x_hbm, x_all), (w_hbm, weights)))
    ]
    levels = act_hbm.shape[1] // width

    def slot(n):
        return back.at[:, pl.ds(pl.multiple_of(n * width, width), width)]

    def block_of(n):
        return pl.ds(pl.multiple_of(n * width, width), width)

    def later(n):
        return (n + 2 * here.other) % levels

    def act_feed(n):
        return pltpu.make_async_copy(act_hbm.at[:, block_of(n)], slot(n % 2), feed_sem.at[n % 2])

    def hidden_feed(n):
        return pltpu.make_async_copy(hidden_hbm.at[:, block_of(later(n))], slot(n % 2), feed_sem.at[n % 2])

    def square(t, left, right):
        def write(offset, value):
            full[t][:, :, :, pl.ds(offset, STEP)] = value.reshape(full[t].shape[:3] + (STEP,))

        product(left, right, width, write)

    @pl.when(step == 0)
    def _():
        gb[...] = jnp.zeros_like(gb)
        ffn_feed = pltpu.make_async_copy(ffn_hbm, slot(2), feed_sem.at[2])
        normed_feed = pltpu.make_async_copy(normed_hbm, x_all, big_sem.at[2])
        mixed_feed = pltpu.make_async_copy(mixed_hbm, slot(2), feed_sem.at[2])
        branch_feed = pltpu.make_async_copy(branch_hbm, slot(0), feed_sem.at[0])
        ffn_feed.start()
        act_feed(0).start()
        act_feed(1).start()
        normed_feed.start()
        meet(here)
        swaps[0][0].start()
        for _, _, send in swaps:
            send.start()
        ffn_feed.wait()

        def down_level(n, _):
            act_feed(n).wait()

            def write(offset, value):
                full[DOWN_A][n, :, :, pl.ds(offset, STEP)] = value.reshape(
                    full[DOWN_A].shape[1:3] + (STEP,)
                )

            product(slot(n % 2), slot(2), width, write)

            @pl.when(n + 2 < levels)
            def _():
                act_feed(n + 2).start()

            @pl.when(n + 2 >= levels)
            def _():
                hidden_feed(n + 2 - levels).start()

            reduce.giving(DOWN_A, n).start()
            reduce.giving(DOWN_B, n).start()
            return 0

        lax.fori_loop(0, levels, down_level, 0)
        mixed_feed.start()
        normed_feed.wait()

        def up_block(n, _):
            for m, stages in EARLY.items():

                @pl.when(n == m)
                def _(stages=stages):
                    reduce.run(stages)

            hidden_feed(n).wait()

            def write(offset, value):
                place = pl.ds(pl.multiple_of(later(n) * width + offset, STEP), STEP)
                full[UP_A][:, :, :, place] = value.reshape(full[UP_A].shape[:3] + (STEP,))

            product(x_all, slot(n % 2), width, write)

            @pl.when(n + 2 < levels)
            def _():
                hidden_feed(n + 2).start()

            @pl.when(n == levels - 2)
            def _():
                branch_feed.start()

            for m in range(2):

                @pl.when(n == m)
                def _(m=m):
                    reduce.giving(UP_A + m, 0).start()

            return 0

        lax.fori_loop(0, levels, up_block, 0)
        mixed_feed.wait()
        branch_feed.wait()
        square(4, slot(2), slot(0))
        reduce.giving(4, 0).start()
        swaps[0][0].wait()
        swaps[0][1].start()
        for copy in big:
            copy.start()
        reduce.run(START)

    for n, stages in DURING.items():

        @pl.when(step == n)
        def _(n=n, stages=stages):
            if n == 1:
                swaps[0][1].wait()
                swaps[1][0].start()
            if n == 2:
                swaps[1][0].wait()
                swaps[1][1].start()
            reduce.run(stages)

    @pl.when(chunk == 0)
    def _():
        after[...] = jnp.zeros_like(after)

    at = pl.multiple_of((seq * chunks + chunks - 1 - chunk) * CHUNK, CHUNK)
    attend_back(
        a_ref, k_ref, v_ref, e_ref, s_ref, sq_ref, sk_ref, cs_ref, after, back.at[pl.ds(at, CHUNK), :], gb
    )

    @pl.when(step == last)
    def _():
        for copy in big:
            copy.wait()
        rows[0:3, :] = jnp.concatenate([gb[:, n * width : (n + 1) * width] for n in range(3)])
        rows[3:9, :] = gvec_ref[0:6, :]
        rows[9:16, :] = jnp.zeros((7, width), F32)
        pack_rows(rows, gub_ref, full[0])
        reduce.giving(0, 0).start()
        tiles = pairs * length // CHUNK
        per_seq = length // CHUNK

        def rows_of(i):
            return pl.ds(pl.multiple_of(i * CHUNK, CHUNK), CHUNK)

        def load(i):
            return pltpu.make_async_copy(
                resid_hbm.at[rows_of(i), :], resid_tile.at[i % 2], tile_sem.at[i % 2, 0]
            )

        load(0).start()
        for n in range(3):
            square(1 + n, x_all, slot(n))
            reduce.giving(1 + n, 0).start()
            reduce.run(WEIGHTS.get(n, ()))

        def writes(i):
            s, c = i // per_seq, i % per_seq
            spot = grad4.at[here.core * pairs + s, pl.ds((c % (per_seq // 2)) * CHUNK, CHUNK), :]
            local = pltpu.make_async_copy(grad_tile.at[i % 2], spot, tile_sem.at[i % 2, 1])
            away = remote(grad_tile.at[i % 2], spot, tile_sem.at[i % 2, 2], swap_sem.at[2 + i, 0], here.sibling)
            return local, away, here.core == c // (per_seq // 2)

        def written(i):
            local, away, stays = writes(i)

            @pl.when(stays)
            def _():
                local.wait()

            @pl.when(jnp.logical_not(stays))
            def _():
                away.wait_send()

        def tile(i, _):
            for n in range(tiles - 1):

                @pl.when(i == n)
                def _():
                    reduce.run(AFTER[n])

            @pl.when(i + 1 < tiles)
            def _():
                load(i + 1).start()

            load(i).wait()

            @pl.when(i >= 2)
            def _():
                written(i - 2)

            grad_tile[i % 2] = resid_tile[i % 2] + dot_nt(back[rows_of(i), :], weights[...])
            local, away, stays = writes(i)

            @pl.when(stays)
            def _():
                local.start()

            @pl.when(jnp.logical_not(stays))
            def _():
                away.start()

            return 0

        lax.fori_loop(0, tiles, tile, 0)
        reduce.run(AFTER[tiles - 1])
        for i in range(tiles - 2, tiles):
            written(i)
        for i in range(tiles):
            _, away, stays = writes(i)

            @pl.when(stays)
            def _(away=away):
                away.wait_recv()

        swaps[1][1].wait()
        for _, _, send in swaps:
            send.wait()
        reduce.drain()


def reduce_attend_call(
    x, resid, w, out, gvec, gub, act, hidden, normed, ffn, mixed, branch, a, k, v, e, s, sq, sk, cs
):
    chips = DEPTH * PLANE
    seqs, length, width = out.shape
    total, chunks, wide = seqs * length, length // CHUNK, HEADS * LANES
    anywhere = pl.BlockSpec(memory_space=pl.ANY)
    place = lambda s, c: s * chunks + chunks - 1 - c
    row = lambda n: pl.BlockSpec((CHUNK, n), lambda s, c: (place(s, c), 0))
    once = lambda a: pl.BlockSpec(
        a.shape, lambda s, c: (0,) * len(a.shape), pipeline_mode=pl.Buffered(1)
    )
    part, tall = width // chips, act.shape[1]
    pieces = [(8, LANES, F32)] + [(part, width // 2, BF16)] * 4
    pieces += [(part, tall // 4, BF16)] * 2 + [(tall // chips // 2, width // 2, BF16)] * 2
    kinds, sem = len(pieces), pltpu.SemaphoreType.DMA
    grid = (DEPTH, PLANE)
    scratch = [pltpu.VMEM((2,) + grid + pieces[0][:2], F32)]
    scratch += [pltpu.VMEM(grid + (part, width), BF16)] * 4
    scratch += [pltpu.VMEM(grid + (part, tall), BF16), pltpu.VMEM(grid + (tall // chips, width), BF16)]
    for lead in (grid, (2,), (2,), (DEPTH,), (DEPTH,), (DEPTH,)):
        scratch += [pltpu.VMEM(lead + p[:2], p[2]) for p in pieces]
    scratch += [pltpu.VMEM(p[:2], F32) for p in pieces]
    scratch += [sem((2 + total // CHUNK, 4)), sem((3,)), sem((2, 3)), sem((3,))]
    scratch += [sem((kinds, 4))] * 6 + [sem((kinds, 3))]
    shard = lambda rows, cols: jax.ShapeDtypeStruct((rows, cols), F32)
    return pl.pallas_call(
        reduce_attend,
        grid=(seqs, chunks),
        in_specs=[anywhere] * 4
        + [once(gvec), once(gub)]
        + [anywhere] * 6
        + [row(wide), row(wide), row(width), row(wide)]
        + [pl.BlockSpec((None, HEADS, LANES, LANES), lambda s, c: (place(s, c), 0, 0, 0))]
        + [row(width), row(width), row(LANES)],
        out_specs=[anywhere] * 9,
        out_shape=[
            jax.ShapeDtypeStruct((seqs * 2, length // 2, width), BF16),
            jax.ShapeDtypeStruct((seqs * 2, length // 2, width), F32),
            shard(16, LANES),
            shard(part, width),
            shard(part, width),
            shard(part, width),
            shard(part, width),
            shard(part, tall),
            shard(tall // chips, width),
        ],
        scratch_shapes=[
            pltpu.VMEM((HEADS, LANES, LANES), F32),
            pltpu.VMEM((total, 3 * width), BF16),
            pltpu.VMEM((total, width), BF16),
            pltpu.VMEM(w.shape, BF16),
            pltpu.VMEM((1, 3 * width), F32),
            pltpu.VMEM((16, width), F32),
            pltpu.VMEM((length // 2, width), BF16),
            pltpu.VMEM((2, CHUNK, width), F32),
            pltpu.VMEM((2, CHUNK, width), F32),
        ]
        + scratch,
        compiler_params=pltpu.CompilerParams(
            collective_id=1,
            has_side_effects=True,
            vmem_limit_bytes=VMEM_LIMIT,
            dimension_semantics=("arbitrary", "arbitrary"),
        ),
        name="reduce_attend",
    )(x, resid, w, out, gvec, gub, act, hidden, normed, ffn, mixed, branch, a, k, v, e, s, sq, sk, cs)


def pack_vectors(vectors, up_bias):
    part = vectors[0].shape[0]
    stacked = jnp.concatenate([jnp.stack(vectors), up_bias.reshape(-1, part)])
    return jnp.pad(stacked, ((0, 16 - stacked.shape[0]), (0, LANES - part)))


def unpack_vectors(gathered, part):
    chips = gathered.shape[0] // 16
    grid = gathered.reshape(chips, 16, LANES)[:, :13, :part].astype(F32)
    rows = jnp.transpose(grid[:, :9], (1, 0, 2)).reshape(9, chips * part)
    up_bias = grid[:, 9:].reshape(1, chips * 4 * part)
    return rows[0:3], jnp.pad(rows[3:9], ((0, 2), (0, 0))), up_bias


def pack_vector_grads(gb, gvec, gub, chips):
    width = gvec.shape[1]
    part = width // chips
    rows = jnp.concatenate([gb.reshape(3, width), gvec[0:6]]).reshape(9, chips, part)
    rows = jnp.transpose(rows, (1, 0, 2))
    grid = jnp.concatenate([rows, gub.reshape(chips, 4, part)], axis=1)
    grid = jnp.pad(grid, ((0, 0), (0, 3), (0, LANES - part)))
    return grid.reshape(chips * 16, LANES)


def finish(part, out_in, grad_in, vec_in, *refs):
    weights, (out_ref, grad_ref, *rest) = refs[:6], refs[6:]
    out_ref[...] = out_in[...]
    grad_ref[...] = grad_in[...]

    @pl.when(pl.program_id(0) == 0)
    def _():
        for source, target in zip(weights, rest[:6]):
            target[...] = source[...]
        for n, target in enumerate(rest[6:15]):
            target[...] = vec_in[n, :part]
        for n in range(4):
            rest[15][n * part : (n + 1) * part] = vec_in[9 + n, :part]


def finish_call(out, grad, vec, weights, part):
    row = pl.BlockSpec((None,) + out.shape[1:], lambda i: (i, 0, 0))
    whole = lambda shape: pl.BlockSpec(shape, lambda i: (0,) * len(shape))
    flat = [(part,)] * 9 + [(4 * part,)]
    return pl.pallas_call(
        functools.partial(finish, part),
        grid=(out.shape[0],),
        in_specs=[row, row, whole(vec.shape)] + [whole(w.shape) for w in weights],
        out_specs=[row, row] + [whole(w.shape) for w in weights] + [whole(s) for s in flat],
        out_shape=[
            jax.ShapeDtypeStruct(out.shape, out.dtype),
            jax.ShapeDtypeStruct(grad.shape, grad.dtype),
        ]
        + [jax.ShapeDtypeStruct(w.shape, F32) for w in weights]
        + [jax.ShapeDtypeStruct(s, F32) for s in flat],
        compiler_params=pltpu.CompilerParams(
            dimension_semantics=("arbitrary",), vmem_limit_bytes=VMEM_LIMIT
        ),
        name="finish",
    )(out, grad, vec, *weights)


def local(
    inputs,
    horizon,
    query_weight,
    query_bias,
    key_weight,
    key_bias,
    value_weight,
    value_bias,
    out_weight,
    out_bias,
    first_gain,
    first_shift,
    up_weight,
    up_bias,
    down_weight,
    down_bias,
    second_gain,
    second_shift,
    cotangent,
):
    chips = lax.axis_size("dp")
    core = lax.axis_index("seq")
    part = query_bias.shape[0]
    seqs = inputs.shape[0] // 2
    direct = chips == DEPTH * PLANE
    vectors = pack_vectors(
        (
            query_bias,
            key_bias,
            value_bias,
            out_bias,
            first_gain,
            first_shift,
            down_bias,
            second_gain,
            second_shift,
        ),
        up_bias,
    )
    weights = (query_weight, key_weight, value_weight, out_weight, up_weight, down_weight)
    spans = lax.dynamic_slice_in_dim(horizon, core * seqs, seqs)
    length = 2 * inputs.shape[1]
    chunks = length // CHUNK
    cs = rotation(spans, length)
    flat = lambda a: a.reshape(-1, a.shape[-1])
    if direct:
        x, ct, wqkv, wo, wu, wd, _, *saved, vec, ubias = gather_attend_call(
            inputs, cotangent, *weights, vectors, cs
        )
    else:
        gather = lambda a: lax.all_gather(a, "dp", axis=0, tiled=True)
        x, ct = (lax.all_to_all(a, "seq", 0, 1, tiled=True) for a in (inputs, cotangent))
        wqkv = gather(jnp.concatenate(weights[:3], axis=1))
        wo, wu, wd, gathered = (gather(a) for a in (*weights[3:], vectors))
        bqkv, vec, ubias = unpack_vectors(gathered, part)
        saved = forward_call(flat(x), wqkv, bqkv, cs, chunks)
    a, k, v, sq, sk, mixed, den, s = saved
    fx = flat(x)
    out, resid, e, act, hidden, normed, ffn, branch, gvec, gub = middle_call(
        fx, flat(ct), mixed, den, vec, ubias, wo, wu, wd
    )
    out = out.reshape(x.shape)
    if direct:
        out, grad, gvectors, gq, gk, gv, go, gu, gd = reduce_attend_call(
            fx, resid, wqkv, out, gvec, gub, act, hidden, normed, ffn, mixed, branch,
            a, k, v, e, s, sq, sk, cs,
        )
    else:
        go, gu, gd = dot_tn(mixed, branch), dot_tn(normed, hidden), dot_tn(act, ffn)
        grad, gw, gb = backward_call(fx, a, k, v, e, s, sq, sk, cs, resid, wqkv, chunks)
        gvectors = pack_vector_grads(gb, gvec, gub, chips)
        out, grad = (
            lax.all_to_all(a, "seq", 1, 0, tiled=True) for a in (out, grad.reshape(x.shape))
        )
        total = lambda g: lax.psum(
            lax.psum_scatter(g.astype(F32), "dp", scatter_dimension=0, tiled=True), "seq"
        )
        gw, go, gu, gd, gvectors = (total(g) for g in (gw, go, gu, gd, gvectors))
        gq, gk, gv = jnp.split(gw, 3, axis=1)
    if direct:
        weights = (gq, gk, gv, go, gu, gd)
        out, grad, gq, gk, gv, go, gu, gd, *thin, wide = finish_call(out, grad, gvectors, weights, part)
    else:
        rows = gvectors[:, :part]
        thin, wide = [rows[n] for n in range(9)], rows[9:13].reshape(-1)
    bq, bk, bv, bo, g1, s1, bd, g2, s2 = thin
    return out, grad, gq, bq, gk, bk, gv, bv, go, bo, g1, s1, gu, wide, gd, bd, g2, s2


def solution(mesh):
    long, wide, thin = P("dp", "seq", None), P("dp", None), P("dp")
    shards = (wide, thin, wide, thin, wide, thin, wide, thin, thin, thin, wide, thin, wide, thin, thin, thin)
    return jax.shard_map(
        local,
        mesh=mesh,
        in_specs=(long, thin, *shards, long),
        out_specs=(long, long, *shards),
        check_vma=False,
    )
```

```python
import functools
import math

import jax
import jax.numpy as jnp
from jax import lax
from jax.experimental import pallas as pl
from jax.experimental.pallas import tpu as pltpu
from jax.sharding import PartitionSpec as P

HEADS = 12
HEAD = 64
PAIRS = HEADS // 2
LANES = 128
CHUNK = 256
ROWS = 512
PARTS = 2
NORM_EPS = 1e-05
GELU_A = 0.7978845608
GELU_B = 0.044715
VMEM_LIMIT = 60 * 1024 * 1024
F32, BF16 = jnp.float32, jnp.bfloat16


def dot_nn(a, b):
    return lax.dot_general(a, b, (((1,), (0,)), ((), ())), preferred_element_type=F32)


def dot_nt(a, b):
    return lax.dot_general(a, b, (((1,), (1,)), ((), ())), preferred_element_type=F32)


def dot_tn(a, b):
    return lax.dot_general(a, b, (((0,), (0,)), ((), ())), preferred_element_type=F32)


def low_lanes(rows):
    return lax.broadcasted_iota(jnp.int32, (rows, LANES), 1) < HEAD


def swap(values):
    return pltpu.roll(values, HEAD, 1)


def softplus_and_slope(values):
    e = jnp.exp(-jnp.abs(values))
    plus = jnp.maximum(values, 0.0) + jnp.log1p(e)
    slope = jnp.where(values >= 0.0, 1.0, e) / (1.0 + e)
    return plus, slope


def attend_forward(
    x_ref, w_ref, b_ref, cs_ref, a_ref, k_ref, v_ref, sq_ref, sk_ref, mixed_ref, den_ref, s_ref, state
):
    @pl.when(pl.program_id(1) == 0)
    def _():
        state[...] = jnp.zeros_like(state)

    attend(
        x_ref[...],
        w_ref,
        b_ref,
        cs_ref,
        a_ref,
        k_ref,
        v_ref,
        sq_ref,
        sk_ref,
        mixed_ref,
        den_ref,
        s_ref,
        state,
    )


def attend(
    x, w_ref, b_ref, cs_ref, a_ref, k_ref, v_ref, sq_ref, sk_ref, mixed_ref, den_ref, s_ref, state
):
    rows, width = x.shape
    cs = cs_ref[...]
    low = low_lanes(rows)
    causal = lax.broadcasted_iota(jnp.int32, (rows, rows), 0) >= lax.broadcasted_iota(
        jnp.int32, (rows, rows), 1
    )

    for half in range(2):
        slope_ref = (sq_ref, sk_ref)[half]
        feature_ref = (a_ref, k_ref)[half]
        pre = dot_nn(x, w_ref[:, half * width : (half + 1) * width])
        pre = pre + b_ref[half : half + 1, :]
        plus, slope = softplus_and_slope(pre)
        slope_ref[...] = slope.astype(BF16)
        for pair in range(PAIRS):
            both = plus[:, pair * LANES : (pair + 1) * LANES]
            other = swap(both)
            even = jnp.where(low, both, other) * cs
            odd = jnp.where(low, other, both) * cs
            feature_ref[:, (2 * pair) * LANES : (2 * pair + 1) * LANES] = even.astype(BF16)
            feature_ref[:, (2 * pair + 1) * LANES : (2 * pair + 2) * LANES] = odd.astype(BF16)
    values = dot_nn(x, w_ref[:, 2 * width :]) + b_ref[2:3, :]
    v_ref[...] = values.astype(BF16)
    for pair in range(PAIRS):
        both = values[:, pair * LANES : (pair + 1) * LANES]
        results = []
        for odd in range(2):
            head = 2 * pair + odd
            query = a_ref[:, head * LANES : (head + 1) * LANES]
            key = k_ref[:, head * LANES : (head + 1) * LANES]
            wide = (jnp.where(low, 1.0, both) if odd else jnp.where(low, both, 1.0)).astype(BF16)
            scores = jnp.where(causal, dot_nt(query, key), 0.0).astype(BF16)
            before = state[head]
            before_low = before.astype(BF16)
            s_ref[head] = before_low
            results.append(dot_nn(scores, wide) + dot_nn(query, before_low))
            state[head] = before + dot_tn(key, wide)
        numer = jnp.where(low, results[0], results[1])
        denom = swap(jnp.where(low, results[1], results[0]))
        mixed_ref[:, pair * LANES : (pair + 1) * LANES] = (numer / denom).astype(BF16)
        den_ref[:, pair * LANES : (pair + 1) * LANES] = denom


def forward_call(x, w, b, cs, chunks):
    total, width = x.shape
    seqs = total // (chunks * CHUNK)
    row = lambda n: pl.BlockSpec((CHUNK, n), lambda s, c: (s * chunks + c, 0))
    once = lambda shape: pl.BlockSpec(
        shape, lambda s, c: (0,) * len(shape), pipeline_mode=pl.Buffered(1)
    )
    wide = HEADS * LANES
    return pl.pallas_call(
        attend_forward,
        grid=(seqs, chunks),
        in_specs=[row(width), once(w.shape), once(b.shape), row(LANES)],
        out_specs=[
            row(wide),
            row(wide),
            row(width),
            row(width),
            row(width),
            row(width),
            row(width),
            pl.BlockSpec((None, HEADS, LANES, LANES), lambda s, c: (s * chunks + c, 0, 0, 0)),
        ],
        out_shape=[
            jax.ShapeDtypeStruct((total, wide), BF16),
            jax.ShapeDtypeStruct((total, wide), BF16),
            jax.ShapeDtypeStruct((total, width), BF16),
            jax.ShapeDtypeStruct((total, width), BF16),
            jax.ShapeDtypeStruct((total, width), BF16),
            jax.ShapeDtypeStruct((total, width), BF16),
            jax.ShapeDtypeStruct((total, width), F32),
            jax.ShapeDtypeStruct((seqs * chunks, HEADS, LANES, LANES), BF16),
        ],
        scratch_shapes=[pltpu.VMEM((HEADS, LANES, LANES), F32)],
        compiler_params=pltpu.CompilerParams(
            dimension_semantics=("arbitrary", "arbitrary"), vmem_limit_bytes=VMEM_LIMIT
        ),
        name="attend_forward",
    )(x, w, b, cs)


def row_mean(values):
    return jnp.mean(values, axis=-1, keepdims=True)


def norm_parts(values):
    center = values - row_mean(values)
    scale = lax.rsqrt(row_mean(center * center) + NORM_EPS)
    return center * scale, scale


def norm_back(grad, gain, unit, scale):
    scaled = grad * gain
    return (scaled - row_mean(scaled) - unit * row_mean(scaled * unit)) * scale


def add_rows(values):
    return jnp.sum(values, axis=0, keepdims=True)


def middle(
    tiles,
    x_ref,
    ct_ref,
    mixed_ref,
    den_ref,
    vec_ref,
    ubias_ref,
    wo_ref,
    wu_ref,
    wd_ref,
    out_ref,
    resid_ref,
    e_ref,
    act,
    hidden_ref,
    normed_ref,
    ffn_ref,
    branch_ref,
    gvec_ref,
    gub_ref,
    slope,
):
    step = pl.program_id(0)
    rows, width = x_ref.shape
    hidden_width = wu_ref.shape[1]
    tile = hidden_width // tiles

    @pl.when(step == 0)
    def _():
        gvec_ref[...] = jnp.zeros_like(gvec_ref)
        gub_ref[...] = jnp.zeros_like(gub_ref)

    out_bias, gain1, shift1 = vec_ref[0:1], vec_ref[1:2], vec_ref[2:3]
    down_bias, gain2, shift2 = vec_ref[3:4], vec_ref[4:5], vec_ref[5:6]
    depth = rows // PARTS
    groups = [slice(n * depth, (n + 1) * depth) for n in range(PARTS)]
    low = low_lanes(depth)
    even_lane = lax.broadcasted_iota(jnp.int32, (depth, LANES), 1) % 2 == 0
    same_head = (
        lax.broadcasted_iota(jnp.int32, (2 * LANES, 2 * LANES), 0) // HEAD
        == lax.broadcasted_iota(jnp.int32, (2 * LANES, 2 * LANES), 1) // HEAD
    ).astype(F32).astype(BF16)

    def mix(part):
        mixed = mixed_ref[part, :]
        resid = x_ref[part, :].astype(F32) + (dot_nn(mixed, wo_ref[...]) + out_bias)
        unit1, scale1 = norm_parts(resid)
        normed = unit1 * gain1 + shift1
        normed_low = normed.astype(BF16)
        normed_ref[part, :] = normed_low
        return unit1, scale1, normed, normed_low

    def feed(part, state):
        unit1, scale1, normed, normed_low = state
        ffn = jnp.zeros((depth, width), F32)
        for t in range(tiles):
            cols = slice(t * tile, (t + 1) * tile)
            hidden = dot_nn(normed_low, wu_ref[:, cols]) + ubias_ref[:, cols]
            square = hidden * hidden
            inner = hidden * (GELU_A + (GELU_A * GELU_B) * square)
            tanh = jnp.tanh(inner)
            half = 0.5 + 0.5 * tanh
            active = (hidden * half).astype(BF16)
            curve = half + (0.5 * hidden) * (1.0 - tanh * tanh) * (
                GELU_A + (3.0 * GELU_A * GELU_B) * square
            )
            act[part, cols] = active
            slope[part, cols] = curve.astype(BF16)
            ffn = ffn + dot_nn(active, wd_ref[cols, :])
        unit2, scale2 = norm_parts(normed + (ffn + down_bias))
        out_ref[part, :] = (unit2 * gain2 + shift2).astype(BF16)
        grad = ct_ref[part, :].astype(F32)
        back_final = norm_back(grad, gain2, unit2, scale2)
        back_ffn = back_final.astype(BF16)
        ffn_ref[part, :] = back_ffn
        gvec_ref[4:5] += add_rows(grad * unit2)
        gvec_ref[5:6] += add_rows(grad)
        gvec_ref[3:4] += add_rows(back_ffn.astype(F32))
        return unit1, scale1, back_final, back_ffn

    def feed_back(part, state):
        unit1, scale1, back_normed, back_ffn = state
        for t in range(tiles):
            cols = slice(t * tile, (t + 1) * tile)
            back_active = dot_nt(back_ffn, wd_ref[cols, :])
            back_hidden = (back_active * slope[part, cols].astype(F32)).astype(BF16)
            hidden_ref[part, cols] = back_hidden
            gub_ref[:, cols] += add_rows(back_hidden.astype(F32))
            back_normed = back_normed + dot_nt(back_hidden, wu_ref[:, cols])
        gvec_ref[1:2] += add_rows(back_normed * unit1)
        gvec_ref[2:3] += add_rows(back_normed)
        back_resid = norm_back(back_normed, gain1, unit1, scale1)
        resid_ref[part, :] = back_resid
        back_branch = back_resid.astype(BF16)
        branch_ref[part, :] = back_branch
        gvec_ref[0:1] += add_rows(back_branch.astype(F32))
        return back_branch

    def mix_back(part, back_branch):
        back_mixed = dot_nt(back_branch, wo_ref[...])
        back_numer = back_mixed / den_ref[part, :]
        product = back_numer * mixed_ref[part, :].astype(F32)
        high = product.astype(BF16)
        rest = (product - high.astype(F32)).astype(BF16)
        for block in range(width // (2 * LANES)):
            cols = slice(block * 2 * LANES, (block + 1) * 2 * LANES)
            sums = dot_nn(high[:, cols], same_head) + dot_nn(rest[:, cols], same_head)
            for inside in range(2):
                pair = 2 * block + inside
                back = -sums[:, inside * LANES : (inside + 1) * LANES]
                back_high = back.astype(BF16).astype(F32)
                spread = swap(jnp.where(even_lane, back_high, back - back_high) * (2.0 / HEAD))
                numer = back_numer[:, pair * LANES : (pair + 1) * LANES]
                e_ref[part, (2 * pair) * LANES : (2 * pair + 1) * LANES] = jnp.where(
                    low, numer, spread
                ).astype(BF16)
                e_ref[part, (2 * pair + 1) * LANES : (2 * pair + 2) * LANES] = jnp.where(
                    low, spread, numer
                ).astype(BF16)

    states = [mix(part) for part in groups]
    for stage in (feed, feed_back, mix_back):
        states = [stage(part, state) for part, state in zip(groups, states)]


def middle_call(x, ct, mixed, den, vec, ubias, wo, wu, wd, tiles=4):
    total, width = x.shape
    hidden_width = wu.shape[1]
    row = lambda n: pl.BlockSpec((ROWS, n), lambda i: (i, 0))
    once = lambda shape: pl.BlockSpec(
        shape, lambda i: (0,) * len(shape), pipeline_mode=pl.Buffered(1)
    )
    keep = lambda shape: pl.BlockSpec(shape, lambda i: (0,) * len(shape))
    wide = HEADS * LANES
    shape = lambda n, kind=BF16: jax.ShapeDtypeStruct((total, n), kind)
    return pl.pallas_call(
        functools.partial(middle, tiles),
        grid=(total // ROWS,),
        in_specs=[
            row(width),
            row(width),
            row(width),
            row(width),
            once(vec.shape),
            once(ubias.shape),
            once(wo.shape),
            once(wu.shape),
            once(wd.shape),
        ],
        out_specs=[
            row(width),
            row(width),
            row(wide),
            row(hidden_width),
            row(hidden_width),
            row(width),
            row(width),
            row(width),
            keep((8, width)),
            keep((1, hidden_width)),
        ],
        out_shape=[
            shape(width),
            shape(width, F32),
            shape(wide),
            shape(hidden_width),
            shape(hidden_width),
            shape(width),
            shape(width),
            shape(width),
            jax.ShapeDtypeStruct((8, width), F32),
            jax.ShapeDtypeStruct((1, hidden_width), F32),
        ],
        scratch_shapes=[pltpu.VMEM((ROWS, hidden_width), BF16)],
        compiler_params=pltpu.CompilerParams(
            dimension_semantics=("arbitrary",), vmem_limit_bytes=VMEM_LIMIT
        ),
        name="middle",
    )(x, ct, mixed, den, vec, ubias, wo, wu, wd)


def attend_back(a_ref, k_ref, v_ref, e_ref, s_ref, sq_ref, sk_ref, cs_ref, after, back, gb_ref):
    rows, width = v_ref.shape
    cs = cs_ref[...]
    low = low_lanes(rows)
    i = lax.broadcasted_iota(jnp.int32, (rows, rows), 0)
    j = lax.broadcasted_iota(jnp.int32, (rows, rows), 1)
    causal, anti = i >= j, i <= j
    for pair in range(PAIRS):
        both = v_ref[:, pair * LANES : (pair + 1) * LANES].astype(F32)
        back_q, back_k, back_v = [], [], []
        for odd in range(2):
            head = 2 * pair + odd
            cols = slice(head * LANES, (head + 1) * LANES)
            query, key, e = a_ref[:, cols], k_ref[:, cols], e_ref[:, cols]
            wide = (jnp.where(low, 1.0, both) if odd else jnp.where(low, both, 1.0)).astype(BF16)
            state = s_ref[head]
            later = after[head]
            later_low = later.astype(BF16)
            scores_t = jnp.where(anti, dot_nt(key, query), 0.0).astype(BF16)
            back_s = jnp.where(causal, dot_nt(e, wide), 0.0).astype(BF16)
            back_st = jnp.where(anti, dot_nt(wide, e), 0.0).astype(BF16)
            y = (dot_nn(back_s, key) + dot_nt(e, state)) * cs
            back_q.append(y + swap(y))
            y = (dot_nn(back_st, query) + dot_nt(wide, later_low)) * cs
            back_k.append(y + swap(y))
            back_v.append(dot_nn(scores_t, e) + dot_nn(key, later_low))
            after[head] = later + dot_tn(query, e)
        cols = slice(pair * LANES, (pair + 1) * LANES)
        dq = jnp.where(low, back_q[0], back_q[1]) * sq_ref[:, cols].astype(F32)
        dk = jnp.where(low, back_k[0], back_k[1]) * sk_ref[:, cols].astype(F32)
        dv = jnp.where(low, back_v[0], back_v[1])
        for n, piece in enumerate((dq, dk, dv)):
            piece = piece.astype(BF16)
            cols = slice(n * width + pair * LANES, n * width + (pair + 1) * LANES)
            back[:, cols] = piece
            gb_ref[:, cols] += add_rows(piece.astype(F32))


def attend_backward(
    x_ref,
    a_ref,
    k_ref,
    v_ref,
    e_ref,
    s_ref,
    sq_ref,
    sk_ref,
    cs_ref,
    resid_ref,
    w_ref,
    grad_ref,
    gw_ref,
    gb_ref,
    after,
    back,
    gw,
):
    rows, width = x_ref.shape

    @pl.when((pl.program_id(0) == 0) & (pl.program_id(1) == 0))
    def _():
        gw[...] = jnp.zeros_like(gw)
        gb_ref[...] = jnp.zeros_like(gb_ref)

    @pl.when(pl.program_id(1) == 0)
    def _():
        after[...] = jnp.zeros_like(after)

    attend_back(a_ref, k_ref, v_ref, e_ref, s_ref, sq_ref, sk_ref, cs_ref, after, back, gb_ref)
    x = x_ref[...]
    total = resid_ref[...]
    for n in range(3):
        cols = slice(n * width, (n + 1) * width)
        piece = back[:, cols]
        gw[:, cols] += dot_tn(x, piece)
        total = total + dot_nt(piece, w_ref[:, cols])
    grad_ref[...] = total

    @pl.when((pl.program_id(0) == pl.num_programs(0) - 1) & (pl.program_id(1) == pl.num_programs(1) - 1))
    def _():
        gw_ref[...] = gw[...].astype(BF16)


def backward_call(x, a, k, v, e, s, sq, sk, cs, resid, w, chunks):
    total, width = x.shape
    seqs = total // (chunks * CHUNK)
    place = lambda s, c: s * chunks + chunks - 1 - c
    row = lambda n: pl.BlockSpec((CHUNK, n), lambda s, c: (place(s, c), 0))
    once = lambda shape: pl.BlockSpec(
        shape, lambda s, c: (0,) * len(shape), pipeline_mode=pl.Buffered(1)
    )
    keep = lambda shape: pl.BlockSpec(shape, lambda s, c: (0,) * len(shape))
    wide = HEADS * LANES
    return pl.pallas_call(
        attend_backward,
        grid=(seqs, chunks),
        in_specs=[
            row(width),
            row(wide),
            row(wide),
            row(width),
            row(wide),
            pl.BlockSpec((None, HEADS, LANES, LANES), lambda s, c: (place(s, c), 0, 0, 0)),
            row(width),
            row(width),
            row(LANES),
            row(width),
            once(w.shape),
        ],
        out_specs=[row(width), keep(w.shape), keep((1, w.shape[1]))],
        out_shape=[
            jax.ShapeDtypeStruct((total, width), F32),
            jax.ShapeDtypeStruct(w.shape, BF16),
            jax.ShapeDtypeStruct((1, w.shape[1]), F32),
        ],
        scratch_shapes=[
            pltpu.VMEM((HEADS, LANES, LANES), F32),
            pltpu.VMEM((CHUNK, w.shape[1]), BF16),
            pltpu.VMEM(w.shape, F32),
        ],
        compiler_params=pltpu.CompilerParams(
            dimension_semantics=("arbitrary", "arbitrary"), vmem_limit_bytes=VMEM_LIMIT
        ),
        name="attend_backward",
    )(x, a, k, v, e, s, sq, sk, cs, resid, w)


def rotation(horizon, length):
    seqs = horizon.shape[0]
    position = jnp.arange(length, dtype=F32)
    angles = 0.5 * math.pi * position[None, :] / horizon.astype(F32)[:, None]
    return jnp.concatenate(
        [
            jnp.broadcast_to(jnp.cos(angles)[..., None], (seqs, length, HEAD)),
            jnp.broadcast_to(jnp.sin(angles)[..., None], (seqs, length, HEAD)),
        ],
        axis=-1,
    ).reshape(seqs * length, LANES)


DEPTH, PLANE = 4, 4


class Place:
    def __init__(self):
        self.dp, self.core = lax.axis_index("dp"), lax.axis_index("seq")
        self.z, self.spot = self.dp // PLANE, self.dp % PLANE
        self.other = 1 - self.core
        self.levels = [(self.z + step) % DEPTH for step in range(DEPTH)]
        self.across_x = self.spot + 1 - 2 * (self.spot % 2)
        self.across_y = (self.spot + 2) % PLANE
        self.diagonal = PLANE - 1 - self.spot
        self.x_peer = (self.z * PLANE + self.across_x, self.core)
        self.y_peer = (self.z * PLANE + self.across_y, self.core)
        self.sibling = (self.dp, self.other)

    def level(self, step):
        return self.levels[step]

    def z_peer(self, step):
        return (self.level(step) * PLANE + self.spot, self.core)


def remote(source, target, send, recv, peer):
    copy = pltpu.make_async_remote_copy(
        src_ref=source,
        dst_ref=target,
        send_sem=send,
        recv_sem=recv,
        device_id=peer,
        device_id_type=pl.DeviceIdType.MESH,
    )
    return copy


def meet(here):
    barrier = pltpu.get_barrier_semaphore()
    peers = [here.x_peer, here.y_peer, here.sibling] + [here.z_peer(n) for n in range(1, DEPTH)]
    for peer in peers:
        pl.semaphore_signal(barrier, inc=1, device_id=peer, device_id_type=pl.DeviceIdType.MESH)
    pl.semaphore_wait(barrier, len(peers))


class Gather:
    def __init__(self, here, shards, outs, own_send, x_send, y_send, c_send, link_recv, core_recv):
        self.here, self.shards, self.outs = here, shards, outs
        self.own_send, self.link_recv, self.core_recv = own_send, link_recv, core_recv
        self.sems = {"x": x_send, "y": y_send, "c": c_send}
        self.heights = [out.shape[0] // (DEPTH * PLANE) for out in outs]
        self.started = []

    def index(self, level, spot):
        return level * PLANE + spot

    def rows(self, t, level, spot):
        height = self.heights[t]
        return pl.ds(pl.multiple_of(self.index(level, spot) * height, height), height)

    def piece(self, t, level, spot, core):
        half = self.heights[t] // 2
        start = self.index(level, spot) * self.heights[t] + core * half
        return self.outs[t].at[pl.ds(pl.multiple_of(start, half), half), :]

    def passing(self, t, level, spot, kind):
        here, at = self.here, self.index(level, spot)
        peer = {"x": here.x_peer, "y": here.y_peer, "c": here.sibling}[kind]
        arrive = self.core_recv if kind == "c" else self.link_recv
        ref = self.piece(t, level, spot, here.core)
        return [remote(ref, ref, self.sems[kind].at[t, at], arrive.at[t, at], peer)]

    def spreading(self, t, slot):
        here, height = self.here, self.heights[t]
        whole = slot == 2
        peer = (here.x_peer, here.y_peer, here.sibling)[slot] if slot < 3 else here.z_peer(slot - 2)
        mine = self.index(here.z, here.spot)
        arrive = (self.core_recv if whole else self.link_recv).at[t, mine]
        half = height // 2
        if whole:
            take, place = pl.ds(0, height), self.rows(t, here.z, here.spot)
        else:
            take = pl.ds(pl.multiple_of(here.core * half, half), half)
            place = pl.ds(pl.multiple_of(mine * height + here.core * half, half), half)
        copies = []
        for n, ref in enumerate(self.shards[t]):
            target = self.outs[t].at[place, n * ref.shape[1] : (n + 1) * ref.shape[1]]
            copies.append(
                remote(ref.at[take, :], target, self.own_send.at[t, slot, n], arrive, peer)
            )
        return copies

    def start(self, make, *args):
        for copy in make(*args):
            copy.start()
        self.started.append((make, args))

    def drain(self):
        for make, args in self.started:
            for copy in make(*args):
                copy.wait_send()

    def arrived(self, t, level, spot):
        ref = self.piece(t, level, spot, self.here.core)
        sem = self.link_recv.at[t, self.index(level, spot)]
        remote(ref, ref, sem, sem, self.here.x_peer).wait_recv()

    def begin(self, t):
        for slot in range(3):
            self.start(self.spreading, t, slot)

    def rise(self, t):
        for n in (1, 3, 2):
            self.start(self.spreading, t, 2 + n)

    def column(self, t):
        here = self.here
        for n in (1, 3, 2):
            self.arrived(t, here.level(n), here.spot)
            for kind in "xyc":
                self.start(self.passing, t, here.level(n), here.spot, kind)

    def cross(self, t):
        here = self.here
        for n in (0, 1, 3, 2):
            for spot, kind in ((here.across_x, "y"), (here.across_y, "x")):
                self.arrived(t, here.level(n), spot)
                if (n < 2) == (kind == "y"):
                    self.start(self.passing, t, here.level(n), spot, kind)
                self.start(self.passing, t, here.level(n), spot, "c")

    def corner(self, t):
        here = self.here
        for n in range(DEPTH):
            self.arrived(t, here.level(n), here.diagonal)
            self.start(self.passing, t, here.level(n), here.diagonal, "c")

    def finish(self, t):
        here = self.here
        for n in range(DEPTH):
            for spot in (here.spot, here.across_x, here.across_y, here.diagonal):
                if n == 0 and spot is here.spot:
                    ref = self.outs[t].at[self.rows(t, here.z, here.spot), :]
                else:
                    ref = self.piece(t, here.level(n), spot, here.other)
                sem = self.core_recv.at[t, self.index(here.level(n), spot)]
                remote(ref, ref, sem, sem, here.sibling).wait_recv()


def place_vectors(gathered, vec_ref, ub_ref, rows_out):
    chips = DEPTH * PLANE
    part = vec_ref.shape[1] // chips
    lane = lax.broadcasted_iota(jnp.int32, (16, LANES), 1)
    blocks = [gathered[c * 16 : (c + 1) * 16, :].astype(F32) for c in range(chips)]
    blocks = [jnp.where(lane < part, block, 0.0) for block in blocks]

    def spots(position):
        return position // LANES, position % LANES

    rows = [jnp.zeros((16, LANES), F32) for _ in range(vec_ref.shape[1] // LANES)]
    for c in range(chips):
        group, shift = spots(c * part)
        turned = pltpu.roll(blocks[c], shift, 1) if shift else blocks[c]
        if shift + part > LANES:
            rows[group] = rows[group] + jnp.where(lane >= shift, turned, 0.0)
            rows[group + 1] = rows[group + 1] + jnp.where(lane < shift, turned, 0.0)
        else:
            rows[group] = rows[group] + turned
    for group, row in enumerate(rows):
        cols = slice(group * LANES, (group + 1) * LANES)
        rows_out[:, cols] = row
        vec_ref[0:6, cols] = row[3:9]
    vec_ref[6:8, :] = jnp.zeros((2, vec_ref.shape[1]), F32)
    wide = [jnp.zeros((16, LANES), F32) for _ in range(ub_ref.shape[1] // LANES)]
    for c in range(chips):
        for r in range(4):
            group, shift = spots((4 * c + r) * part)
            row = jnp.broadcast_to(blocks[c][9 + r : 10 + r], (16, LANES))
            turned = pltpu.roll(row, shift, 1) if shift else row
            if shift + part > LANES:
                wide[group] = wide[group] + jnp.where(lane >= shift, turned, 0.0)
                wide[group + 1] = wide[group + 1] + jnp.where(lane < shift, turned, 0.0)
            else:
                wide[group] = wide[group] + turned
    for group, row in enumerate(wide):
        ub_ref[:, group * LANES : (group + 1) * LANES] = row[0:1]


BETWEEN = {
    1: (("cross", 2), ("column", 3)),
    2: (("corner", 2), ("column", 4)),
    3: (("cross", 3),),
    4: (("finish", 2), ("corner", 3)),
    5: (("cross", 4),),
    6: (("finish", 3),),
}


def gather_attend(
    x_ref, ct_ref, q_ref, k_ref, v_ref, o_ref, u_ref, d_ref, b_ref, cs_ref,
    xs_out, cts_out, qkv_out, o_out, u_out, d_out, b_out,
    a_ref, key_ref, val_ref, sq_ref, sk_ref, mixed_ref, den_ref, s_ref, vec_ref, ub_ref,
    state, xs, bounce, weights, vectors, rows,
    swap_sem, load_sem, own_send, x_send, y_send, c_send, link_recv, core_recv,
):
    here = Place()
    seq, chunk, chunks = pl.program_id(0), pl.program_id(1), pl.num_programs(1)
    step = seq * chunks + chunk
    last = pl.num_programs(0) * chunks - 1
    shards = ((b_ref,), (q_ref, k_ref, v_ref), (o_ref,), (u_ref,), (d_ref,))
    outs = (b_out, qkv_out, o_out, u_out, d_out)
    gather = Gather(
        here, shards, outs, own_send, x_send, y_send, c_send, link_recv, core_recv
    )
    pairs, block = x_ref.shape[0] // 2, x_ref.shape[1]

    def swapping():
        place = pl.ds(pl.multiple_of(here.core * block, block), block)
        mine, theirs = pl.ds(here.core * pairs, pairs), pl.ds(here.other * pairs, pairs)
        keep_x = pltpu.make_async_copy(x_ref.at[mine], xs.at[:, place, :], swap_sem.at[0])
        give_x = remote(
            x_ref.at[theirs], xs.at[:, place, :], swap_sem.at[1], swap_sem.at[2], here.sibling
        )
        fetch = pltpu.make_async_copy(ct_ref.at[mine], bounce, swap_sem.at[3])
        keep_ct = pltpu.make_async_copy(bounce, cts_out.at[:, place, :], swap_sem.at[4])
        give_ct = remote(
            ct_ref.at[theirs], cts_out.at[:, place, :], swap_sem.at[5], swap_sem.at[6], here.sibling
        )
        store = pltpu.make_async_copy(xs, xs_out, swap_sem.at[7])
        return keep_x, give_x, fetch, keep_ct, give_ct, store

    @pl.when(step == 0)
    def _():
        keep_x, give_x, fetch, keep_ct, give_ct, store = swapping()
        keep_x.start()
        fetch.start()
        meet(here)
        for t in range(2):
            gather.begin(t)
            gather.rise(t)
        give_x.start()
        give_ct.start()
        for t in range(2, 5):
            gather.begin(t)
        gather.rise(2)
        gather.column(0)
        gather.column(1)
        gather.rise(3)
        fetch.wait()
        keep_ct.start()
        gather.cross(0)
        gather.cross(1)
        gather.column(2)
        gather.rise(4)
        gather.corner(0)
        gather.corner(1)
        gather.finish(0)
        small = pltpu.make_async_copy(b_out, vectors, load_sem.at[0])
        small.start()
        keep_x.wait()
        give_x.wait()
        store.start()
        gather.finish(1)
        large = pltpu.make_async_copy(qkv_out, weights, load_sem.at[1])
        large.start()
        small.wait()
        place_vectors(vectors[...], vec_ref, ub_ref, rows)
        large.wait()

    for n, stages in BETWEEN.items():

        @pl.when(step == n)
        def _(stages=stages):
            for stage, t in stages:
                getattr(gather, stage)(t)

    @pl.when(chunk == 0)
    def _():
        state[...] = jnp.zeros_like(state)

    x = xs[seq, pl.ds(pl.multiple_of(chunk * CHUNK, CHUNK), CHUNK), :]
    attend(x, weights, rows, cs_ref, a_ref, key_ref, val_ref, sq_ref, sk_ref, mixed_ref, den_ref, s_ref, state)

    @pl.when(step == last)
    def _():
        gather.corner(4)
        gather.finish(4)
        _, _, _, keep_ct, give_ct, store = swapping()
        store.wait()
        keep_ct.wait()
        give_ct.wait()
        gather.drain()


def gather_attend_call(x, ct, q, k, v, o, u, d, b, cs):
    chips = DEPTH * PLANE
    anywhere = pl.BlockSpec(memory_space=pl.ANY)
    shape = lambda rows, cols: jax.ShapeDtypeStruct((rows, cols), BF16)
    seqs, length, width = x.shape[0] // 2, x.shape[1] * 2, x.shape[2]
    swapped = jax.ShapeDtypeStruct((seqs, length, width), BF16)
    chunks, total = length // CHUNK, seqs * length
    row = lambda n: pl.BlockSpec((CHUNK, n), lambda s, c: (s * chunks + c, 0))
    keep = lambda *shape: pl.BlockSpec(shape, lambda s, c: (0,) * len(shape))
    wide, count, sem = HEADS * LANES, 5, pltpu.SemaphoreType.DMA
    return pl.pallas_call(
        gather_attend,
        grid=(seqs, chunks),
        in_specs=[anywhere] * 9 + [row(LANES)],
        out_specs=[anywhere] * 7
        + [row(wide), row(wide)]
        + [row(width)] * 5
        + [
            pl.BlockSpec((None, HEADS, LANES, LANES), lambda s, c: (s * chunks + c, 0, 0, 0)),
            keep(8, width),
            keep(1, u.shape[1]),
        ],
        out_shape=[
            swapped,
            swapped,
            shape(q.shape[0] * chips, 3 * q.shape[1]),
            shape(o.shape[0] * chips, o.shape[1]),
            shape(u.shape[0] * chips, u.shape[1]),
            shape(d.shape[0] * chips, d.shape[1]),
            shape(b.shape[0] * chips, b.shape[1]),
            shape(total, wide),
            shape(total, wide),
            shape(total, width),
            shape(total, width),
            shape(total, width),
            shape(total, width),
            jax.ShapeDtypeStruct((total, width), F32),
            jax.ShapeDtypeStruct((seqs * chunks, HEADS, LANES, LANES), BF16),
            jax.ShapeDtypeStruct((8, width), F32),
            jax.ShapeDtypeStruct((1, u.shape[1]), F32),
        ],
        scratch_shapes=[
            pltpu.VMEM((HEADS, LANES, LANES), F32),
            pltpu.VMEM((seqs, length, width), BF16),
            pltpu.VMEM((seqs, x.shape[1], width), BF16),
            pltpu.VMEM((q.shape[0] * chips, 3 * q.shape[1]), BF16),
            pltpu.VMEM((b.shape[0] * chips, b.shape[1]), BF16),
            pltpu.VMEM((16, width), F32),
            sem((8,)),
            sem((2,)),
            sem((count, 6, 3)),
            sem((count, chips)),
            sem((count, chips)),
            sem((count, chips)),
            sem((count, chips)),
            sem((count, chips)),
        ],
        compiler_params=pltpu.CompilerParams(
            collective_id=0,
            has_side_effects=True,
            vmem_limit_bytes=VMEM_LIMIT,
            dimension_semantics=("arbitrary", "arbitrary"),
        ),
        name="gather_attend",
    )(x, ct, q, k, v, o, u, d, b, cs)


class Reduce:
    def __init__(self, here, full, got, corner_x, corner_y, side_x, side_y, column, final, outs, sems):
        self.here, self.outs = here, outs
        self.full, self.got = full, got
        self.corner_x, self.corner_y = corner_x, corner_y
        self.side_x, self.side_y = side_x, side_y
        self.levels, self.final = column, final
        self.core_send, self.core_recv, self.send_sem, self.recv_sem, self.z_send, self.z_recv, self.last_sem = sems
        self.started = []

    def cut(self, t):
        core, (rows, cols) = self.here.core, self.final[t].shape
        if t == 0:
            return pl.ds(pl.multiple_of(core * rows, rows), rows), slice(None)
        return self.window(t, core)

    def window(self, t, core):
        rows, cols = self.final[t].shape
        if t in (UP_A, UP_B):
            start = (2 * core + (t - UP_A)) * cols
            return slice(None), pl.ds(pl.multiple_of(start, cols), cols)
        place = pl.ds(pl.multiple_of(core * cols, cols), cols)
        if t in (DOWN_A, DOWN_B):
            return slice((t - DOWN_A) * rows, (t - DOWN_A + 1) * rows), place
        return slice(None), place

    def part(self, t, core):
        if t == 0:
            return self.full[t].at[core]
        rows, cols = self.window(t, core)
        return self.full[t].at[:, :, rows, cols]

    def mine(self, t):
        return self.part(t, self.here.core)

    def giving(self, t, n):
        source, target = self.part(t, self.here.other), self.got[t]
        if t in (DOWN_A, DOWN_B):
            source, target = source.at[n], target.at[n]
        return remote(
            source, target, self.core_send.at[t, n], self.core_recv.at[t, n], self.here.sibling
        )

    def gifts(self, t):
        return DEPTH if t in (DOWN_A, DOWN_B) else 1

    def pushing(self, t, slot):
        here, own = self.here, self.mine(t)
        source, target, peer = (
            (own.at[0:2, here.diagonal], self.corner_x[t], here.x_peer),
            (own.at[2:4, here.diagonal], self.corner_y[t], here.y_peer),
            (own.at[:, here.across_x], self.side_x[t], here.x_peer),
            (own.at[:, here.across_y], self.side_y[t], here.y_peer),
        )[slot]
        return remote(source, target, self.send_sem.at[t, slot], self.recv_sem.at[t, slot], peer)

    def sinking(self, t, n):
        here = self.here
        return remote(
            self.mine(t).at[here.level(n), here.spot],
            self.levels[t].at[n],
            self.z_send.at[t, n],
            self.z_recv.at[t, n],
            here.z_peer(n),
        )

    def ending(self, t):
        here = self.here
        rows, cols = self.cut(t)
        place = self.outs[t].at[rows, cols]
        keep = pltpu.make_async_copy(self.final[t], place, self.last_sem.at[t, 0])
        give = remote(
            self.final[t], place, self.last_sem.at[t, 1], self.last_sem.at[t, 2], here.sibling
        )
        return keep, give

    def start(self, make, *args):
        make(*args).start()
        self.started.append((make, args))

    def add(self, t, spot, first, count, parts):
        own = self.mine(t)

        def one(z, _):
            total = own[z, spot]
            for part in parts:
                total = total + part(z)
            own[z, spot] = total
            return 0

        lax.fori_loop(first, first + count, one, 0)

    def first(self, t):
        spot, got = self.here.diagonal, self.got[t]
        for n in range(self.gifts(t)):
            self.giving(t, n).wait_recv()
        self.add(t, spot, 0, DEPTH, [lambda z: got[z, spot]])
        self.start(self.pushing, t, 0)
        self.start(self.pushing, t, 1)

    def second(self, t):
        here, got = self.here, self.got[t]
        half = DEPTH // 2
        self.add(t, here.across_x, 0, half, [lambda z: got[z, here.across_x]])
        self.add(t, here.across_y, half, half, [lambda z: got[z, here.across_y]])
        self.pushing(t, 1).wait_recv()
        corner = self.corner_y[t]
        self.add(
            t, here.across_x, half, half, [lambda z: got[z, here.across_x], lambda z: corner[z - half]]
        )
        self.start(self.pushing, t, 2)
        self.pushing(t, 0).wait_recv()
        other = self.corner_x[t]
        self.add(t, here.across_y, 0, half, [lambda z: got[z, here.across_y], lambda z: other[z]])
        self.start(self.pushing, t, 3)

    def third(self, t):
        here, got = self.here, self.got[t]
        side_x, side_y = self.side_x[t], self.side_y[t]
        self.pushing(t, 2).wait_recv()
        self.pushing(t, 3).wait_recv()
        own = self.mine(t)

        def one(z, _):
            total = own[z, here.spot].astype(F32) + got[z, here.spot].astype(F32)
            total = total + (side_x[z].astype(F32) + side_y[z].astype(F32))
            own[z, here.spot] = total.astype(own.dtype)
            return 0

        lax.fori_loop(0, DEPTH, one, 0)
        for n in (2, 1, 3):
            self.start(self.sinking, t, n)

    def fourth(self, t):
        for n in range(1, DEPTH):
            self.sinking(t, n).wait_recv()
        total = self.mine(t)[self.here.z, self.here.spot].astype(F32)
        for n in range(1, DEPTH):
            total = total + self.levels[t][n].astype(F32)
        self.final[t][...] = total
        keep, give = self.ending(t)
        keep.start()
        give.start()

    def run(self, stages):
        for stage, t in stages:
            getattr(self, stage)(t)

    def drain(self):
        for make, args in self.started:
            make(*args).wait_send()
        for t in range(len(self.outs)):
            for n in range(self.gifts(t)):
                self.giving(t, n).wait_send()
            for copy in self.ending(t):
                copy.wait()


def pack_rows(vector_rows, ub_ref, buffer):
    chips = DEPTH * PLANE
    part = vector_rows.shape[1] // chips
    lane = lax.broadcasted_iota(jnp.int32, (16, LANES), 1)

    def cut(read, position):
        group, shift = position // LANES, position % LANES
        block = read(group)
        if not shift:
            return block
        turned = pltpu.roll(block, LANES - shift, 1)
        if shift + part > LANES:
            turned = jnp.where(lane < LANES - shift, turned, pltpu.roll(read(group + 1), LANES - shift, 1))
        return turned

    line = lax.broadcasted_iota(jnp.int32, (16, LANES), 0)

    def vectors(g):
        return vector_rows[:, g * LANES : (g + 1) * LANES]

    def up(g):
        return jnp.broadcast_to(ub_ref[0:1, g * LANES : (g + 1) * LANES], (16, LANES))

    for c in range(chips):
        block = cut(vectors, c * part)
        for r in range(4):
            block = jnp.where(line == 9 + r, cut(up, (4 * c + r) * part), block)
        for half in range(2):
            buffer[half, c // PLANE, c % PLANE] = block[8 * half : 8 * half + 8]


STEP = 256


def product(left, right, width, write):
    def one(n, _):
        offset = pl.multiple_of(n * STEP, STEP)
        write(offset, dot_tn(left[...], right[:, pl.ds(offset, STEP)]).astype(BF16))
        return 0

    lax.fori_loop(0, width // STEP, one, 0)


UP_A, UP_B, DOWN_A, DOWN_B = 5, 6, 7, 8
EARLY = {
    0: (("first", DOWN_A), ("first", DOWN_B)),
    2: (("second", DOWN_A),),
    3: (("second", DOWN_B),),
}
START = (("first", UP_A), ("first", UP_B), ("third", DOWN_A))
DURING = {
    1: (("third", DOWN_B), ("first", 4)),
    2: (("second", UP_A),),
    3: (("fourth", DOWN_A), ("second", UP_B)),
    4: (("fourth", DOWN_B), ("third", UP_A), ("second", 4)),
    5: (("third", UP_B),),
    6: (("third", 4), ("fourth", UP_A)),
    7: (("fourth", UP_B), ("fourth", 4)),
}
WEIGHTS = {1: (("first", 1),), 2: (("first", 2), ("second", 1))}
AFTER = {
    0: (("first", 3),),
    1: (("first", 0),),
    2: (("second", 2),),
    3: (("third", 1),),
    4: (("second", 3),),
    5: (("second", 0),),
    6: (("third", 2),),
    7: (("third", 3), ("fourth", 1), ("third", 0), ("fourth", 2), ("fourth", 3), ("fourth", 0)),
}


def reduce_attend(
    x_hbm, resid_hbm, w_hbm, out_hbm, gvec_ref, gub_ref,
    act_hbm, hidden_hbm, normed_hbm, ffn_hbm, mixed_hbm, branch_hbm,
    a_ref, k_ref, v_ref, e_ref, s_ref, sq_ref, sk_ref, cs_ref,
    out4, grad4, r_b, r_q, r_k, r_v, r_o, r_u, r_d,
    after, back, x_all, weights, gb, rows, bounce, resid_tile, grad_tile, *scratch,
):
    kinds = 9
    names = ("got", "corner_x", "corner_y", "side_x", "side_y", "column", "final")
    full, scratch = scratch[:7], scratch[7:]
    full = (*full[:5], full[5], full[5], full[6], full[6])
    parts = [full] + [scratch[n * kinds : (n + 1) * kinds] for n in range(len(names))]
    swap_sem, big_sem, tile_sem, feed_sem, *sems = scratch[len(names) * kinds :]
    here = Place()
    seq, chunk, chunks = pl.program_id(0), pl.program_id(1), pl.num_programs(1)
    step = seq * chunks + chunk
    last = pl.num_programs(0) * chunks - 1
    reduce = Reduce(here, *parts, (r_b, r_q, r_k, r_v, r_o, r_u, r_u, r_d, r_d), sems)
    pairs, length, width = out_hbm.shape
    block = length // 2
    swaps = []
    for n in range(pairs):
        source = out_hbm.at[n]
        mine = pl.ds(pl.multiple_of(here.core * block, block), block)
        theirs = pl.ds(pl.multiple_of(here.other * block, block), block)
        place = out4.at[here.core * pairs + n]
        swaps.append(
            (
                pltpu.make_async_copy(source.at[mine, :], bounce, swap_sem.at[n, 0]),
                pltpu.make_async_copy(bounce, place, swap_sem.at[n, 1]),
                remote(source.at[theirs, :], place, swap_sem.at[n, 2], swap_sem.at[n, 3], here.sibling),
            )
        )
    big = [
        pltpu.make_async_copy(source, target, big_sem.at[n])
        for n, (source, target) in enumerate(((x_hbm, x_all), (w_hbm, weights)))
    ]
    levels = act_hbm.shape[1] // width

    def slot(n):
        return back.at[:, pl.ds(pl.multiple_of(n * width, width), width)]

    def block_of(n):
        return pl.ds(pl.multiple_of(n * width, width), width)

    def later(n):
        return (n + 2 * here.other) % levels

    def act_feed(n):
        return pltpu.make_async_copy(act_hbm.at[:, block_of(n)], slot(n % 2), feed_sem.at[n % 2])

    def hidden_feed(n):
        return pltpu.make_async_copy(hidden_hbm.at[:, block_of(later(n))], slot(n % 2), feed_sem.at[n % 2])

    def square(t, left, right):
        def write(offset, value):
            full[t][:, :, :, pl.ds(offset, STEP)] = value.reshape(full[t].shape[:3] + (STEP,))

        product(left, right, width, write)

    @pl.when(step == 0)
    def _():
        gb[...] = jnp.zeros_like(gb)
        ffn_feed = pltpu.make_async_copy(ffn_hbm, slot(2), feed_sem.at[2])
        normed_feed = pltpu.make_async_copy(normed_hbm, x_all, big_sem.at[2])
        mixed_feed = pltpu.make_async_copy(mixed_hbm, slot(2), feed_sem.at[2])
        branch_feed = pltpu.make_async_copy(branch_hbm, slot(0), feed_sem.at[0])
        ffn_feed.start()
        act_feed(0).start()
        act_feed(1).start()
        normed_feed.start()
        meet(here)
        swaps[0][0].start()
        for _, _, send in swaps:
            send.start()
        ffn_feed.wait()

        def down_level(n, _):
            act_feed(n).wait()

            def write(offset, value):
                full[DOWN_A][n, :, :, pl.ds(offset, STEP)] = value.reshape(
                    full[DOWN_A].shape[1:3] + (STEP,)
                )

            product(slot(n % 2), slot(2), width, write)

            @pl.when(n + 2 < levels)
            def _():
                act_feed(n + 2).start()

            @pl.when(n + 2 >= levels)
            def _():
                hidden_feed(n + 2 - levels).start()

            reduce.giving(DOWN_A, n).start()
            reduce.giving(DOWN_B, n).start()
            return 0

        lax.fori_loop(0, levels, down_level, 0)
        mixed_feed.start()
        normed_feed.wait()

        def up_block(n, _):
            for m, stages in EARLY.items():

                @pl.when(n == m)
                def _(stages=stages):
                    reduce.run(stages)

            hidden_feed(n).wait()

            def write(offset, value):
                place = pl.ds(pl.multiple_of(later(n) * width + offset, STEP), STEP)
                full[UP_A][:, :, :, place] = value.reshape(full[UP_A].shape[:3] + (STEP,))

            product(x_all, slot(n % 2), width, write)

            @pl.when(n + 2 < levels)
            def _():
                hidden_feed(n + 2).start()

            @pl.when(n == levels - 2)
            def _():
                branch_feed.start()

            for m in range(2):

                @pl.when(n == m)
                def _(m=m):
                    reduce.giving(UP_A + m, 0).start()

            return 0

        lax.fori_loop(0, levels, up_block, 0)
        mixed_feed.wait()
        branch_feed.wait()
        square(4, slot(2), slot(0))
        reduce.giving(4, 0).start()
        swaps[0][0].wait()
        swaps[0][1].start()
        for copy in big:
            copy.start()
        reduce.run(START)

    for n, stages in DURING.items():

        @pl.when(step == n)
        def _(n=n, stages=stages):
            if n == 1:
                swaps[0][1].wait()
                swaps[1][0].start()
            if n == 2:
                swaps[1][0].wait()
                swaps[1][1].start()
            reduce.run(stages)

    @pl.when(chunk == 0)
    def _():
        after[...] = jnp.zeros_like(after)

    at = pl.multiple_of((seq * chunks + chunks - 1 - chunk) * CHUNK, CHUNK)
    attend_back(
        a_ref, k_ref, v_ref, e_ref, s_ref, sq_ref, sk_ref, cs_ref, after, back.at[pl.ds(at, CHUNK), :], gb
    )

    @pl.when(step == last)
    def _():
        for copy in big:
            copy.wait()
        rows[0:3, :] = jnp.concatenate([gb[:, n * width : (n + 1) * width] for n in range(3)])
        rows[3:9, :] = gvec_ref[0:6, :]
        rows[9:16, :] = jnp.zeros((7, width), F32)
        pack_rows(rows, gub_ref, full[0])
        reduce.giving(0, 0).start()
        tiles = pairs * length // CHUNK
        per_seq = length // CHUNK

        def rows_of(i):
            return pl.ds(pl.multiple_of(i * CHUNK, CHUNK), CHUNK)

        def load(i):
            return pltpu.make_async_copy(
                resid_hbm.at[rows_of(i), :], resid_tile.at[i % 2], tile_sem.at[i % 2, 0]
            )

        load(0).start()
        for n in range(3):
            square(1 + n, x_all, slot(n))
            reduce.giving(1 + n, 0).start()
            reduce.run(WEIGHTS.get(n, ()))

        def writes(i):
            s, c = i // per_seq, i % per_seq
            spot = grad4.at[here.core * pairs + s, pl.ds((c % (per_seq // 2)) * CHUNK, CHUNK), :]
            local = pltpu.make_async_copy(grad_tile.at[i % 2], spot, tile_sem.at[i % 2, 1])
            away = remote(grad_tile.at[i % 2], spot, tile_sem.at[i % 2, 2], swap_sem.at[2 + i, 0], here.sibling)
            return local, away, here.core == c // (per_seq // 2)

        def written(i):
            local, away, stays = writes(i)

            @pl.when(stays)
            def _():
                local.wait()

            @pl.when(jnp.logical_not(stays))
            def _():
                away.wait_send()

        def tile(i, _):
            for n in range(tiles - 1):

                @pl.when(i == n)
                def _():
                    reduce.run(AFTER[n])

            @pl.when(i + 1 < tiles)
            def _():
                load(i + 1).start()

            load(i).wait()

            @pl.when(i >= 2)
            def _():
                written(i - 2)

            grad_tile[i % 2] = resid_tile[i % 2] + dot_nt(back[rows_of(i), :], weights[...])
            local, away, stays = writes(i)

            @pl.when(stays)
            def _():
                local.start()

            @pl.when(jnp.logical_not(stays))
            def _():
                away.start()

            return 0

        lax.fori_loop(0, tiles, tile, 0)
        reduce.run(AFTER[tiles - 1])
        for i in range(tiles - 2, tiles):
            written(i)
        for i in range(tiles):
            _, away, stays = writes(i)

            @pl.when(stays)
            def _(away=away):
                away.wait_recv()

        swaps[1][1].wait()
        for _, _, send in swaps:
            send.wait()
        reduce.drain()


def reduce_attend_call(
    x, resid, w, out, gvec, gub, act, hidden, normed, ffn, mixed, branch, a, k, v, e, s, sq, sk, cs
):
    chips = DEPTH * PLANE
    seqs, length, width = out.shape
    total, chunks, wide = seqs * length, length // CHUNK, HEADS * LANES
    anywhere = pl.BlockSpec(memory_space=pl.ANY)
    place = lambda s, c: s * chunks + chunks - 1 - c
    row = lambda n: pl.BlockSpec((CHUNK, n), lambda s, c: (place(s, c), 0))
    once = lambda a: pl.BlockSpec(
        a.shape, lambda s, c: (0,) * len(a.shape), pipeline_mode=pl.Buffered(1)
    )
    part, tall = width // chips, act.shape[1]
    pieces = [(8, LANES, F32)] + [(part, width // 2, BF16)] * 4
    pieces += [(part, tall // 4, BF16)] * 2 + [(tall // chips // 2, width // 2, BF16)] * 2
    kinds, sem = len(pieces), pltpu.SemaphoreType.DMA
    grid = (DEPTH, PLANE)
    scratch = [pltpu.VMEM((2,) + grid + pieces[0][:2], F32)]
    scratch += [pltpu.VMEM(grid + (part, width), BF16)] * 4
    scratch += [pltpu.VMEM(grid + (part, tall), BF16), pltpu.VMEM(grid + (tall // chips, width), BF16)]
    for lead in (grid, (2,), (2,), (DEPTH,), (DEPTH,), (DEPTH,)):
        scratch += [pltpu.VMEM(lead + p[:2], p[2]) for p in pieces]
    scratch += [pltpu.VMEM(p[:2], F32) for p in pieces]
    scratch += [sem((2 + total // CHUNK, 4)), sem((3,)), sem((2, 3)), sem((3,))]
    scratch += [sem((kinds, 4))] * 6 + [sem((kinds, 3))]
    shard = lambda rows, cols: jax.ShapeDtypeStruct((rows, cols), F32)
    return pl.pallas_call(
        reduce_attend,
        grid=(seqs, chunks),
        in_specs=[anywhere] * 4
        + [once(gvec), once(gub)]
        + [anywhere] * 6
        + [row(wide), row(wide), row(width), row(wide)]
        + [pl.BlockSpec((None, HEADS, LANES, LANES), lambda s, c: (place(s, c), 0, 0, 0))]
        + [row(width), row(width), row(LANES)],
        out_specs=[anywhere] * 9,
        out_shape=[
            jax.ShapeDtypeStruct((seqs * 2, length // 2, width), BF16),
            jax.ShapeDtypeStruct((seqs * 2, length // 2, width), F32),
            shard(16, LANES),
            shard(part, width),
            shard(part, width),
            shard(part, width),
            shard(part, width),
            shard(part, tall),
            shard(tall // chips, width),
        ],
        scratch_shapes=[
            pltpu.VMEM((HEADS, LANES, LANES), F32),
            pltpu.VMEM((total, 3 * width), BF16),
            pltpu.VMEM((total, width), BF16),
            pltpu.VMEM(w.shape, BF16),
            pltpu.VMEM((1, 3 * width), F32),
            pltpu.VMEM((16, width), F32),
            pltpu.VMEM((length // 2, width), BF16),
            pltpu.VMEM((2, CHUNK, width), F32),
            pltpu.VMEM((2, CHUNK, width), F32),
        ]
        + scratch,
        compiler_params=pltpu.CompilerParams(
            collective_id=1,
            has_side_effects=True,
            vmem_limit_bytes=VMEM_LIMIT,
            dimension_semantics=("arbitrary", "arbitrary"),
        ),
        name="reduce_attend",
    )(x, resid, w, out, gvec, gub, act, hidden, normed, ffn, mixed, branch, a, k, v, e, s, sq, sk, cs)


def pack_vectors(vectors, up_bias):
    part = vectors[0].shape[0]
    stacked = jnp.concatenate([jnp.stack(vectors), up_bias.reshape(-1, part)])
    return jnp.pad(stacked, ((0, 16 - stacked.shape[0]), (0, LANES - part)))


def unpack_vectors(gathered, part):
    chips = gathered.shape[0] // 16
    grid = gathered.reshape(chips, 16, LANES)[:, :13, :part].astype(F32)
    rows = jnp.transpose(grid[:, :9], (1, 0, 2)).reshape(9, chips * part)
    up_bias = grid[:, 9:].reshape(1, chips * 4 * part)
    return rows[0:3], jnp.pad(rows[3:9], ((0, 2), (0, 0))), up_bias


def pack_vector_grads(gb, gvec, gub, chips):
    width = gvec.shape[1]
    part = width // chips
    rows = jnp.concatenate([gb.reshape(3, width), gvec[0:6]]).reshape(9, chips, part)
    rows = jnp.transpose(rows, (1, 0, 2))
    grid = jnp.concatenate([rows, gub.reshape(chips, 4, part)], axis=1)
    grid = jnp.pad(grid, ((0, 0), (0, 3), (0, LANES - part)))
    return grid.reshape(chips * 16, LANES)


def finish(part, out_in, grad_in, vec_in, *refs):
    weights, (out_ref, grad_ref, *rest) = refs[:6], refs[6:]
    out_ref[...] = out_in[...]
    grad_ref[...] = grad_in[...]

    @pl.when(pl.program_id(0) == 0)
    def _():
        for source, target in zip(weights, rest[:6]):
            target[...] = source[...]
        for n, target in enumerate(rest[6:15]):
            target[...] = vec_in[n, :part]
        for n in range(4):
            rest[15][n * part : (n + 1) * part] = vec_in[9 + n, :part]


def finish_call(out, grad, vec, weights, part):
    row = pl.BlockSpec((None,) + out.shape[1:], lambda i: (i, 0, 0))
    whole = lambda shape: pl.BlockSpec(shape, lambda i: (0,) * len(shape))
    flat = [(part,)] * 9 + [(4 * part,)]
    return pl.pallas_call(
        functools.partial(finish, part),
        grid=(out.shape[0],),
        in_specs=[row, row, whole(vec.shape)] + [whole(w.shape) for w in weights],
        out_specs=[row, row] + [whole(w.shape) for w in weights] + [whole(s) for s in flat],
        out_shape=[
            jax.ShapeDtypeStruct(out.shape, out.dtype),
            jax.ShapeDtypeStruct(grad.shape, grad.dtype),
        ]
        + [jax.ShapeDtypeStruct(w.shape, F32) for w in weights]
        + [jax.ShapeDtypeStruct(s, F32) for s in flat],
        compiler_params=pltpu.CompilerParams(
            dimension_semantics=("arbitrary",), vmem_limit_bytes=VMEM_LIMIT
        ),
        name="finish",
    )(out, grad, vec, *weights)


def local(
    inputs,
    horizon,
    query_weight,
    query_bias,
    key_weight,
    key_bias,
    value_weight,
    value_bias,
    out_weight,
    out_bias,
    first_gain,
    first_shift,
    up_weight,
    up_bias,
    down_weight,
    down_bias,
    second_gain,
    second_shift,
    cotangent,
):
    chips = lax.axis_size("dp")
    core = lax.axis_index("seq")
    part = query_bias.shape[0]
    seqs = inputs.shape[0] // 2
    direct = chips == DEPTH * PLANE
    vectors = pack_vectors(
        (
            query_bias,
            key_bias,
            value_bias,
            out_bias,
            first_gain,
            first_shift,
            down_bias,
            second_gain,
            second_shift,
        ),
        up_bias,
    )
    weights = (query_weight, key_weight, value_weight, out_weight, up_weight, down_weight)
    spans = lax.dynamic_slice_in_dim(horizon, core * seqs, seqs)
    length = 2 * inputs.shape[1]
    chunks = length // CHUNK
    cs = rotation(spans, length)
    flat = lambda a: a.reshape(-1, a.shape[-1])
    if direct:
        x, ct, wqkv, wo, wu, wd, _, *saved, vec, ubias = gather_attend_call(
            inputs, cotangent, *weights, vectors, cs
        )
    else:
        gather = lambda a: lax.all_gather(a, "dp", axis=0, tiled=True)
        x, ct = (lax.all_to_all(a, "seq", 0, 1, tiled=True) for a in (inputs, cotangent))
        wqkv = gather(jnp.concatenate(weights[:3], axis=1))
        wo, wu, wd, gathered = (gather(a) for a in (*weights[3:], vectors))
        bqkv, vec, ubias = unpack_vectors(gathered, part)
        saved = forward_call(flat(x), wqkv, bqkv, cs, chunks)
    a, k, v, sq, sk, mixed, den, s = saved
    fx = flat(x)
    out, resid, e, act, hidden, normed, ffn, branch, gvec, gub = middle_call(
        fx, flat(ct), mixed, den, vec, ubias, wo, wu, wd
    )
    out = out.reshape(x.shape)
    if direct:
        out, grad, gvectors, gq, gk, gv, go, gu, gd = reduce_attend_call(
            fx, resid, wqkv, out, gvec, gub, act, hidden, normed, ffn, mixed, branch,
            a, k, v, e, s, sq, sk, cs,
        )
    else:
        go, gu, gd = dot_tn(mixed, branch), dot_tn(normed, hidden), dot_tn(act, ffn)
        grad, gw, gb = backward_call(fx, a, k, v, e, s, sq, sk, cs, resid, wqkv, chunks)
        gvectors = pack_vector_grads(gb, gvec, gub, chips)
        out, grad = (
            lax.all_to_all(a, "seq", 1, 0, tiled=True) for a in (out, grad.reshape(x.shape))
        )
        total = lambda g: lax.psum(
            lax.psum_scatter(g.astype(F32), "dp", scatter_dimension=0, tiled=True), "seq"
        )
        gw, go, gu, gd, gvectors = (total(g) for g in (gw, go, gu, gd, gvectors))
        gq, gk, gv = jnp.split(gw, 3, axis=1)
    if direct:
        weights = (gq, gk, gv, go, gu, gd)
        out, grad, gq, gk, gv, go, gu, gd, *thin, wide = finish_call(out, grad, gvectors, weights, part)
    else:
        rows = gvectors[:, :part]
        thin, wide = [rows[n] for n in range(9)], rows[9:13].reshape(-1)
    bq, bk, bv, bo, g1, s1, bd, g2, s2 = thin
    return out, grad, gq, bq, gk, bk, gv, bv, go, bo, g1, s1, gu, wide, gd, bd, g2, s2


def solution(mesh):
    long, wide, thin = P("dp", "seq", None), P("dp", None), P("dp")
    shards = (wide, thin, wide, thin, wide, thin, wide, thin, thin, thin, wide, thin, wide, thin, thin, thin)
    return jax.shard_map(
        local,
        mesh=mesh,
        in_specs=(long, thin, *shards, long),
        out_specs=(long, long, *shards),
        check_vma=False,
    )
```
